256 devices in a mesh: dp: 32 (over y, x, core), tensor: 8 (over z).
Axes of the slice: x: 4, y: 4, z: 8, core: 2. Of those that a mesh axis runs over, the one named last changes fastest.
Arguments:
- hidden: bfloat16 [32, 1024, 4096], P('dp', None, 'tensor'), as said below
- gain: float32 [4096], replicated, may hold values from 0.5 to 1.5
- head: bfloat16 [4096, 131072], P(None, ('dp', 'tensor'))
- lengths: int32 [32], P('dp'), may hold values from 256 to 1024, as said below
- offsets: int32 [32, 32], P('dp'), may hold values from 0 to 255
- targets: int32 [32, 32], P('dp'), may hold values from 0 to 131071
- mask: int32 [32, 32], P('dp'), may hold values from 0 to 1, as said below
Outputs:
- logprob: float32 [32, 32], P('dp')
- entropy: float32 [32, 32], P('dp')
The draws below stay inside these ranges and needn't reach their ends.
Inputs may be any that keep to these rules, and one draw needn't show every extreme that they name: `lengths`: each length is at least 256; some sequence has length exactly 1024 in every draw. `mask`: among the 32 slots of the sequences of one index of dp, at most 16 are scored; some index of dp has exactly 16. `hidden`: entries are of order one or a few tens in magnitude.
All inputs are finite; a program needn't handle non-finite values.
Results may differ from the reference program's by a relative error of at most 0.0089.
Values may be sent and summed in bfloat16 or wider, within the bound.
A program may use at most 64 MiB of HBM per device.

```python
import math
import jax
import jax.numpy as jnp
import numpy as np
from jax import lax

D = 4096
SEQ_DEV = 1
SLOTS = 32
MAXLEN = 1024
MINLEN = 256
VOCAB = 131072
SEQS = 32
LIVE_DEV = 16


def draw_hidden(key, part):
    first, second = jax.random.split(jax.random.fold_in(key, 11))
    scales = jnp.exp(jax.random.uniform(second, (SEQS, MAXLEN, 1), minval=math.log(0.3), maxval=math.log(3.0)))
    noise = jax.random.normal(first, (SEQS, MAXLEN, D))
    return (noise * scales).astype(jnp.bfloat16)


def draw_head(key, part):
    first, second = jax.random.split(jax.random.fold_in(key, 13), 2)
    colscale = jnp.exp(jax.random.uniform(second, (1, VOCAB), minval=0.0, maxval=math.log(10.0))) / math.sqrt(D)
    values = jax.random.normal(first, (D, VOCAB)) * colscale
    return values.astype(jnp.bfloat16)


def draw_lengths(key, part):
    first, second, third = jax.random.split(jax.random.fold_in(key, 21), 3)
    shifts = jax.random.randint(first, (SEQS,), 0, 6)
    spans = jnp.right_shift(jnp.full((SEQS,), MAXLEN - MINLEN, jnp.int32), shifts) + 1
    extra = jax.random.randint(second, (SEQS,), 0, spans)
    longest = jax.random.randint(third, (), 0, SEQS)
    return jnp.where(jnp.arange(SEQS) == longest, MAXLEN, MINLEN + extra).astype(jnp.int32)


def draw_mask(key, part):
    first, second, third = jax.random.split(jax.random.fold_in(key, 31), 3)
    blocks = SEQS // SEQ_DEV
    per_block = SEQ_DEV * SLOTS
    live = jnp.right_shift(jnp.full((blocks,), LIVE_DEV, jnp.int32), jax.random.randint(first, (blocks,), 0, 3))
    fullest = jax.random.randint(second, (), 0, blocks)
    live = jnp.where(jnp.arange(blocks) == fullest, LIVE_DEV, live)
    orders = jax.vmap(lambda k: jax.random.permutation(k, per_block))(jax.random.split(third, blocks))
    return (orders < live[:, None]).astype(jnp.int32).reshape(SEQS, SLOTS)


def plant(entries, key, smallest, top_value):
    place = [jax.random.randint(jax.random.fold_in(key, axis), (), 0, length) for axis, length in enumerate(entries.shape)]
    widest = entries.shape.index(max(entries.shape))
    neighbour = place[:widest] + [(place[widest] + 1) % entries.shape[widest]] + place[widest + 1:]
    return entries.at[tuple(place)].set(smallest).at[tuple(neighbour)].set(top_value)


def wide_ids(stream_key, dims, amount, lean):
    weights = [min(1 << octave, amount + 1 - (1 << octave)) * (1 << 20) // math.isqrt((1 << octave) ** lean) + 1 for octave in range((amount + 1).bit_length()) if 1 << octave <= amount]
    scale = 1 + sum(weights) // (1 << 30)
    table = np.cumsum(np.array([max(1, weight // scale) for weight in weights]))
    ticket = jax.random.randint(jax.random.fold_in(stream_key, 1), dims, 0, int(table[len(weights) - 1]))
    start = jnp.left_shift(1, jnp.searchsorted(jnp.asarray(table, jnp.int32), ticket, side="right").astype(jnp.int32))
    grade = start - 1 + jax.random.randint(jax.random.fold_in(stream_key, 4), dims, 0, 1 << 30) % jnp.minimum(start, amount + 1 - start)
    return jax.random.permutation(jax.random.fold_in(stream_key, 2), amount)[grade].astype(jnp.int32)


def setup_inputs(seed: int = 0) -> dict:
    key_of = jax.random.split(jax.random.key(seed), 8)
    hidden = draw_hidden(jax.random.fold_in(key_of[7], 71), 0)
    gain = jnp.clip(1.0 + 0.1 * jax.random.normal(key_of[1], (D,), jnp.float32), 0.5, 1.5)
    head = draw_head(jax.random.fold_in(key_of[7], 71), 0)
    lengths = draw_lengths(jax.random.fold_in(key_of[7], 71), 0)
    offsets = plant(jax.random.randint(key_of[4], (SEQS, SLOTS), 0, MINLEN), jax.random.fold_in(key_of[4], 1), 0, MINLEN - 1).astype(jnp.int32)
    targets = plant(wide_ids(key_of[5], (SEQS, SLOTS), VOCAB, 2), jax.random.fold_in(key_of[5], 3), 0, VOCAB - 1).astype(jnp.int32)
    mask = draw_mask(jax.random.fold_in(key_of[7], 71), 0)
    return {"hidden": hidden, "gain": gain, "head": head, "lengths": lengths, "offsets": offsets, "targets": targets, "mask": mask}


def score_sequence(items, gain, head):
    states, length, offset, target, live = items
    position = (length - 1 - offset).astype(jnp.int32)
    rows = jnp.take(states, position, axis=0)
    values = rows.astype(jnp.float32)
    meansq = lax.optimization_barrier(jnp.mean(values * values, axis=-1, keepdims=True))
    normed = (values * lax.rsqrt(meansq + 1e-06) * gain).astype(jnp.bfloat16)
    logits = jnp.dot(normed, head, preferred_element_type=jnp.float32)
    top = lax.optimization_barrier(jnp.max(logits, axis=-1, keepdims=True))
    expo = jnp.exp(logits - top)
    total = lax.optimization_barrier(jnp.sum(expo, axis=-1))
    lse = top[:, 0] + jnp.log(total)
    picked = jnp.take_along_axis(logits, target[:, None].astype(jnp.int32), axis=1)[:, 0]
    weighted = lax.optimization_barrier(jnp.sum(expo * logits, axis=-1)) / total
    keep = live.astype(jnp.float32)
    return (keep * (picked - lse), keep * (lse - weighted))

def reference(hidden, gain, head, lengths, offsets, targets, mask):
    return lax.map(lambda items: score_sequence(items, gain, head), (hidden, lengths, offsets, targets, mask))
```

```python
import functools

import jax
import jax.numpy as jnp
from jax import lax
from jax.experimental import pallas as pl
from jax.experimental.pallas import tpu as pltpu
from jax.sharding import PartitionSpec as P

MESH = pl.DeviceIdType.MESH
LIVE = 16


def merge(parts):
    tops = parts[:, 0, :]
    top = jnp.max(tops, axis=0, keepdims=True)
    factor = jnp.exp(tops - top)
    total = jnp.sum(parts[:, 1, :] * factor, axis=0, keepdims=True)
    weighted = jnp.sum(parts[:, 2, :] * factor, axis=0, keepdims=True)
    chosen = jnp.sum(parts[:, 3, :], axis=0, keepdims=True)
    return jnp.concatenate([top, total, weighted, chosen], axis=0)


def stats_kernel(part_ref, out_ref, got1, sent, got2, send1, recv1, send2, recv2, local):
    n_dp = part_ref.shape[0]
    n_t = got2.shape[0]
    me = lax.axis_index("dp")
    mt = lax.axis_index("tensor")

    barrier = pltpu.get_barrier_semaphore()

    def greet_dp(i, carry):
        p = lax.rem(me + 1 + i, n_dp)
        pl.semaphore_signal(barrier, 1, device_id=(p, mt), device_id_type=MESH)
        return carry

    def greet_t(i, carry):
        q = lax.rem(mt + 1 + i, n_t)
        pl.semaphore_signal(barrier, 1, device_id=(me, q), device_id_type=MESH)
        return carry

    lax.fori_loop(0, n_dp - 1, greet_dp, 0)
    lax.fori_loop(0, n_t - 1, greet_t, 0)
    pl.semaphore_wait(barrier, n_dp - 1 + n_t - 1)

    def out1(p):
        return pltpu.make_async_remote_copy(
            src_ref=part_ref.at[p], dst_ref=got1.at[me], send_sem=send1.at[p],
            recv_sem=recv1.at[me], device_id=(p, mt), device_id_type=MESH)

    def in1(p):
        return pltpu.make_async_remote_copy(
            src_ref=part_ref.at[p], dst_ref=got1.at[p], send_sem=send1.at[p],
            recv_sem=recv1.at[p], device_id=(p, mt), device_id_type=MESH)

    def start1(i, carry):
        out1(lax.rem(me + 1 + i, n_dp)).start()
        return carry

    lax.fori_loop(0, n_dp - 1, start1, 0)
    own1 = pltpu.make_async_copy(part_ref.at[me], got1.at[me], local.at[0])
    own1.start()

    def finish1(i, carry):
        p = lax.rem(me + 1 + i, n_dp)
        in1(p).wait_recv()
        out1(p).wait_send()
        return carry

    lax.fori_loop(0, n_dp - 1, finish1, 0)
    own1.wait()

    sent[...] = merge(got1[...])

    def out2(q):
        return pltpu.make_async_remote_copy(
            src_ref=sent, dst_ref=got2.at[mt], send_sem=send2.at[q],
            recv_sem=recv2.at[mt], device_id=(me, q), device_id_type=MESH)

    def in2(q):
        return pltpu.make_async_remote_copy(
            src_ref=sent, dst_ref=got2.at[q], send_sem=send2.at[q],
            recv_sem=recv2.at[q], device_id=(me, q), device_id_type=MESH)

    def start2(i, carry):
        out2(lax.rem(mt + 1 + i, n_t)).start()
        return carry

    lax.fori_loop(0, n_t - 1, start2, 0)
    own2 = pltpu.make_async_copy(sent, got2.at[mt], local.at[1])
    own2.start()

    def finish2(i, carry):
        q = lax.rem(mt + 1 + i, n_t)
        in2(q).wait_recv()
        out2(q).wait_send()
        return carry

    lax.fori_loop(0, n_t - 1, finish2, 0)
    own2.wait()

    out_ref[...] = merge(got2[...])


def exchange_stats(parts, n_t):
    n_dp, four, k = parts.shape
    return pl.pallas_call(
        stats_kernel,
        out_shape=jax.ShapeDtypeStruct((four, k), jnp.float32),
        in_specs=[pl.BlockSpec(memory_space=pltpu.VMEM)],
        out_specs=pl.BlockSpec(memory_space=pltpu.VMEM),
        scratch_shapes=[
            pltpu.VMEM((n_dp, four, k), jnp.float32),
            pltpu.VMEM((four, k), jnp.float32),
            pltpu.VMEM((n_t, four, k), jnp.float32),
            pltpu.SemaphoreType.DMA((n_dp,)),
            pltpu.SemaphoreType.DMA((n_dp,)),
            pltpu.SemaphoreType.DMA((n_t,)),
            pltpu.SemaphoreType.DMA((n_t,)),
            pltpu.SemaphoreType.DMA((2,)),
        ],
        compiler_params=pltpu.CompilerParams(collective_id=0, has_side_effects=True),
    )(parts)


def per_device(hidden, gain, head, lengths, offsets, targets, mask):
    seq_count, slot_count = offsets.shape
    slots = seq_count * slot_count
    maxlen = hidden.shape[1]
    n_dp = lax.axis_size("dp")
    n_t = lax.axis_size("tensor")
    k = min(LIVE, slots)

    live = mask.reshape(slots) != 0
    rank = jnp.cumsum(live.astype(jnp.int32)) - 1
    sel = live[None, :] & (rank[None, :] == jnp.arange(k, dtype=jnp.int32)[:, None])
    idx = jnp.sum(jnp.where(sel, jnp.arange(slots, dtype=jnp.int32)[None, :], 0), axis=1)
    seq_of = idx // slot_count
    position = lengths[seq_of] - 1 - offsets.reshape(slots)[idx]
    flat_hidden = hidden.reshape(seq_count * maxlen, hidden.shape[2])
    picked = jnp.take(flat_hidden, seq_of * maxlen + position, axis=0)
    flat_target = targets.reshape(slots)[idx]

    full_rows = lax.all_gather(picked, "tensor", axis=1, tiled=True)
    values = full_rows.astype(jnp.float32)
    meansq = jnp.mean(values * values, axis=-1, keepdims=True)
    normed = (values * lax.rsqrt(meansq + 1e-06) * gain).astype(jnp.bfloat16)

    vocab_width = head.shape[1]
    vocab_start = (lax.axis_index("dp") * n_t + lax.axis_index("tensor")) * vocab_width
    columns = jnp.arange(vocab_width, dtype=jnp.int32)
    rows_piece = lax.all_gather(normed, "dp", axis=0, tiled=True)
    target_piece = lax.all_gather(flat_target, "dp", axis=0, tiled=True)
    logits = jnp.dot(rows_piece, head, preferred_element_type=jnp.float32)
    top = jnp.max(logits, axis=-1)
    expo = jnp.exp(logits - top[:, None])
    total = jnp.sum(expo, axis=-1)
    weighted = jnp.sum(expo * logits, axis=-1)
    hit = columns[None, :] == (target_piece - vocab_start)[:, None]
    chosen = jnp.sum(jnp.where(hit, logits, 0.0), axis=-1)

    parts = jnp.stack([top, total, weighted, chosen]).reshape(4, n_dp, k).transpose(1, 0, 2)
    top, total, weighted, chosen = exchange_stats(parts, n_t)
    lse = top + jnp.log(total)
    score = chosen - lse
    spread = lse - weighted / total

    logprob = jnp.sum(jnp.where(sel, score[:, None], 0.0), axis=0)
    entropy = jnp.sum(jnp.where(sel, spread[:, None], 0.0), axis=0)
    return (logprob.reshape(seq_count, slot_count), entropy.reshape(seq_count, slot_count))


def solution(mesh):
    return jax.shard_map(
        per_device,
        mesh=mesh,
        in_specs=(
            P("dp", None, "tensor"),
            P(),
            P(None, ("dp", "tensor")),
            P("dp"),
            P("dp", None),
            P("dp", None),
            P("dp", None),
        ),
        out_specs=(P("dp", None), P("dp", None)),
        check_vma=False,
    )
```

```python
import functools

import jax
import jax.numpy as jnp
from jax import lax
from jax.experimental import pallas as pl
from jax.experimental.pallas import tpu as pltpu
from jax.sharding import PartitionSpec as P

MESH = pl.DeviceIdType.MESH
LIVE = 16


def merge(parts):
    tops = parts[:, 0, :]
    top = jnp.max(tops, axis=0, keepdims=True)
    factor = jnp.exp(tops - top)
    total = jnp.sum(parts[:, 1, :] * factor, axis=0, keepdims=True)
    weighted = jnp.sum(parts[:, 2, :] * factor, axis=0, keepdims=True)
    chosen = jnp.sum(parts[:, 3, :], axis=0, keepdims=True)
    return jnp.concatenate([top, total, weighted, chosen], axis=0)


def stats_kernel(part_ref, out_ref, got1, sent, got2, send1, recv1, send2, recv2, local):
    n_dp = part_ref.shape[0]
    n_t = got2.shape[0]
    me = lax.axis_index("dp")
    mt = lax.axis_index("tensor")

    barrier = pltpu.get_barrier_semaphore()

    def greet_dp(i, carry):
        p = lax.rem(me + 1 + i, n_dp)
        pl.semaphore_signal(barrier, 1, device_id=(p, mt), device_id_type=MESH)
        return carry

    def greet_t(i, carry):
        q = lax.rem(mt + 1 + i, n_t)
        pl.semaphore_signal(barrier, 1, device_id=(me, q), device_id_type=MESH)
        return carry

    lax.fori_loop(0, n_dp - 1, greet_dp, 0)
    lax.fori_loop(0, n_t - 1, greet_t, 0)
    pl.semaphore_wait(barrier, n_dp - 1 + n_t - 1)

    def out1(p):
        return pltpu.make_async_remote_copy(
            src_ref=part_ref.at[p], dst_ref=got1.at[me], send_sem=send1.at[p],
            recv_sem=recv1.at[me], device_id=(p, mt), device_id_type=MESH)

    def in1(p):
        return pltpu.make_async_remote_copy(
            src_ref=part_ref.at[p], dst_ref=got1.at[p], send_sem=send1.at[p],
            recv_sem=recv1.at[p], device_id=(p, mt), device_id_type=MESH)

    def start1(i, carry):
        out1(lax.rem(me + 1 + i, n_dp)).start()
        return carry

    lax.fori_loop(0, n_dp - 1, start1, 0)
    own1 = pltpu.make_async_copy(part_ref.at[me], got1.at[me], local.at[0])
    own1.start()

    def finish1(i, carry):
        p = lax.rem(me + 1 + i, n_dp)
        in1(p).wait_recv()
        out1(p).wait_send()
        return carry

    lax.fori_loop(0, n_dp - 1, finish1, 0)
    own1.wait()

    sent[...] = merge(got1[...])

    def out2(q):
        return pltpu.make_async_remote_copy(
            src_ref=sent, dst_ref=got2.at[mt], send_sem=send2.at[q],
            recv_sem=recv2.at[mt], device_id=(me, q), device_id_type=MESH)

    def in2(q):
        return pltpu.make_async_remote_copy(
            src_ref=sent, dst_ref=got2.at[q], send_sem=send2.at[q],
            recv_sem=recv2.at[q], device_id=(me, q), device_id_type=MESH)

    def start2(i, carry):
        out2(lax.rem(mt + 1 + i, n_t)).start()
        return carry

    lax.fori_loop(0, n_t - 1, start2, 0)
    own2 = pltpu.make_async_copy(sent, got2.at[mt], local.at[1])
    own2.start()

    def finish2(i, carry):
        q = lax.rem(mt + 1 + i, n_t)
        in2(q).wait_recv()
        out2(q).wait_send()
        return carry

    lax.fori_loop(0, n_t - 1, finish2, 0)
    own2.wait()

    out_ref[...] = merge(got2[...])


def exchange_stats(parts, n_t):
    n_dp, four, k = parts.shape
    return pl.pallas_call(
        stats_kernel,
        out_shape=jax.ShapeDtypeStruct((four, k), jnp.float32),
        in_specs=[pl.BlockSpec(memory_space=pltpu.VMEM)],
        out_specs=pl.BlockSpec(memory_space=pltpu.VMEM),
        scratch_shapes=[
            pltpu.VMEM((n_dp, four, k), jnp.float32),
            pltpu.VMEM((four, k), jnp.float32),
            pltpu.VMEM((n_t, four, k), jnp.float32),
            pltpu.SemaphoreType.DMA((n_dp,)),
            pltpu.SemaphoreType.DMA((n_dp,)),
            pltpu.SemaphoreType.DMA((n_t,)),
            pltpu.SemaphoreType.DMA((n_t,)),
            pltpu.SemaphoreType.DMA((2,)),
        ],
        compiler_params=pltpu.CompilerParams(collective_id=0, has_side_effects=True),
    )(parts)


def per_device(hidden, gain, head, lengths, offsets, targets, mask):
    seq_count, slot_count = offsets.shape
    slots = seq_count * slot_count
    maxlen = hidden.shape[1]
    n_dp = lax.axis_size("dp")
    n_t = lax.axis_size("tensor")
    k = min(LIVE, slots)

    live = mask.reshape(slots) != 0
    rank = jnp.cumsum(live.astype(jnp.int32)) - 1
    sel = live[None, :] & (rank[None, :] == jnp.arange(k, dtype=jnp.int32)[:, None])
    idx = jnp.sum(jnp.where(sel, jnp.arange(slots, dtype=jnp.int32)[None, :], 0), axis=1)
    seq_of = idx // slot_count
    position = lengths[seq_of] - 1 - offsets.reshape(slots)[idx]
    flat_hidden = hidden.reshape(seq_count * maxlen, hidden.shape[2])
    picked = jnp.take(flat_hidden, seq_of * maxlen + position, axis=0)
    flat_target = targets.reshape(slots)[idx]

    full_rows = lax.all_gather(picked, "tensor", axis=1, tiled=True)
    values = full_rows.astype(jnp.float32)
    meansq = jnp.mean(values * values, axis=-1, keepdims=True)
    normed = (values * lax.rsqrt(meansq + 1e-06) * gain).astype(jnp.bfloat16)

    vocab_width = head.shape[1]
    vocab_start = (lax.axis_index("dp") * n_t + lax.axis_index("tensor")) * vocab_width
    columns = jnp.arange(vocab_width, dtype=jnp.int32)
    width = normed.shape[1]
    digits = jnp.stack([flat_target // 65536, (flat_target // 256) % 256, flat_target % 256], axis=1)
    tail = jnp.zeros((k, 128), jnp.bfloat16).at[:, :3].set(digits.astype(jnp.bfloat16))
    block = jnp.concatenate([normed, tail], axis=1)
    gathered = lax.all_gather(block, "dp", axis=0, tiled=True)
    rows_piece = gathered[:, :width]
    got_digits = gathered[:, width : width + 3].astype(jnp.int32)
    target_piece = got_digits[:, 0] * 65536 + got_digits[:, 1] * 256 + got_digits[:, 2]
    logits = jnp.dot(rows_piece, head, preferred_element_type=jnp.float32)
    top = jnp.max(logits, axis=-1)
    expo = jnp.exp(logits - top[:, None])
    total = jnp.sum(expo, axis=-1)
    weighted = jnp.sum(expo * logits, axis=-1)
    hit = columns[None, :] == (target_piece - vocab_start)[:, None]
    chosen = jnp.sum(jnp.where(hit, logits, 0.0), axis=-1)

    parts = jnp.stack([top, total, weighted, chosen]).reshape(4, n_dp, k).transpose(1, 0, 2)
    top, total, weighted, chosen = exchange_stats(parts, n_t)
    lse = top + jnp.log(total)
    score = chosen - lse
    spread = lse - weighted / total

    logprob = jnp.sum(jnp.where(sel, score[:, None], 0.0), axis=0)
    entropy = jnp.sum(jnp.where(sel, spread[:, None], 0.0), axis=0)
    return (logprob.reshape(seq_count, slot_count), entropy.reshape(seq_count, slot_count))


def solution(mesh):
    return jax.shard_map(
        per_device,
        mesh=mesh,
        in_specs=(
            P("dp", None, "tensor"),
            P(),
            P(None, ("dp", "tensor")),
            P("dp"),
            P("dp", None),
            P("dp", None),
            P("dp", None),
        ),
        out_specs=(P("dp", None), P("dp", None)),
        check_vma=False,
    )
```

```python
import functools

import jax
import jax.numpy as jnp
from jax import lax
from jax.experimental import pallas as pl
from jax.experimental.pallas import tpu as pltpu
from jax.sharding import PartitionSpec as P

MESH = pl.DeviceIdType.MESH
LIVE = 16


def merge(parts):
    tops = parts[:, 0, :]
    top = jnp.max(tops, axis=0, keepdims=True)
    factor = jnp.exp(tops - top)
    total = jnp.sum(parts[:, 1, :] * factor, axis=0, keepdims=True)
    weighted = jnp.sum(parts[:, 2, :] * factor, axis=0, keepdims=True)
    chosen = jnp.sum(parts[:, 3, :], axis=0, keepdims=True)
    return jnp.concatenate([top, total, weighted, chosen], axis=0)


def stats_kernel(part_ref, out_ref, got1, sent, got2, send1, recv1, send2, recv2, local):
    n_dp = part_ref.shape[0]
    n_t = got2.shape[0]
    me = lax.axis_index("dp")
    mt = lax.axis_index("tensor")

    barrier = pltpu.get_barrier_semaphore()

    def greet_dp(i, carry):
        p = lax.rem(me + 1 + i, n_dp)
        pl.semaphore_signal(barrier, 1, device_id=(p, mt), device_id_type=MESH)
        return carry

    def greet_t(i, carry):
        q = lax.rem(mt + 1 + i, n_t)
        pl.semaphore_signal(barrier, 1, device_id=(me, q), device_id_type=MESH)
        return carry

    lax.fori_loop(0, n_dp - 1, greet_dp, 0)
    lax.fori_loop(0, n_t - 1, greet_t, 0)
    pl.semaphore_wait(barrier, n_dp - 1 + n_t - 1)

    def out1(p):
        return pltpu.make_async_remote_copy(
            src_ref=part_ref.at[p], dst_ref=got1.at[me], send_sem=send1.at[p],
            recv_sem=recv1.at[me], device_id=(p, mt), device_id_type=MESH)

    def in1(p):
        return pltpu.make_async_remote_copy(
            src_ref=part_ref.at[p], dst_ref=got1.at[p], send_sem=send1.at[p],
            recv_sem=recv1.at[p], device_id=(p, mt), device_id_type=MESH)

    def start1(i, carry):
        out1(lax.rem(me + 1 + i, n_dp)).start()
        return carry

    lax.fori_loop(0, n_dp - 1, start1, 0)
    own1 = pltpu.make_async_copy(part_ref.at[me], got1.at[me], local.at[0])
    own1.start()

    def finish1(i, carry):
        p = lax.rem(me + 1 + i, n_dp)
        in1(p).wait_recv()
        out1(p).wait_send()
        return carry

    lax.fori_loop(0, n_dp - 1, finish1, 0)
    own1.wait()

    sent[...] = merge(got1[...])

    def out2(q):
        return pltpu.make_async_remote_copy(
            src_ref=sent, dst_ref=got2.at[mt], send_sem=send2.at[q],
            recv_sem=recv2.at[mt], device_id=(me, q), device_id_type=MESH)

    def in2(q):
        return pltpu.make_async_remote_copy(
            src_ref=sent, dst_ref=got2.at[q], send_sem=send2.at[q],
            recv_sem=recv2.at[q], device_id=(me, q), device_id_type=MESH)

    def start2(i, carry):
        out2(lax.rem(mt + 1 + i, n_t)).start()
        return carry

    lax.fori_loop(0, n_t - 1, start2, 0)
    own2 = pltpu.make_async_copy(sent, got2.at[mt], local.at[1])
    own2.start()

    def finish2(i, carry):
        q = lax.rem(mt + 1 + i, n_t)
        in2(q).wait_recv()
        out2(q).wait_send()
        return carry

    lax.fori_loop(0, n_t - 1, finish2, 0)
    own2.wait()

    out_ref[...] = merge(got2[...])


def exchange_stats(parts, n_t):
    n_dp, four, k = parts.shape
    return pl.pallas_call(
        stats_kernel,
        out_shape=jax.ShapeDtypeStruct((four, k), jnp.float32),
        in_specs=[pl.BlockSpec(memory_space=pltpu.VMEM)],
        out_specs=pl.BlockSpec(memory_space=pltpu.VMEM),
        scratch_shapes=[
            pltpu.VMEM((n_dp, four, k), jnp.float32),
            pltpu.VMEM((four, k), jnp.float32),
            pltpu.VMEM((n_t, four, k), jnp.float32),
            pltpu.SemaphoreType.DMA((n_dp,)),
            pltpu.SemaphoreType.DMA((n_dp,)),
            pltpu.SemaphoreType.DMA((n_t,)),
            pltpu.SemaphoreType.DMA((n_t,)),
            pltpu.SemaphoreType.DMA((2,)),
        ],
        compiler_params=pltpu.CompilerParams(collective_id=0, has_side_effects=True),
    )(parts)


def per_device(hidden, gain, head, lengths, offsets, targets, mask):
    seq_count, slot_count = offsets.shape
    slots = seq_count * slot_count
    maxlen = hidden.shape[1]
    n_dp = lax.axis_size("dp")
    n_t = lax.axis_size("tensor")
    k = min(LIVE, slots)

    live = mask.reshape(slots) != 0
    rank = jnp.cumsum(live.astype(jnp.int32)) - 1
    sel = live[None, :] & (rank[None, :] == jnp.arange(k, dtype=jnp.int32)[:, None])
    idx = jnp.sum(jnp.where(sel, jnp.arange(slots, dtype=jnp.int32)[None, :], 0), axis=1)
    seq_of = idx // slot_count
    position = lengths[seq_of] - 1 - offsets.reshape(slots)[idx]
    flat_hidden = hidden.reshape(seq_count * maxlen, hidden.shape[2])
    picked = jnp.take(flat_hidden, seq_of * maxlen + position, axis=0)
    flat_target = targets.reshape(slots)[idx]

    width = picked.shape[1]
    raw = lax.all_gather(picked, ("dp", "tensor"), axis=0, tiled=True).reshape(n_dp, n_t, k, width)
    values = raw.astype(jnp.float32)
    meansq = jnp.sum(values * values, axis=(1, 3), keepdims=True) / (n_t * width)
    scaled = values * lax.rsqrt(meansq + 1e-06) * gain.reshape(1, n_t, 1, width)
    rows_piece = scaled.astype(jnp.bfloat16).transpose(0, 2, 1, 3).reshape(n_dp * k, n_t * width)

    vocab_width = head.shape[1]
    vocab_start = (lax.axis_index("dp") * n_t + lax.axis_index("tensor")) * vocab_width
    columns = jnp.arange(vocab_width, dtype=jnp.int32)
    target_piece = lax.all_gather(flat_target, "dp", axis=0, tiled=True)
    logits = jnp.dot(rows_piece, head, preferred_element_type=jnp.float32)
    top = jnp.max(logits, axis=-1)
    expo = jnp.exp(logits - top[:, None])
    total = jnp.sum(expo, axis=-1)
    weighted = jnp.sum(expo * logits, axis=-1)
    hit = columns[None, :] == (target_piece - vocab_start)[:, None]
    chosen = jnp.sum(jnp.where(hit, logits, 0.0), axis=-1)

    parts = jnp.stack([top, total, weighted, chosen]).reshape(4, n_dp, k).transpose(1, 0, 2)
    top, total, weighted, chosen = exchange_stats(parts, n_t)
    lse = top + jnp.log(total)
    score = chosen - lse
    spread = lse - weighted / total

    logprob = jnp.sum(jnp.where(sel, score[:, None], 0.0), axis=0)
    entropy = jnp.sum(jnp.where(sel, spread[:, None], 0.0), axis=0)
    return (logprob.reshape(seq_count, slot_count), entropy.reshape(seq_count, slot_count))


def solution(mesh):
    return jax.shard_map(
        per_device,
        mesh=mesh,
        in_specs=(
            P("dp", None, "tensor"),
            P(),
            P(None, ("dp", "tensor")),
            P("dp"),
            P("dp", None),
            P("dp", None),
            P("dp", None),
        ),
        out_specs=(P("dp", None), P("dp", None)),
        check_vma=False,
    )
```

```python
import functools

import jax
import jax.numpy as jnp
from jax import lax
from jax.experimental import pallas as pl
from jax.experimental.pallas import tpu as pltpu
from jax.sharding import PartitionSpec as P

MESH = pl.DeviceIdType.MESH
LIVE = 16


def merge(parts):
    tops = parts[:, 0, :]
    top = jnp.max(tops, axis=0, keepdims=True)
    factor = jnp.exp(tops - top)
    total = jnp.sum(parts[:, 1, :] * factor, axis=0, keepdims=True)
    weighted = jnp.sum(parts[:, 2, :] * factor, axis=0, keepdims=True)
    chosen = jnp.sum(parts[:, 3, :], axis=0, keepdims=True)
    return jnp.concatenate([top, total, weighted, chosen], axis=0)


def stats_kernel(part_ref, out_ref, got1, sent, got2, send1, recv1, send2, recv2, local):
    n_dp = part_ref.shape[0]
    n_t = got2.shape[0]
    me = lax.axis_index("dp")
    mt = lax.axis_index("tensor")

    barrier = pltpu.get_barrier_semaphore()

    def greet_dp(i, carry):
        p = lax.rem(me + 1 + i, n_dp)
        pl.semaphore_signal(barrier, 1, device_id=(p, mt), device_id_type=MESH)
        return carry

    def greet_t(i, carry):
        q = lax.rem(mt + 1 + i, n_t)
        pl.semaphore_signal(barrier, 1, device_id=(me, q), device_id_type=MESH)
        return carry

    lax.fori_loop(0, n_dp - 1, greet_dp, 0)
    lax.fori_loop(0, n_t - 1, greet_t, 0)
    pl.semaphore_wait(barrier, n_dp - 1 + n_t - 1)

    def out1(p):
        return pltpu.make_async_remote_copy(
            src_ref=part_ref.at[p], dst_ref=got1.at[me], send_sem=send1.at[p],
            recv_sem=recv1.at[me], device_id=(p, mt), device_id_type=MESH)

    def in1(p):
        return pltpu.make_async_remote_copy(
            src_ref=part_ref.at[p], dst_ref=got1.at[p], send_sem=send1.at[p],
            recv_sem=recv1.at[p], device_id=(p, mt), device_id_type=MESH)

    def start1(i, carry):
        out1(lax.rem(me + 1 + i, n_dp)).start()
        return carry

    lax.fori_loop(0, n_dp - 1, start1, 0)
    own1 = pltpu.make_async_copy(part_ref.at[me], got1.at[me], local.at[0])
    own1.start()

    def finish1(i, carry):
        p = lax.rem(me + 1 + i, n_dp)
        in1(p).wait_recv()
        out1(p).wait_send()
        return carry

    lax.fori_loop(0, n_dp - 1, finish1, 0)
    own1.wait()

    sent[...] = merge(got1[...])

    def out2(q):
        return pltpu.make_async_remote_copy(
            src_ref=sent, dst_ref=got2.at[mt], send_sem=send2.at[q],
            recv_sem=recv2.at[mt], device_id=(me, q), device_id_type=MESH)

    def in2(q):
        return pltpu.make_async_remote_copy(
            src_ref=sent, dst_ref=got2.at[q], send_sem=send2.at[q],
            recv_sem=recv2.at[q], device_id=(me, q), device_id_type=MESH)

    def start2(i, carry):
        out2(lax.rem(mt + 1 + i, n_t)).start()
        return carry

    lax.fori_loop(0, n_t - 1, start2, 0)
    own2 = pltpu.make_async_copy(sent, got2.at[mt], local.at[1])
    own2.start()

    def finish2(i, carry):
        q = lax.rem(mt + 1 + i, n_t)
        in2(q).wait_recv()
        out2(q).wait_send()
        return carry

    lax.fori_loop(0, n_t - 1, finish2, 0)
    own2.wait()

    out_ref[...] = merge(got2[...])


def exchange_stats(parts, n_t):
    n_dp, four, k = parts.shape
    return pl.pallas_call(
        stats_kernel,
        out_shape=jax.ShapeDtypeStruct((four, k), jnp.float32),
        in_specs=[pl.BlockSpec(memory_space=pltpu.VMEM)],
        out_specs=pl.BlockSpec(memory_space=pltpu.VMEM),
        scratch_shapes=[
            pltpu.VMEM((n_dp, four, k), jnp.float32),
            pltpu.VMEM((four, k), jnp.float32),
            pltpu.VMEM((n_t, four, k), jnp.float32),
            pltpu.SemaphoreType.DMA((n_dp,)),
            pltpu.SemaphoreType.DMA((n_dp,)),
            pltpu.SemaphoreType.DMA((n_t,)),
            pltpu.SemaphoreType.DMA((n_t,)),
            pltpu.SemaphoreType.DMA((2,)),
        ],
        compiler_params=pltpu.CompilerParams(collective_id=0, has_side_effects=True),
    )(parts)


def tensor_kernel(rows_ref, out_ref, got, send, recv, local):
    n_t = got.shape[0]
    me = lax.axis_index("dp")
    mt = lax.axis_index("tensor")

    barrier = pltpu.get_barrier_semaphore()

    def greet(i, carry):
        q = lax.rem(mt + 1 + i, n_t)
        pl.semaphore_signal(barrier, 1, device_id=(me, q), device_id_type=MESH)
        return carry

    lax.fori_loop(0, n_t - 1, greet, 0)
    pl.semaphore_wait(barrier, n_t - 1)

    def outgoing(q):
        return pltpu.make_async_remote_copy(
            src_ref=rows_ref, dst_ref=got.at[mt], send_sem=send.at[q],
            recv_sem=recv.at[mt], device_id=(me, q), device_id_type=MESH)

    def incoming(q):
        return pltpu.make_async_remote_copy(
            src_ref=rows_ref, dst_ref=got.at[q], send_sem=send.at[q],
            recv_sem=recv.at[q], device_id=(me, q), device_id_type=MESH)

    def start(i, carry):
        outgoing(lax.rem(mt + 1 + i, n_t)).start()
        return carry

    lax.fori_loop(0, n_t - 1, start, 0)
    own = pltpu.make_async_copy(rows_ref, got.at[mt], local.at[0])
    own.start()

    def finish(i, carry):
        q = lax.rem(mt + 1 + i, n_t)
        incoming(q).wait_recv()
        outgoing(q).wait_send()
        return carry

    lax.fori_loop(0, n_t - 1, finish, 0)
    own.wait()
    out_ref[...] = got[...]


def gather_tensor(rows, n_t):
    k, width = rows.shape
    return pl.pallas_call(
        tensor_kernel,
        out_shape=jax.ShapeDtypeStruct((n_t, k, width), rows.dtype),
        in_specs=[pl.BlockSpec(memory_space=pltpu.VMEM)],
        out_specs=pl.BlockSpec(memory_space=pltpu.VMEM),
        scratch_shapes=[
            pltpu.VMEM((n_t, k, width), rows.dtype),
            pltpu.SemaphoreType.DMA((n_t,)),
            pltpu.SemaphoreType.DMA((n_t,)),
            pltpu.SemaphoreType.DMA((1,)),
        ],
        compiler_params=pltpu.CompilerParams(collective_id=1, has_side_effects=True),
    )(rows)


def per_device(hidden, gain, head, lengths, offsets, targets, mask):
    seq_count, slot_count = offsets.shape
    slots = seq_count * slot_count
    maxlen = hidden.shape[1]
    n_dp = lax.axis_size("dp")
    n_t = lax.axis_size("tensor")
    k = min(LIVE, slots)

    live = mask.reshape(slots) != 0
    rank = jnp.cumsum(live.astype(jnp.int32)) - 1
    sel = live[None, :] & (rank[None, :] == jnp.arange(k, dtype=jnp.int32)[:, None])
    idx = jnp.sum(jnp.where(sel, jnp.arange(slots, dtype=jnp.int32)[None, :], 0), axis=1)
    seq_of = idx // slot_count
    position = lengths[seq_of] - 1 - offsets.reshape(slots)[idx]
    flat_hidden = hidden.reshape(seq_count * maxlen, hidden.shape[2])
    picked = jnp.take(flat_hidden, seq_of * maxlen + position, axis=0)
    flat_target = targets.reshape(slots)[idx]

    full_rows = gather_tensor(picked, n_t).transpose(1, 0, 2).reshape(k, n_t * picked.shape[1])
    values = full_rows.astype(jnp.float32)
    meansq = jnp.mean(values * values, axis=-1, keepdims=True)
    normed = (values * lax.rsqrt(meansq + 1e-06) * gain).astype(jnp.bfloat16)

    vocab_width = head.shape[1]
    vocab_start = (lax.axis_index("dp") * n_t + lax.axis_index("tensor")) * vocab_width
    columns = jnp.arange(vocab_width, dtype=jnp.int32)
    rows_piece = lax.all_gather(normed, "dp", axis=0, tiled=True)
    target_piece = lax.all_gather(flat_target, "dp", axis=0, tiled=True)
    logits = jnp.dot(rows_piece, head, preferred_element_type=jnp.float32)
    top = jnp.max(logits, axis=-1)
    expo = jnp.exp(logits - top[:, None])
    total = jnp.sum(expo, axis=-1)
    weighted = jnp.sum(expo * logits, axis=-1)
    hit = columns[None, :] == (target_piece - vocab_start)[:, None]
    chosen = jnp.sum(jnp.where(hit, logits, 0.0), axis=-1)

    parts = jnp.stack([top, total, weighted, chosen]).reshape(4, n_dp, k).transpose(1, 0, 2)
    top, total, weighted, chosen = exchange_stats(parts, n_t)
    lse = top + jnp.log(total)
    score = chosen - lse
    spread = lse - weighted / total

    logprob = jnp.sum(jnp.where(sel, score[:, None], 0.0), axis=0)
    entropy = jnp.sum(jnp.where(sel, spread[:, None], 0.0), axis=0)
    return (logprob.reshape(seq_count, slot_count), entropy.reshape(seq_count, slot_count))


def solution(mesh):
    return jax.shard_map(
        per_device,
        mesh=mesh,
        in_specs=(
            P("dp", None, "tensor"),
            P(),
            P(None, ("dp", "tensor")),
            P("dp"),
            P("dp", None),
            P("dp", None),
            P("dp", None),
        ),
        out_specs=(P("dp", None), P("dp", None)),
        check_vma=False,
    )
```

```python
import functools

import jax
import jax.numpy as jnp
from jax import lax
from jax.experimental import pallas as pl
from jax.experimental.pallas import tpu as pltpu
from jax.sharding import PartitionSpec as P

MESH = pl.DeviceIdType.MESH
LIVE = 16


def merge(parts):
    tops = parts[:, 0, :]
    top = jnp.max(tops, axis=0, keepdims=True)
    factor = jnp.exp(tops - top)
    total = jnp.sum(parts[:, 1, :] * factor, axis=0, keepdims=True)
    weighted = jnp.sum(parts[:, 2, :] * factor, axis=0, keepdims=True)
    chosen = jnp.sum(parts[:, 3, :], axis=0, keepdims=True)
    return jnp.concatenate([top, total, weighted, chosen], axis=0)


def stats_kernel(part_ref, out_ref, got1, sent, got2, send1, recv1, send2, recv2, local):
    n_dp = part_ref.shape[0]
    n_t = got2.shape[0]
    me = lax.axis_index("dp")
    mt = lax.axis_index("tensor")

    barrier = pltpu.get_barrier_semaphore()

    def greet_dp(i, carry):
        p = lax.rem(me + 1 + i, n_dp)
        pl.semaphore_signal(barrier, 1, device_id=(p, mt), device_id_type=MESH)
        return carry

    def greet_t(i, carry):
        q = lax.rem(mt + 1 + i, n_t)
        pl.semaphore_signal(barrier, 1, device_id=(me, q), device_id_type=MESH)
        return carry

    lax.fori_loop(0, n_dp - 1, greet_dp, 0)
    lax.fori_loop(0, n_t - 1, greet_t, 0)
    pl.semaphore_wait(barrier, n_dp - 1 + n_t - 1)

    def out1(p):
        return pltpu.make_async_remote_copy(
            src_ref=part_ref.at[p], dst_ref=got1.at[me], send_sem=send1.at[p],
            recv_sem=recv1.at[me], device_id=(p, mt), device_id_type=MESH)

    def in1(p):
        return pltpu.make_async_remote_copy(
            src_ref=part_ref.at[p], dst_ref=got1.at[p], send_sem=send1.at[p],
            recv_sem=recv1.at[p], device_id=(p, mt), device_id_type=MESH)

    def start1(i, carry):
        out1(lax.rem(me + 1 + i, n_dp)).start()
        return carry

    lax.fori_loop(0, n_dp - 1, start1, 0)
    own1 = pltpu.make_async_copy(part_ref.at[me], got1.at[me], local.at[0])
    own1.start()

    def finish1(i, carry):
        p = lax.rem(me + 1 + i, n_dp)
        in1(p).wait_recv()
        out1(p).wait_send()
        return carry

    lax.fori_loop(0, n_dp - 1, finish1, 0)
    own1.wait()

    sent[...] = merge(got1[...])

    def out2(q):
        return pltpu.make_async_remote_copy(
            src_ref=sent, dst_ref=got2.at[mt], send_sem=send2.at[q],
            recv_sem=recv2.at[mt], device_id=(me, q), device_id_type=MESH)

    def in2(q):
        return pltpu.make_async_remote_copy(
            src_ref=sent, dst_ref=got2.at[q], send_sem=send2.at[q],
            recv_sem=recv2.at[q], device_id=(me, q), device_id_type=MESH)

    def start2(i, carry):
        out2(lax.rem(mt + 1 + i, n_t)).start()
        return carry

    lax.fori_loop(0, n_t - 1, start2, 0)
    own2 = pltpu.make_async_copy(sent, got2.at[mt], local.at[1])
    own2.start()

    def finish2(i, carry):
        q = lax.rem(mt + 1 + i, n_t)
        in2(q).wait_recv()
        out2(q).wait_send()
        return carry

    lax.fori_loop(0, n_t - 1, finish2, 0)
    own2.wait()

    out_ref[...] = merge(got2[...])


def exchange_stats(parts, n_t):
    n_dp, four, k = parts.shape
    return pl.pallas_call(
        stats_kernel,
        out_shape=jax.ShapeDtypeStruct((four, k), jnp.float32),
        in_specs=[pl.BlockSpec(memory_space=pltpu.VMEM)],
        out_specs=pl.BlockSpec(memory_space=pltpu.VMEM),
        scratch_shapes=[
            pltpu.VMEM((n_dp, four, k), jnp.float32),
            pltpu.VMEM((four, k), jnp.float32),
            pltpu.VMEM((n_t, four, k), jnp.float32),
            pltpu.SemaphoreType.DMA((n_dp,)),
            pltpu.SemaphoreType.DMA((n_dp,)),
            pltpu.SemaphoreType.DMA((n_t,)),
            pltpu.SemaphoreType.DMA((n_t,)),
            pltpu.SemaphoreType.DMA((2,)),
        ],
        compiler_params=pltpu.CompilerParams(collective_id=0, has_side_effects=True),
    )(parts)


def tensor_kernel(rows_ref, out_ref, got, send, recv, local):
    n_t = got.shape[0]
    me = lax.axis_index("dp")
    mt = lax.axis_index("tensor")

    barrier = pltpu.get_barrier_semaphore()

    def greet(i, carry):
        q = lax.rem(mt + 1 + i, n_t)
        pl.semaphore_signal(barrier, 1, device_id=(me, q), device_id_type=MESH)
        return carry

    lax.fori_loop(0, n_t - 1, greet, 0)
    pl.semaphore_wait(barrier, n_t - 1)

    def outgoing(q):
        return pltpu.make_async_remote_copy(
            src_ref=rows_ref, dst_ref=got.at[mt], send_sem=send.at[q],
            recv_sem=recv.at[mt], device_id=(me, q), device_id_type=MESH)

    def incoming(q):
        return pltpu.make_async_remote_copy(
            src_ref=rows_ref, dst_ref=got.at[q], send_sem=send.at[q],
            recv_sem=recv.at[q], device_id=(me, q), device_id_type=MESH)

    def start(i, carry):
        outgoing(lax.rem(mt + 1 + i, n_t)).start()
        return carry

    lax.fori_loop(0, n_t - 1, start, 0)
    own = pltpu.make_async_copy(rows_ref, got.at[mt], local.at[0])
    own.start()

    def finish(i, carry):
        q = lax.rem(mt + 1 + i, n_t)
        incoming(q).wait_recv()
        outgoing(q).wait_send()
        return carry

    lax.fori_loop(0, n_t - 1, finish, 0)
    own.wait()
    out_ref[...] = got[...]


def gather_tensor(rows, n_t):
    k, width = rows.shape
    return pl.pallas_call(
        tensor_kernel,
        out_shape=jax.ShapeDtypeStruct((n_t, k, width), rows.dtype),
        in_specs=[pl.BlockSpec(memory_space=pltpu.VMEM)],
        out_specs=pl.BlockSpec(memory_space=pltpu.VMEM),
        scratch_shapes=[
            pltpu.VMEM((n_t, k, width), rows.dtype),
            pltpu.SemaphoreType.DMA((n_t,)),
            pltpu.SemaphoreType.DMA((n_t,)),
            pltpu.SemaphoreType.DMA((1,)),
        ],
        compiler_params=pltpu.CompilerParams(collective_id=1, has_side_effects=True),
    )(rows)


def rows_kernel(block_ref, out_ref, send_d, recv_d, send_f, recv_f, send_s, recv_s, local):
    n_chip = send_d.shape[0]
    me = lax.axis_index("dp")
    mt = lax.axis_index("tensor")
    chip = me // 2
    core = me % 2
    sib = me + 1 - 2 * core

    barrier = pltpu.get_barrier_semaphore()

    def greet(i, carry):
        c = lax.rem(chip + 1 + i, n_chip)
        pl.semaphore_signal(barrier, 1, device_id=(c * 2 + core, mt), device_id_type=MESH)
        return carry

    lax.fori_loop(0, n_chip - 1, greet, 0)
    pl.semaphore_signal(barrier, 1, device_id=(sib, mt), device_id_type=MESH)
    pl.semaphore_wait(barrier, n_chip)

    def direct(c):
        return pltpu.make_async_remote_copy(
            src_ref=block_ref, dst_ref=out_ref.at[me], send_sem=send_d.at[c],
            recv_sem=recv_d.at[chip], device_id=(c * 2 + core, mt), device_id_type=MESH)

    def direct_in(c):
        return pltpu.make_async_remote_copy(
            src_ref=block_ref, dst_ref=out_ref.at[c * 2 + core], send_sem=send_d.at[c],
            recv_sem=recv_d.at[c], device_id=(c * 2 + core, mt), device_id_type=MESH)

    def forward(c):
        return pltpu.make_async_remote_copy(
            src_ref=out_ref.at[c * 2 + core], dst_ref=out_ref.at[c * 2 + core], send_sem=send_f.at[c],
            recv_sem=recv_f.at[c], device_id=(sib, mt), device_id_type=MESH)

    def forward_in(c):
        return pltpu.make_async_remote_copy(
            src_ref=out_ref.at[c * 2 + 1 - core], dst_ref=out_ref.at[c * 2 + 1 - core],
            send_sem=send_f.at[c], recv_sem=recv_f.at[c], device_id=(sib, mt), device_id_type=MESH)

    to_sib = pltpu.make_async_remote_copy(
        src_ref=block_ref, dst_ref=out_ref.at[me], send_sem=send_s.at[0],
        recv_sem=recv_s.at[0], device_id=(sib, mt), device_id_type=MESH)
    from_sib = pltpu.make_async_remote_copy(
        src_ref=block_ref, dst_ref=out_ref.at[sib], send_sem=send_s.at[0],
        recv_sem=recv_s.at[0], device_id=(sib, mt), device_id_type=MESH)

    def start(i, carry):
        direct(lax.rem(chip + 1 + i, n_chip)).start()
        return carry

    lax.fori_loop(0, n_chip - 1, start, 0)
    to_sib.start()
    own = pltpu.make_async_copy(block_ref, out_ref.at[me], local.at[0])
    own.start()

    def relay(i, carry):
        c = lax.rem(chip + n_chip - 1 - i, n_chip)
        direct_in(c).wait_recv()
        forward(c).start()
        return carry

    lax.fori_loop(0, n_chip - 1, relay, 0)

    def finish(i, carry):
        c = lax.rem(chip + 1 + i, n_chip)
        forward_in(c).wait_recv()
        direct(c).wait_send()
        forward(c).wait_send()
        return carry

    lax.fori_loop(0, n_chip - 1, finish, 0)
    from_sib.wait_recv()
    to_sib.wait_send()
    own.wait()


def gather_rows(block, n_dp):
    n_chip = n_dp // 2
    return pl.pallas_call(
        rows_kernel,
        out_shape=jax.ShapeDtypeStruct((n_dp,) + block.shape, block.dtype),
        in_specs=[pl.BlockSpec(memory_space=pltpu.VMEM)],
        out_specs=pl.BlockSpec(memory_space=pl.ANY),
        scratch_shapes=[
            pltpu.SemaphoreType.DMA((n_chip,)),
            pltpu.SemaphoreType.DMA((n_chip,)),
            pltpu.SemaphoreType.DMA((n_chip,)),
            pltpu.SemaphoreType.DMA((n_chip,)),
            pltpu.SemaphoreType.DMA((1,)),
            pltpu.SemaphoreType.DMA((1,)),
            pltpu.SemaphoreType.DMA((1,)),
        ],
        compiler_params=pltpu.CompilerParams(collective_id=2, has_side_effects=True),
    )(block)


def per_device(hidden, gain, head, lengths, offsets, targets, mask):
    seq_count, slot_count = offsets.shape
    slots = seq_count * slot_count
    maxlen = hidden.shape[1]
    n_dp = lax.axis_size("dp")
    n_t = lax.axis_size("tensor")
    k = min(LIVE, slots)

    live = mask.reshape(slots) != 0
    rank = jnp.cumsum(live.astype(jnp.int32)) - 1
    sel = live[None, :] & (rank[None, :] == jnp.arange(k, dtype=jnp.int32)[:, None])
    idx = jnp.sum(jnp.where(sel, jnp.arange(slots, dtype=jnp.int32)[None, :], 0), axis=1)
    seq_of = idx // slot_count
    position = lengths[seq_of] - 1 - offsets.reshape(slots)[idx]
    flat_hidden = hidden.reshape(seq_count * maxlen, hidden.shape[2])
    picked = jnp.take(flat_hidden, seq_of * maxlen + position, axis=0)
    flat_target = targets.reshape(slots)[idx]

    full_rows = gather_tensor(picked, n_t).transpose(1, 0, 2).reshape(k, n_t * picked.shape[1])
    values = full_rows.astype(jnp.float32)
    meansq = jnp.mean(values * values, axis=-1, keepdims=True)
    normed = (values * lax.rsqrt(meansq + 1e-06) * gain).astype(jnp.bfloat16)

    vocab_width = head.shape[1]
    vocab_start = (lax.axis_index("dp") * n_t + lax.axis_index("tensor")) * vocab_width
    columns = jnp.arange(vocab_width, dtype=jnp.int32)
    width = normed.shape[1]
    digits = jnp.stack([flat_target // 65536, (flat_target // 256) % 256, flat_target % 256], axis=1)
    tail = jnp.zeros((k, 128), jnp.bfloat16).at[:, :3].set(digits.astype(jnp.bfloat16))
    block = jnp.concatenate([normed, tail], axis=1)
    gathered = gather_rows(block, n_dp).reshape(n_dp * k, width + 128)
    rows_piece = gathered[:, :width]
    got_digits = gathered[:, width : width + 3].astype(jnp.int32)
    target_piece = got_digits[:, 0] * 65536 + got_digits[:, 1] * 256 + got_digits[:, 2]
    logits = jnp.dot(rows_piece, head, preferred_element_type=jnp.float32)
    top = jnp.max(logits, axis=-1)
    expo = jnp.exp(logits - top[:, None])
    total = jnp.sum(expo, axis=-1)
    weighted = jnp.sum(expo * logits, axis=-1)
    hit = columns[None, :] == (target_piece - vocab_start)[:, None]
    chosen = jnp.sum(jnp.where(hit, logits, 0.0), axis=-1)

    parts = jnp.stack([top, total, weighted, chosen]).reshape(4, n_dp, k).transpose(1, 0, 2)
    top, total, weighted, chosen = exchange_stats(parts, n_t)
    lse = top + jnp.log(total)
    score = chosen - lse
    spread = lse - weighted / total

    logprob = jnp.sum(jnp.where(sel, score[:, None], 0.0), axis=0)
    entropy = jnp.sum(jnp.where(sel, spread[:, None], 0.0), axis=0)
    return (logprob.reshape(seq_count, slot_count), entropy.reshape(seq_count, slot_count))


def solution(mesh):
    return jax.shard_map(
        per_device,
        mesh=mesh,
        in_specs=(
            P("dp", None, "tensor"),
            P(),
            P(None, ("dp", "tensor")),
            P("dp"),
            P("dp", None),
            P("dp", None),
            P("dp", None),
        ),
        out_specs=(P("dp", None), P("dp", None)),
        check_vma=False,
    )
```

```python
import functools

import jax
import jax.numpy as jnp
from jax import lax
from jax.experimental import pallas as pl
from jax.experimental.pallas import tpu as pltpu
from jax.sharding import PartitionSpec as P

MESH = pl.DeviceIdType.MESH
LIVE = 16


def merge(parts):
    tops = parts[:, 0, :]
    top = jnp.max(tops, axis=0, keepdims=True)
    factor = jnp.exp(tops - top)
    total = jnp.sum(parts[:, 1, :] * factor, axis=0, keepdims=True)
    weighted = jnp.sum(parts[:, 2, :] * factor, axis=0, keepdims=True)
    chosen = jnp.sum(parts[:, 3, :], axis=0, keepdims=True)
    return jnp.concatenate([top, total, weighted, chosen], axis=0)


def stats_kernel(part_ref, out_ref, got1, sent, got2, send1, recv1, send2, recv2, local):
    n_dp = part_ref.shape[0]
    n_t = got2.shape[0]
    me = lax.axis_index("dp")
    mt = lax.axis_index("tensor")

    barrier = pltpu.get_barrier_semaphore()

    def greet_dp(i, carry):
        p = lax.rem(me + 1 + i, n_dp)
        pl.semaphore_signal(barrier, 1, device_id=(p, mt), device_id_type=MESH)
        return carry

    def greet_t(i, carry):
        q = lax.rem(mt + 1 + i, n_t)
        pl.semaphore_signal(barrier, 1, device_id=(me, q), device_id_type=MESH)
        return carry

    lax.fori_loop(0, n_dp - 1, greet_dp, 0)
    lax.fori_loop(0, n_t - 1, greet_t, 0)
    pl.semaphore_wait(barrier, n_dp - 1 + n_t - 1)

    def out1(p):
        return pltpu.make_async_remote_copy(
            src_ref=part_ref.at[p], dst_ref=got1.at[me], send_sem=send1.at[p],
            recv_sem=recv1.at[me], device_id=(p, mt), device_id_type=MESH)

    def in1(p):
        return pltpu.make_async_remote_copy(
            src_ref=part_ref.at[p], dst_ref=got1.at[p], send_sem=send1.at[p],
            recv_sem=recv1.at[p], device_id=(p, mt), device_id_type=MESH)

    def start1(i, carry):
        out1(lax.rem(me + 1 + i, n_dp)).start()
        return carry

    lax.fori_loop(0, n_dp - 1, start1, 0)
    own1 = pltpu.make_async_copy(part_ref.at[me], got1.at[me], local.at[0])
    own1.start()

    def finish1(i, carry):
        p = lax.rem(me + 1 + i, n_dp)
        in1(p).wait_recv()
        out1(p).wait_send()
        return carry

    lax.fori_loop(0, n_dp - 1, finish1, 0)
    own1.wait()

    sent[...] = merge(got1[...])

    def out2(q):
        return pltpu.make_async_remote_copy(
            src_ref=sent, dst_ref=got2.at[mt], send_sem=send2.at[q],
            recv_sem=recv2.at[mt], device_id=(me, q), device_id_type=MESH)

    def in2(q):
        return pltpu.make_async_remote_copy(
            src_ref=sent, dst_ref=got2.at[q], send_sem=send2.at[q],
            recv_sem=recv2.at[q], device_id=(me, q), device_id_type=MESH)

    def start2(i, carry):
        out2(lax.rem(mt + 1 + i, n_t)).start()
        return carry

    lax.fori_loop(0, n_t - 1, start2, 0)
    own2 = pltpu.make_async_copy(sent, got2.at[mt], local.at[1])
    own2.start()

    def finish2(i, carry):
        q = lax.rem(mt + 1 + i, n_t)
        in2(q).wait_recv()
        out2(q).wait_send()
        return carry

    lax.fori_loop(0, n_t - 1, finish2, 0)
    own2.wait()

    out_ref[...] = merge(got2[...])


def exchange_stats(parts, n_t):
    n_dp, four, k = parts.shape
    return pl.pallas_call(
        stats_kernel,
        out_shape=jax.ShapeDtypeStruct((four, k), jnp.float32),
        in_specs=[pl.BlockSpec(memory_space=pltpu.VMEM)],
        out_specs=pl.BlockSpec(memory_space=pltpu.VMEM),
        scratch_shapes=[
            pltpu.VMEM((n_dp, four, k), jnp.float32),
            pltpu.VMEM((four, k), jnp.float32),
            pltpu.VMEM((n_t, four, k), jnp.float32),
            pltpu.SemaphoreType.DMA((n_dp,)),
            pltpu.SemaphoreType.DMA((n_dp,)),
            pltpu.SemaphoreType.DMA((n_t,)),
            pltpu.SemaphoreType.DMA((n_t,)),
            pltpu.SemaphoreType.DMA((2,)),
        ],
        compiler_params=pltpu.CompilerParams(collective_id=0, has_side_effects=True),
    )(parts)


def tensor_kernel(rows_ref, gain_ref, tail_ref, out_ref, got, send, recv, local):
    n_t = got.shape[0]
    me = lax.axis_index("dp")
    mt = lax.axis_index("tensor")

    barrier = pltpu.get_barrier_semaphore()

    def greet(i, carry):
        q = lax.rem(mt + 1 + i, n_t)
        pl.semaphore_signal(barrier, 1, device_id=(me, q), device_id_type=MESH)
        return carry

    lax.fori_loop(0, n_t - 1, greet, 0)
    pl.semaphore_wait(barrier, n_t - 1)

    def outgoing(q):
        return pltpu.make_async_remote_copy(
            src_ref=rows_ref, dst_ref=got.at[mt], send_sem=send.at[q],
            recv_sem=recv.at[mt], device_id=(me, q), device_id_type=MESH)

    def incoming(q):
        return pltpu.make_async_remote_copy(
            src_ref=rows_ref, dst_ref=got.at[q], send_sem=send.at[q],
            recv_sem=recv.at[q], device_id=(me, q), device_id_type=MESH)

    def start(i, carry):
        outgoing(lax.rem(mt + 1 + i, n_t)).start()
        return carry

    lax.fori_loop(0, n_t - 1, start, 0)
    own = pltpu.make_async_copy(rows_ref, got.at[mt], local.at[0])
    own.start()

    def finish(i, carry):
        q = lax.rem(mt + 1 + i, n_t)
        incoming(q).wait_recv()
        outgoing(q).wait_send()
        return carry

    lax.fori_loop(0, n_t - 1, finish, 0)
    own.wait()

    width = got.shape[2]
    values = got[...].astype(jnp.float32)
    sumsq = jnp.sum(jnp.sum(values * values, axis=0), axis=-1, keepdims=True)
    scale = lax.rsqrt(sumsq / (n_t * width) + 1e-06)
    for t in range(n_t):
        piece = values[t] * scale * gain_ref[pl.ds(t, 1), :]
        out_ref[:, pl.ds(t * width, width)] = piece.astype(out_ref.dtype)
    out_ref[:, pl.ds(n_t * width, tail_ref.shape[1])] = tail_ref[...]


def normed_block(rows, gain, tail, n_t):
    k, width = rows.shape
    return pl.pallas_call(
        tensor_kernel,
        out_shape=jax.ShapeDtypeStruct((k, n_t * width + tail.shape[1]), rows.dtype),
        in_specs=[pl.BlockSpec(memory_space=pltpu.VMEM)] * 3,
        out_specs=pl.BlockSpec(memory_space=pltpu.VMEM),
        scratch_shapes=[
            pltpu.VMEM((n_t, k, width), rows.dtype),
            pltpu.SemaphoreType.DMA((n_t,)),
            pltpu.SemaphoreType.DMA((n_t,)),
            pltpu.SemaphoreType.DMA((1,)),
        ],
        compiler_params=pltpu.CompilerParams(collective_id=1, has_side_effects=True),
    )(rows, gain.reshape(n_t, width), tail)


def rows_kernel(block_ref, out_ref, send_d, recv_d, send_f, recv_f, send_s, recv_s, local):
    n_chip = send_d.shape[0]
    me = lax.axis_index("dp")
    mt = lax.axis_index("tensor")
    chip = me // 2
    core = me % 2
    sib = me + 1 - 2 * core

    barrier = pltpu.get_barrier_semaphore()

    def greet(i, carry):
        c = lax.rem(chip + 1 + i, n_chip)
        pl.semaphore_signal(barrier, 1, device_id=(c * 2 + core, mt), device_id_type=MESH)
        return carry

    lax.fori_loop(0, n_chip - 1, greet, 0)
    pl.semaphore_signal(barrier, 1, device_id=(sib, mt), device_id_type=MESH)
    pl.semaphore_wait(barrier, n_chip)

    def direct(c):
        return pltpu.make_async_remote_copy(
            src_ref=block_ref, dst_ref=out_ref.at[me], send_sem=send_d.at[c],
            recv_sem=recv_d.at[chip], device_id=(c * 2 + core, mt), device_id_type=MESH)

    def direct_in(c):
        return pltpu.make_async_remote_copy(
            src_ref=block_ref, dst_ref=out_ref.at[c * 2 + core], send_sem=send_d.at[c],
            recv_sem=recv_d.at[c], device_id=(c * 2 + core, mt), device_id_type=MESH)

    def forward(c):
        return pltpu.make_async_remote_copy(
            src_ref=out_ref.at[c * 2 + core], dst_ref=out_ref.at[c * 2 + core], send_sem=send_f.at[c],
            recv_sem=recv_f.at[c], device_id=(sib, mt), device_id_type=MESH)

    def forward_in(c):
        return pltpu.make_async_remote_copy(
            src_ref=out_ref.at[c * 2 + 1 - core], dst_ref=out_ref.at[c * 2 + 1 - core],
            send_sem=send_f.at[c], recv_sem=recv_f.at[c], device_id=(sib, mt), device_id_type=MESH)

    to_sib = pltpu.make_async_remote_copy(
        src_ref=block_ref, dst_ref=out_ref.at[me], send_sem=send_s.at[0],
        recv_sem=recv_s.at[0], device_id=(sib, mt), device_id_type=MESH)
    from_sib = pltpu.make_async_remote_copy(
        src_ref=block_ref, dst_ref=out_ref.at[sib], send_sem=send_s.at[0],
        recv_sem=recv_s.at[0], device_id=(sib, mt), device_id_type=MESH)

    def start(i, carry):
        direct(lax.rem(chip + 1 + i, n_chip)).start()
        return carry

    lax.fori_loop(0, n_chip - 1, start, 0)
    to_sib.start()
    own = pltpu.make_async_copy(block_ref, out_ref.at[me], local.at[0])
    own.start()

    def relay(i, carry):
        c = lax.rem(chip + n_chip - 1 - i, n_chip)
        direct_in(c).wait_recv()
        forward(c).start()
        return carry

    lax.fori_loop(0, n_chip - 1, relay, 0)

    def finish(i, carry):
        c = lax.rem(chip + 1 + i, n_chip)
        forward_in(c).wait_recv()
        direct(c).wait_send()
        forward(c).wait_send()
        return carry

    lax.fori_loop(0, n_chip - 1, finish, 0)
    from_sib.wait_recv()
    to_sib.wait_send()
    own.wait()


def gather_rows(block, n_dp):
    n_chip = n_dp // 2
    return pl.pallas_call(
        rows_kernel,
        out_shape=jax.ShapeDtypeStruct((n_dp,) + block.shape, block.dtype),
        in_specs=[pl.BlockSpec(memory_space=pltpu.VMEM)],
        out_specs=pl.BlockSpec(memory_space=pl.ANY),
        scratch_shapes=[
            pltpu.SemaphoreType.DMA((n_chip,)),
            pltpu.SemaphoreType.DMA((n_chip,)),
            pltpu.SemaphoreType.DMA((n_chip,)),
            pltpu.SemaphoreType.DMA((n_chip,)),
            pltpu.SemaphoreType.DMA((1,)),
            pltpu.SemaphoreType.DMA((1,)),
            pltpu.SemaphoreType.DMA((1,)),
        ],
        compiler_params=pltpu.CompilerParams(collective_id=2, has_side_effects=True),
    )(block)


def per_device(hidden, gain, head, lengths, offsets, targets, mask):
    seq_count, slot_count = offsets.shape
    slots = seq_count * slot_count
    maxlen = hidden.shape[1]
    n_dp = lax.axis_size("dp")
    n_t = lax.axis_size("tensor")
    k = min(LIVE, slots)

    live = mask.reshape(slots) != 0
    rank = jnp.cumsum(live.astype(jnp.int32)) - 1
    sel = live[None, :] & (rank[None, :] == jnp.arange(k, dtype=jnp.int32)[:, None])
    idx = jnp.sum(jnp.where(sel, jnp.arange(slots, dtype=jnp.int32)[None, :], 0), axis=1)
    seq_of = idx // slot_count
    position = lengths[seq_of] - 1 - offsets.reshape(slots)[idx]
    flat_hidden = hidden.reshape(seq_count * maxlen, hidden.shape[2])
    picked = jnp.take(flat_hidden, seq_of * maxlen + position, axis=0)
    flat_target = targets.reshape(slots)[idx]

    vocab_width = head.shape[1]
    vocab_start = (lax.axis_index("dp") * n_t + lax.axis_index("tensor")) * vocab_width
    columns = jnp.arange(vocab_width, dtype=jnp.int32)
    width = n_t * picked.shape[1]
    digits = jnp.stack([flat_target // 65536, (flat_target // 256) % 256, flat_target % 256], axis=1)
    tail = jnp.zeros((k, 128), jnp.bfloat16).at[:, :3].set(digits.astype(jnp.bfloat16))
    block = normed_block(picked, gain, tail, n_t)
    gathered = gather_rows(block, n_dp).reshape(n_dp * k, width + 128)
    rows_piece = gathered[:, :width]
    got_digits = gathered[:, width : width + 3].astype(jnp.int32)
    target_piece = got_digits[:, 0] * 65536 + got_digits[:, 1] * 256 + got_digits[:, 2]
    logits = jnp.dot(rows_piece, head, preferred_element_type=jnp.float32)
    top = jnp.max(logits, axis=-1)
    expo = jnp.exp(logits - top[:, None])
    total = jnp.sum(expo, axis=-1)
    weighted = jnp.sum(expo * logits, axis=-1)
    hit = columns[None, :] == (target_piece - vocab_start)[:, None]
    chosen = jnp.sum(jnp.where(hit, logits, 0.0), axis=-1)

    parts = jnp.stack([top, total, weighted, chosen]).reshape(4, n_dp, k).transpose(1, 0, 2)
    top, total, weighted, chosen = exchange_stats(parts, n_t)
    lse = top + jnp.log(total)
    score = chosen - lse
    spread = lse - weighted / total

    logprob = jnp.sum(jnp.where(sel, score[:, None], 0.0), axis=0)
    entropy = jnp.sum(jnp.where(sel, spread[:, None], 0.0), axis=0)
    return (logprob.reshape(seq_count, slot_count), entropy.reshape(seq_count, slot_count))


def solution(mesh):
    return jax.shard_map(
        per_device,
        mesh=mesh,
        in_specs=(
            P("dp", None, "tensor"),
            P(),
            P(None, ("dp", "tensor")),
            P("dp"),
            P("dp", None),
            P("dp", None),
            P("dp", None),
        ),
        out_specs=(P("dp", None), P("dp", None)),
        check_vma=False,
    )
```

```python
import functools

import jax
import jax.numpy as jnp
from jax import lax
from jax.experimental import pallas as pl
from jax.experimental.pallas import tpu as pltpu
from jax.sharding import PartitionSpec as P

MESH = pl.DeviceIdType.MESH
LIVE = 16
RING = 4


def merge(parts):
    tops = parts[:, 0, :]
    top = jnp.max(tops, axis=0, keepdims=True)
    factor = jnp.exp(tops - top)
    total = jnp.sum(parts[:, 1, :] * factor, axis=0, keepdims=True)
    weighted = jnp.sum(parts[:, 2, :] * factor, axis=0, keepdims=True)
    chosen = jnp.sum(parts[:, 3, :], axis=0, keepdims=True)
    return jnp.concatenate([top, total, weighted, chosen], axis=0)


def stats_kernel(part_ref, out_ref, got1, sent, got2, send1, recv1, send2, recv2, local):
    n_dp = part_ref.shape[0]
    n_t = got2.shape[0]
    me = lax.axis_index("dp")
    mt = lax.axis_index("tensor")

    barrier = pltpu.get_barrier_semaphore()

    def greet_dp(i, carry):
        p = lax.rem(me + 1 + i, n_dp)
        pl.semaphore_signal(barrier, 1, device_id=(p, mt), device_id_type=MESH)
        return carry

    def greet_t(i, carry):
        q = lax.rem(mt + 1 + i, n_t)
        pl.semaphore_signal(barrier, 1, device_id=(me, q), device_id_type=MESH)
        return carry

    lax.fori_loop(0, n_dp - 1, greet_dp, 0)
    lax.fori_loop(0, n_t - 1, greet_t, 0)
    pl.semaphore_wait(barrier, n_dp - 1 + n_t - 1)

    def out1(p):
        return pltpu.make_async_remote_copy(
            src_ref=part_ref.at[p], dst_ref=got1.at[me], send_sem=send1.at[p],
            recv_sem=recv1.at[me], device_id=(p, mt), device_id_type=MESH)

    def in1(p):
        return pltpu.make_async_remote_copy(
            src_ref=part_ref.at[p], dst_ref=got1.at[p], send_sem=send1.at[p],
            recv_sem=recv1.at[p], device_id=(p, mt), device_id_type=MESH)

    def start1(i, carry):
        out1(lax.rem(me + 1 + i, n_dp)).start()
        return carry

    lax.fori_loop(0, n_dp - 1, start1, 0)
    own1 = pltpu.make_async_copy(part_ref.at[me], got1.at[me], local.at[0])
    own1.start()

    def finish1(i, carry):
        p = lax.rem(me + 1 + i, n_dp)
        in1(p).wait_recv()
        out1(p).wait_send()
        return carry

    lax.fori_loop(0, n_dp - 1, finish1, 0)
    own1.wait()

    sent[...] = merge(got1[...])

    def out2(q):
        return pltpu.make_async_remote_copy(
            src_ref=sent, dst_ref=got2.at[mt], send_sem=send2.at[q],
            recv_sem=recv2.at[mt], device_id=(me, q), device_id_type=MESH)

    def in2(q):
        return pltpu.make_async_remote_copy(
            src_ref=sent, dst_ref=got2.at[q], send_sem=send2.at[q],
            recv_sem=recv2.at[q], device_id=(me, q), device_id_type=MESH)

    def start2(i, carry):
        out2(lax.rem(mt + 1 + i, n_t)).start()
        return carry

    lax.fori_loop(0, n_t - 1, start2, 0)
    own2 = pltpu.make_async_copy(sent, got2.at[mt], local.at[1])
    own2.start()

    def finish2(i, carry):
        q = lax.rem(mt + 1 + i, n_t)
        in2(q).wait_recv()
        out2(q).wait_send()
        return carry

    lax.fori_loop(0, n_t - 1, finish2, 0)
    own2.wait()

    out_ref[...] = merge(got2[...])


def exchange_stats(parts, n_t):
    n_dp, four, k = parts.shape
    return pl.pallas_call(
        stats_kernel,
        out_shape=jax.ShapeDtypeStruct((four, k), jnp.float32),
        in_specs=[pl.BlockSpec(memory_space=pltpu.VMEM)],
        out_specs=pl.BlockSpec(memory_space=pltpu.VMEM),
        scratch_shapes=[
            pltpu.VMEM((n_dp, four, k), jnp.float32),
            pltpu.VMEM((four, k), jnp.float32),
            pltpu.VMEM((n_t, four, k), jnp.float32),
            pltpu.SemaphoreType.DMA((n_dp,)),
            pltpu.SemaphoreType.DMA((n_dp,)),
            pltpu.SemaphoreType.DMA((n_t,)),
            pltpu.SemaphoreType.DMA((n_t,)),
            pltpu.SemaphoreType.DMA((2,)),
        ],
        compiler_params=pltpu.CompilerParams(collective_id=0, has_side_effects=True),
    )(parts)


def tensor_kernel(rows_ref, out_ref, got, send, recv, local):
    n_t = got.shape[0]
    me = lax.axis_index("dp")
    mt = lax.axis_index("tensor")

    barrier = pltpu.get_barrier_semaphore()

    def greet(i, carry):
        q = lax.rem(mt + 1 + i, n_t)
        pl.semaphore_signal(barrier, 1, device_id=(me, q), device_id_type=MESH)
        return carry

    lax.fori_loop(0, n_t - 1, greet, 0)
    pl.semaphore_wait(barrier, n_t - 1)

    def outgoing(q):
        return pltpu.make_async_remote_copy(
            src_ref=rows_ref, dst_ref=got.at[mt], send_sem=send.at[q],
            recv_sem=recv.at[mt], device_id=(me, q), device_id_type=MESH)

    def incoming(q):
        return pltpu.make_async_remote_copy(
            src_ref=rows_ref, dst_ref=got.at[q], send_sem=send.at[q],
            recv_sem=recv.at[q], device_id=(me, q), device_id_type=MESH)

    def start(i, carry):
        outgoing(lax.rem(mt + 1 + i, n_t)).start()
        return carry

    lax.fori_loop(0, n_t - 1, start, 0)
    own = pltpu.make_async_copy(rows_ref, got.at[mt], local.at[0])
    own.start()

    def finish(i, carry):
        q = lax.rem(mt + 1 + i, n_t)
        incoming(q).wait_recv()
        outgoing(q).wait_send()
        return carry

    lax.fori_loop(0, n_t - 1, finish, 0)
    own.wait()
    out_ref[...] = got[...]


def gather_tensor(rows, n_t):
    k, width = rows.shape
    return pl.pallas_call(
        tensor_kernel,
        out_shape=jax.ShapeDtypeStruct((n_t, k, width), rows.dtype),
        in_specs=[pl.BlockSpec(memory_space=pltpu.VMEM)],
        out_specs=pl.BlockSpec(memory_space=pltpu.VMEM),
        scratch_shapes=[
            pltpu.VMEM((n_t, k, width), rows.dtype),
            pltpu.SemaphoreType.DMA((n_t,)),
            pltpu.SemaphoreType.DMA((n_t,)),
            pltpu.SemaphoreType.DMA((1,)),
        ],
        compiler_params=pltpu.CompilerParams(collective_id=1, has_side_effects=True),
    )(rows)


def rows_kernel(block_ref, out_ref, send, recv, local):
    n_dp = out_ref.shape[0]
    n_chip = n_dp // 2
    me = lax.axis_index("dp")
    mt = lax.axis_index("tensor")
    chip = me // 2
    core = me % 2
    x = chip % RING
    y = chip // RING
    ua = x + (y - x) * core
    ub = y + (x - y) * core
    sib = me + 1 - 2 * core

    def slot(a, b, parity):
        a = (a + 2 * RING) % RING
        b = (b + 2 * RING) % RING
        xx = a + (b - a) * core
        yy = b + (a - b) * core
        return (yy * RING + xx) * 2 + parity

    def dev(a, b):
        return (slot(a, b, core), mt)

    plus_a, minus_a = dev(ua + 1, ub), dev(ua - 1, ub)
    plus_b, minus_b = dev(ua, ub + 1), dev(ua, ub - 1)
    sib_dev = (sib, mt)

    barrier = pltpu.get_barrier_semaphore()
    for target in (plus_a, minus_a, plus_b, minus_b, sib_dev):
        pl.semaphore_signal(barrier, 1, device_id=target, device_id_type=MESH)
    pl.semaphore_wait(barrier, 5)

    sends = []

    def put(src_slot, dst_slot, target):
        src = block_ref if src_slot is None else out_ref.at[src_slot]
        copy = pltpu.make_async_remote_copy(
            src_ref=src, dst_ref=out_ref.at[dst_slot], send_sem=send.at[len(sends)],
            recv_sem=recv.at[dst_slot], device_id=target, device_id_type=MESH)
        copy.start()
        sends.append(copy)

    def arrive(dst_slot):
        pltpu.make_async_remote_copy(
            src_ref=block_ref, dst_ref=out_ref.at[dst_slot], send_sem=send.at[0],
            recv_sem=recv.at[dst_slot], device_id=sib_dev, device_id_type=MESH).wait_recv()

    own = pltpu.make_async_copy(block_ref, out_ref.at[me], local.at[0])
    own.start()
    for target in (plus_a, minus_a, plus_b, minus_b, sib_dev):
        put(None, me, target)

    left, right, far = slot(ua - 1, ub, core), slot(ua + 1, ub, core), slot(ua + 2, ub, core)
    arrive(left)
    for target in (plus_b, minus_b, sib_dev):
        put(left, left, target)
    arrive(right)
    for target in (plus_b, minus_b, sib_dev):
        put(right, right, target)
    pick = 1 - (ua + 3 + core) % 2
    fwd = pick * left + (1 - pick) * right
    fwd_dev = (pick * plus_a[0] + (1 - pick) * minus_a[0], mt)
    put(fwd, fwd, fwd_dev)
    arrive(far)
    for target in (plus_b, minus_b, sib_dev):
        put(far, far, target)

    pick_b = 1 - (ub + 3 + core) % 2
    for d in (0, -1, 1, 2):
        lo, hi = slot(ua + d, ub - 1, core), slot(ua + d, ub + 1, core)
        arrive(lo)
        put(lo, lo, sib_dev)
        arrive(hi)
        put(hi, hi, sib_dev)
        fwd = pick_b * lo + (1 - pick_b) * hi
        fwd_dev = (pick_b * plus_b[0] + (1 - pick_b) * minus_b[0], mt)
        put(fwd, fwd, fwd_dev)
    for d in (0, -1, 1, 2):
        far_b = slot(ua + d, ub + 2, core)
        arrive(far_b)
        put(far_b, far_b, sib_dev)

    for c in range(n_chip):
        arrive(c * 2 + 1 - core)
    for copy in sends:
        copy.wait_send()
    own.wait()


def gather_rows(block, n_dp):
    return pl.pallas_call(
        rows_kernel,
        out_shape=jax.ShapeDtypeStruct((n_dp,) + block.shape, block.dtype),
        in_specs=[pl.BlockSpec(memory_space=pltpu.VMEM)],
        out_specs=pl.BlockSpec(memory_space=pl.ANY),
        scratch_shapes=[
            pltpu.SemaphoreType.DMA((n_dp,)),
            pltpu.SemaphoreType.DMA((n_dp,)),
            pltpu.SemaphoreType.DMA((1,)),
        ],
        compiler_params=pltpu.CompilerParams(collective_id=2, has_side_effects=True),
    )(block)


def per_device(hidden, gain, head, lengths, offsets, targets, mask):
    seq_count, slot_count = offsets.shape
    slots = seq_count * slot_count
    maxlen = hidden.shape[1]
    n_dp = lax.axis_size("dp")
    n_t = lax.axis_size("tensor")
    k = min(LIVE, slots)

    live = mask.reshape(slots) != 0
    rank = jnp.cumsum(live.astype(jnp.int32)) - 1
    sel = live[None, :] & (rank[None, :] == jnp.arange(k, dtype=jnp.int32)[:, None])
    idx = jnp.sum(jnp.where(sel, jnp.arange(slots, dtype=jnp.int32)[None, :], 0), axis=1)
    seq_of = idx // slot_count
    position = lengths[seq_of] - 1 - offsets.reshape(slots)[idx]
    flat_hidden = hidden.reshape(seq_count * maxlen, hidden.shape[2])
    picked = jnp.take(flat_hidden, seq_of * maxlen + position, axis=0)
    flat_target = targets.reshape(slots)[idx]

    full_rows = gather_tensor(picked, n_t).transpose(1, 0, 2).reshape(k, n_t * picked.shape[1])
    values = full_rows.astype(jnp.float32)
    meansq = jnp.mean(values * values, axis=-1, keepdims=True)
    normed = (values * lax.rsqrt(meansq + 1e-06) * gain).astype(jnp.bfloat16)

    vocab_width = head.shape[1]
    vocab_start = (lax.axis_index("dp") * n_t + lax.axis_index("tensor")) * vocab_width
    columns = jnp.arange(vocab_width, dtype=jnp.int32)
    width = normed.shape[1]
    digits = jnp.stack([flat_target // 65536, (flat_target // 256) % 256, flat_target % 256], axis=1)
    tail = jnp.zeros((k, 128), jnp.bfloat16).at[:, :3].set(digits.astype(jnp.bfloat16))
    block = jnp.concatenate([normed, tail], axis=1)
    gathered = gather_rows(block, n_dp).reshape(n_dp * k, width + 128)
    rows_piece = gathered[:, :width]
    got_digits = gathered[:, width : width + 3].astype(jnp.int32)
    target_piece = got_digits[:, 0] * 65536 + got_digits[:, 1] * 256 + got_digits[:, 2]
    logits = jnp.dot(rows_piece, head, preferred_element_type=jnp.float32)
    top = jnp.max(logits, axis=-1)
    expo = jnp.exp(logits - top[:, None])
    total = jnp.sum(expo, axis=-1)
    weighted = jnp.sum(expo * logits, axis=-1)
    hit = columns[None, :] == (target_piece - vocab_start)[:, None]
    chosen = jnp.sum(jnp.where(hit, logits, 0.0), axis=-1)

    parts = jnp.stack([top, total, weighted, chosen]).reshape(4, n_dp, k).transpose(1, 0, 2)
    top, total, weighted, chosen = exchange_stats(parts, n_t)
    lse = top + jnp.log(total)
    score = chosen - lse
    spread = lse - weighted / total

    logprob = jnp.sum(jnp.where(sel, score[:, None], 0.0), axis=0)
    entropy = jnp.sum(jnp.where(sel, spread[:, None], 0.0), axis=0)
    return (logprob.reshape(seq_count, slot_count), entropy.reshape(seq_count, slot_count))


def solution(mesh):
    return jax.shard_map(
        per_device,
        mesh=mesh,
        in_specs=(
            P("dp", None, "tensor"),
            P(),
            P(None, ("dp", "tensor")),
            P("dp"),
            P("dp", None),
            P("dp", None),
            P("dp", None),
        ),
        out_specs=(P("dp", None), P("dp", None)),
        check_vma=False,
    )
```

```python
import functools

import jax
import jax.numpy as jnp
from jax import lax
from jax.experimental import pallas as pl
from jax.experimental.pallas import tpu as pltpu
from jax.sharding import PartitionSpec as P

MESH = pl.DeviceIdType.MESH
LIVE = 16
RING = 4


def merge(parts):
    tops = parts[:, 0, :]
    top = jnp.max(tops, axis=0, keepdims=True)
    factor = jnp.exp(tops - top)
    total = jnp.sum(parts[:, 1, :] * factor, axis=0, keepdims=True)
    weighted = jnp.sum(parts[:, 2, :] * factor, axis=0, keepdims=True)
    chosen = jnp.sum(parts[:, 3, :], axis=0, keepdims=True)
    return jnp.concatenate([top, total, weighted, chosen], axis=0)


def stats_kernel(part_ref, out_ref, got1, sent, got2, send1, recv1, send2, recv2, local):
    n_dp = part_ref.shape[0]
    n_t = got2.shape[0]
    me = lax.axis_index("dp")
    mt = lax.axis_index("tensor")

    barrier = pltpu.get_barrier_semaphore()

    def greet_dp(i, carry):
        p = lax.rem(me + 1 + i, n_dp)
        pl.semaphore_signal(barrier, 1, device_id=(p, mt), device_id_type=MESH)
        return carry

    def greet_t(i, carry):
        q = lax.rem(mt + 1 + i, n_t)
        pl.semaphore_signal(barrier, 1, device_id=(me, q), device_id_type=MESH)
        return carry

    lax.fori_loop(0, n_dp - 1, greet_dp, 0)
    lax.fori_loop(0, n_t - 1, greet_t, 0)
    pl.semaphore_wait(barrier, n_dp - 1 + n_t - 1)

    def out1(p):
        return pltpu.make_async_remote_copy(
            src_ref=part_ref.at[p], dst_ref=got1.at[me], send_sem=send1.at[p],
            recv_sem=recv1.at[me], device_id=(p, mt), device_id_type=MESH)

    def in1(p):
        return pltpu.make_async_remote_copy(
            src_ref=part_ref.at[p], dst_ref=got1.at[p], send_sem=send1.at[p],
            recv_sem=recv1.at[p], device_id=(p, mt), device_id_type=MESH)

    def start1(i, carry):
        out1(lax.rem(me + 1 + i, n_dp)).start()
        return carry

    lax.fori_loop(0, n_dp - 1, start1, 0)
    own1 = pltpu.make_async_copy(part_ref.at[me], got1.at[me], local.at[0])
    own1.start()

    def finish1(i, carry):
        p = lax.rem(me + 1 + i, n_dp)
        in1(p).wait_recv()
        out1(p).wait_send()
        return carry

    lax.fori_loop(0, n_dp - 1, finish1, 0)
    own1.wait()

    sent[...] = merge(got1[...])

    def out2(q):
        return pltpu.make_async_remote_copy(
            src_ref=sent, dst_ref=got2.at[mt], send_sem=send2.at[q],
            recv_sem=recv2.at[mt], device_id=(me, q), device_id_type=MESH)

    def in2(q):
        return pltpu.make_async_remote_copy(
            src_ref=sent, dst_ref=got2.at[q], send_sem=send2.at[q],
            recv_sem=recv2.at[q], device_id=(me, q), device_id_type=MESH)

    def start2(i, carry):
        out2(lax.rem(mt + 1 + i, n_t)).start()
        return carry

    lax.fori_loop(0, n_t - 1, start2, 0)
    own2 = pltpu.make_async_copy(sent, got2.at[mt], local.at[1])
    own2.start()

    def finish2(i, carry):
        q = lax.rem(mt + 1 + i, n_t)
        in2(q).wait_recv()
        out2(q).wait_send()
        return carry

    lax.fori_loop(0, n_t - 1, finish2, 0)
    own2.wait()

    out_ref[...] = merge(got2[...])


def exchange_stats(parts, n_t):
    n_dp, four, k = parts.shape
    return pl.pallas_call(
        stats_kernel,
        out_shape=jax.ShapeDtypeStruct((four, k), jnp.float32),
        in_specs=[pl.BlockSpec(memory_space=pltpu.VMEM)],
        out_specs=pl.BlockSpec(memory_space=pltpu.VMEM),
        scratch_shapes=[
            pltpu.VMEM((n_dp, four, k), jnp.float32),
            pltpu.VMEM((four, k), jnp.float32),
            pltpu.VMEM((n_t, four, k), jnp.float32),
            pltpu.SemaphoreType.DMA((n_dp,)),
            pltpu.SemaphoreType.DMA((n_dp,)),
            pltpu.SemaphoreType.DMA((n_t,)),
            pltpu.SemaphoreType.DMA((n_t,)),
            pltpu.SemaphoreType.DMA((2,)),
        ],
        compiler_params=pltpu.CompilerParams(collective_id=0, has_side_effects=True),
    )(parts)


def rows_kernel(rows_ref, gain_ref, target_ref, out_ref, got, block_ref, send_t, recv_t, send, recv, local):
    n_dp = out_ref.shape[0]
    n_chip = n_dp // 2
    me = lax.axis_index("dp")
    mt = lax.axis_index("tensor")
    chip = me // 2
    core = me % 2
    x = chip % RING
    y = chip // RING
    ua = x + (y - x) * core
    ub = y + (x - y) * core
    sib = me + 1 - 2 * core

    def slot(a, b, parity):
        a = (a + 2 * RING) % RING
        b = (b + 2 * RING) % RING
        xx = a + (b - a) * core
        yy = b + (a - b) * core
        return (yy * RING + xx) * 2 + parity

    def dev(a, b):
        return (slot(a, b, core), mt)

    plus_a, minus_a = dev(ua + 1, ub), dev(ua - 1, ub)
    plus_b, minus_b = dev(ua, ub + 1), dev(ua, ub - 1)
    sib_dev = (sib, mt)

    n_t = got.shape[0]
    barrier = pltpu.get_barrier_semaphore()
    for target in (plus_a, minus_a, plus_b, minus_b, sib_dev):
        pl.semaphore_signal(barrier, 1, device_id=target, device_id_type=MESH)

    def greet(i, carry):
        q = lax.rem(mt + 1 + i, n_t)
        pl.semaphore_signal(barrier, 1, device_id=(me, q), device_id_type=MESH)
        return carry

    lax.fori_loop(0, n_t - 1, greet, 0)
    pl.semaphore_wait(barrier, 5 + n_t - 1)

    def t_out(q):
        return pltpu.make_async_remote_copy(
            src_ref=rows_ref, dst_ref=got.at[mt], send_sem=send_t.at[q],
            recv_sem=recv_t.at[mt], device_id=(me, q), device_id_type=MESH)

    def t_in(q):
        return pltpu.make_async_remote_copy(
            src_ref=rows_ref, dst_ref=got.at[q], send_sem=send_t.at[q],
            recv_sem=recv_t.at[q], device_id=(me, q), device_id_type=MESH)

    def t_start(i, carry):
        t_out(lax.rem(mt + 1 + i, n_t)).start()
        return carry

    lax.fori_loop(0, n_t - 1, t_start, 0)
    own_t = pltpu.make_async_copy(rows_ref, got.at[mt], local.at[1])
    own_t.start()

    def t_finish(i, carry):
        q = lax.rem(mt + 1 + i, n_t)
        t_in(q).wait_recv()
        t_out(q).wait_send()
        return carry

    lax.fori_loop(0, n_t - 1, t_finish, 0)
    own_t.wait()

    width = got.shape[2]
    values = got[...].astype(jnp.float32)
    sumsq = jnp.sum(jnp.sum(values * values, axis=0), axis=-1, keepdims=True)
    scale = lax.rsqrt(sumsq / (n_t * width) + 1e-06)
    for t in range(n_t):
        piece = values[t] * scale * gain_ref[:, pl.ds(t * width, width)]
        block_ref[:, pl.ds(t * width, width)] = piece.astype(block_ref.dtype)
    tgt = target_ref[...]
    lane = lax.broadcasted_iota(jnp.int32, (tgt.shape[0], 128), 1)
    tail = jnp.where(lane == 0, tgt // 65536, jnp.where(lane == 1, (tgt // 256) % 256,
                                                          jnp.where(lane == 2, tgt % 256, 0)))
    block_ref[:, pl.ds(n_t * width, 128)] = tail.astype(jnp.float32).astype(block_ref.dtype)

    sends = []

    def put(src_slot, dst_slot, target):
        src = block_ref if src_slot is None else out_ref.at[src_slot]
        copy = pltpu.make_async_remote_copy(
            src_ref=src, dst_ref=out_ref.at[dst_slot], send_sem=send.at[len(sends)],
            recv_sem=recv.at[dst_slot], device_id=target, device_id_type=MESH)
        copy.start()
        sends.append(copy)

    def arrive(dst_slot):
        pltpu.make_async_remote_copy(
            src_ref=block_ref, dst_ref=out_ref.at[dst_slot], send_sem=send.at[0],
            recv_sem=recv.at[dst_slot], device_id=sib_dev, device_id_type=MESH).wait_recv()

    own = pltpu.make_async_copy(block_ref, out_ref.at[me], local.at[0])
    own.start()
    for target in (plus_a, minus_a, plus_b, minus_b, sib_dev):
        put(None, me, target)

    left, right, far = slot(ua - 1, ub, core), slot(ua + 1, ub, core), slot(ua + 2, ub, core)
    arrive(left)
    for target in (plus_b, minus_b, sib_dev):
        put(left, left, target)
    arrive(right)
    for target in (plus_b, minus_b, sib_dev):
        put(right, right, target)
    pick = 1 - (ua + 3 + core) % 2
    fwd = pick * left + (1 - pick) * right
    fwd_dev = (pick * plus_a[0] + (1 - pick) * minus_a[0], mt)
    put(fwd, fwd, fwd_dev)
    arrive(far)
    for target in (plus_b, minus_b, sib_dev):
        put(far, far, target)

    pick_b = 1 - (ub + 3 + core) % 2
    for d in (0, -1, 1, 2):
        lo, hi = slot(ua + d, ub - 1, core), slot(ua + d, ub + 1, core)
        arrive(lo)
        put(lo, lo, sib_dev)
        arrive(hi)
        put(hi, hi, sib_dev)
        fwd = pick_b * lo + (1 - pick_b) * hi
        fwd_dev = (pick_b * plus_b[0] + (1 - pick_b) * minus_b[0], mt)
        put(fwd, fwd, fwd_dev)
    for d in (0, -1, 1, 2):
        far_b = slot(ua + d, ub + 2, core)
        arrive(far_b)
        put(far_b, far_b, sib_dev)

    for c in range(n_chip):
        arrive(c * 2 + 1 - core)
    for copy in sends:
        copy.wait_send()
    own.wait()


def gather_rows(rows, gain, target, n_dp, n_t):
    k, width = rows.shape
    shape = (k, n_t * width + 128)
    return pl.pallas_call(
        rows_kernel,
        out_shape=jax.ShapeDtypeStruct((n_dp,) + shape, rows.dtype),
        in_specs=[pl.BlockSpec(memory_space=pltpu.VMEM)] * 3,
        out_specs=pl.BlockSpec(memory_space=pl.ANY),
        scratch_shapes=[
            pltpu.VMEM((n_t, k, width), rows.dtype),
            pltpu.VMEM(shape, rows.dtype),
            pltpu.SemaphoreType.DMA((n_t,)),
            pltpu.SemaphoreType.DMA((n_t,)),
            pltpu.SemaphoreType.DMA((n_dp,)),
            pltpu.SemaphoreType.DMA((n_dp,)),
            pltpu.SemaphoreType.DMA((2,)),
        ],
        compiler_params=pltpu.CompilerParams(collective_id=2, has_side_effects=True),
    )(rows, gain.reshape(1, n_t * width), target.reshape(k, 1))


def per_device(hidden, gain, head, lengths, offsets, targets, mask):
    seq_count, slot_count = offsets.shape
    slots = seq_count * slot_count
    maxlen = hidden.shape[1]
    n_dp = lax.axis_size("dp")
    n_t = lax.axis_size("tensor")
    k = min(LIVE, slots)

    live = mask.reshape(slots) != 0
    rank = jnp.cumsum(live.astype(jnp.int32)) - 1
    sel = live[None, :] & (rank[None, :] == jnp.arange(k, dtype=jnp.int32)[:, None])
    idx = jnp.sum(jnp.where(sel, jnp.arange(slots, dtype=jnp.int32)[None, :], 0), axis=1)
    seq_of = idx // slot_count
    position = lengths[seq_of] - 1 - offsets.reshape(slots)[idx]
    flat_hidden = hidden.reshape(seq_count * maxlen, hidden.shape[2])
    picked = jnp.take(flat_hidden, seq_of * maxlen + position, axis=0)
    flat_target = targets.reshape(slots)[idx]

    vocab_width = head.shape[1]
    vocab_start = (lax.axis_index("dp") * n_t + lax.axis_index("tensor")) * vocab_width
    columns = jnp.arange(vocab_width, dtype=jnp.int32)
    width = n_t * picked.shape[1]
    gathered = gather_rows(picked, gain, flat_target, n_dp, n_t).reshape(n_dp * k, width + 128)
    rows_piece = gathered[:, :width]
    got_digits = gathered[:, width : width + 3].astype(jnp.int32)
    target_piece = got_digits[:, 0] * 65536 + got_digits[:, 1] * 256 + got_digits[:, 2]
    logits = jnp.dot(rows_piece, head, preferred_element_type=jnp.float32)
    top = jnp.max(logits, axis=-1)
    expo = jnp.exp(logits - top[:, None])
    total = jnp.sum(expo, axis=-1)
    weighted = jnp.sum(expo * logits, axis=-1)
    hit = columns[None, :] == (target_piece - vocab_start)[:, None]
    chosen = jnp.sum(jnp.where(hit, logits, 0.0), axis=-1)

    parts = jnp.stack([top, total, weighted, chosen]).reshape(4, n_dp, k).transpose(1, 0, 2)
    top, total, weighted, chosen = exchange_stats(parts, n_t)
    lse = top + jnp.log(total)
    score = chosen - lse
    spread = lse - weighted / total

    logprob = jnp.sum(jnp.where(sel, score[:, None], 0.0), axis=0)
    entropy = jnp.sum(jnp.where(sel, spread[:, None], 0.0), axis=0)
    return (logprob.reshape(seq_count, slot_count), entropy.reshape(seq_count, slot_count))


def solution(mesh):
    return jax.shard_map(
        per_device,
        mesh=mesh,
        in_specs=(
            P("dp", None, "tensor"),
            P(),
            P(None, ("dp", "tensor")),
            P("dp"),
            P("dp", None),
            P("dp", None),
            P("dp", None),
        ),
        out_specs=(P("dp", None), P("dp", None)),
        check_vma=False,
    )
```

```python
import functools

import jax
import jax.numpy as jnp
from jax import lax
from jax.experimental import pallas as pl
from jax.experimental.pallas import tpu as pltpu
from jax.sharding import PartitionSpec as P

MESH = pl.DeviceIdType.MESH
LIVE = 16
RING = 4


def merge(parts):
    tops = parts[:, 0, :]
    top = jnp.max(tops, axis=0, keepdims=True)
    factor = jnp.exp(tops - top)
    total = jnp.sum(parts[:, 1, :] * factor, axis=0, keepdims=True)
    weighted = jnp.sum(parts[:, 2, :] * factor, axis=0, keepdims=True)
    chosen = jnp.sum(parts[:, 3, :], axis=0, keepdims=True)
    return jnp.concatenate([top, total, weighted, chosen], axis=0)


def stats_kernel(part_ref, out_ref, got1, sent, got2, send1, recv1, send2, recv2, local):
    n_dp = part_ref.shape[0]
    n_t = got2.shape[0]
    me = lax.axis_index("dp")
    mt = lax.axis_index("tensor")

    barrier = pltpu.get_barrier_semaphore()

    def greet_dp(i, carry):
        p = lax.rem(me + 1 + i, n_dp)
        pl.semaphore_signal(barrier, 1, device_id=(p, mt), device_id_type=MESH)
        return carry

    def greet_t(i, carry):
        q = lax.rem(mt + 1 + i, n_t)
        pl.semaphore_signal(barrier, 1, device_id=(me, q), device_id_type=MESH)
        return carry

    lax.fori_loop(0, n_dp - 1, greet_dp, 0)
    lax.fori_loop(0, n_t - 1, greet_t, 0)
    pl.semaphore_wait(barrier, n_dp - 1 + n_t - 1)

    def out1(p):
        return pltpu.make_async_remote_copy(
            src_ref=part_ref.at[p], dst_ref=got1.at[me], send_sem=send1.at[p],
            recv_sem=recv1.at[me], device_id=(p, mt), device_id_type=MESH)

    def in1(p):
        return pltpu.make_async_remote_copy(
            src_ref=part_ref.at[p], dst_ref=got1.at[p], send_sem=send1.at[p],
            recv_sem=recv1.at[p], device_id=(p, mt), device_id_type=MESH)

    def start1(i, carry):
        out1(lax.rem(me + 1 + i, n_dp)).start()
        return carry

    lax.fori_loop(0, n_dp - 1, start1, 0)
    own1 = pltpu.make_async_copy(part_ref.at[me], got1.at[me], local.at[0])
    own1.start()

    def finish1(i, carry):
        p = lax.rem(me + 1 + i, n_dp)
        in1(p).wait_recv()
        out1(p).wait_send()
        return carry

    lax.fori_loop(0, n_dp - 1, finish1, 0)
    own1.wait()

    sent[...] = merge(got1[...])

    def out2(q):
        return pltpu.make_async_remote_copy(
            src_ref=sent, dst_ref=got2.at[mt], send_sem=send2.at[q],
            recv_sem=recv2.at[mt], device_id=(me, q), device_id_type=MESH)

    def in2(q):
        return pltpu.make_async_remote_copy(
            src_ref=sent, dst_ref=got2.at[q], send_sem=send2.at[q],
            recv_sem=recv2.at[q], device_id=(me, q), device_id_type=MESH)

    def start2(i, carry):
        out2(lax.rem(mt + 1 + i, n_t)).start()
        return carry

    lax.fori_loop(0, n_t - 1, start2, 0)
    own2 = pltpu.make_async_copy(sent, got2.at[mt], local.at[1])
    own2.start()

    def finish2(i, carry):
        q = lax.rem(mt + 1 + i, n_t)
        in2(q).wait_recv()
        out2(q).wait_send()
        return carry

    lax.fori_loop(0, n_t - 1, finish2, 0)
    own2.wait()

    out_ref[...] = merge(got2[...])


def exchange_stats(parts, n_t):
    n_dp, four, k = parts.shape
    return pl.pallas_call(
        stats_kernel,
        out_shape=jax.ShapeDtypeStruct((four, k), jnp.float32),
        in_specs=[pl.BlockSpec(memory_space=pltpu.VMEM)],
        out_specs=pl.BlockSpec(memory_space=pltpu.VMEM),
        scratch_shapes=[
            pltpu.VMEM((n_dp, four, k), jnp.float32),
            pltpu.VMEM((four, k), jnp.float32),
            pltpu.VMEM((n_t, four, k), jnp.float32),
            pltpu.SemaphoreType.DMA((n_dp,)),
            pltpu.SemaphoreType.DMA((n_dp,)),
            pltpu.SemaphoreType.DMA((n_t,)),
            pltpu.SemaphoreType.DMA((n_t,)),
            pltpu.SemaphoreType.DMA((2,)),
        ],
        compiler_params=pltpu.CompilerParams(collective_id=0, has_side_effects=True, vmem_limit_bytes=16 * 1024 * 1024),
    )(parts)


def rows_kernel(rows_ref, gain_ref, target_ref, out_ref, got, block_ref, send_t, recv_t, send, recv, local):
    n_dp = out_ref.shape[0]
    n_chip = n_dp // 2
    me = lax.axis_index("dp")
    mt = lax.axis_index("tensor")
    chip = me // 2
    core = me % 2
    x = chip % RING
    y = chip // RING
    ua = x + (y - x) * core
    ub = y + (x - y) * core
    sib = me + 1 - 2 * core

    def slot(a, b, parity):
        a = (a + 2 * RING) % RING
        b = (b + 2 * RING) % RING
        xx = a + (b - a) * core
        yy = b + (a - b) * core
        return (yy * RING + xx) * 2 + parity

    def dev(a, b):
        return (slot(a, b, core), mt)

    plus_a, minus_a = dev(ua + 1, ub), dev(ua - 1, ub)
    plus_b, minus_b = dev(ua, ub + 1), dev(ua, ub - 1)
    sib_dev = (sib, mt)

    n_t = got.shape[0]
    barrier = pltpu.get_barrier_semaphore()
    for target in (plus_a, minus_a, plus_b, minus_b, sib_dev):
        pl.semaphore_signal(barrier, 1, device_id=target, device_id_type=MESH)

    def greet(i, carry):
        q = lax.rem(mt + 1 + i, n_t)
        pl.semaphore_signal(barrier, 1, device_id=(me, q), device_id_type=MESH)
        return carry

    lax.fori_loop(0, n_t - 1, greet, 0)
    pl.semaphore_wait(barrier, 5 + n_t - 1)

    def t_out(q):
        return pltpu.make_async_remote_copy(
            src_ref=rows_ref, dst_ref=got.at[mt], send_sem=send_t.at[q],
            recv_sem=recv_t.at[mt], device_id=(me, q), device_id_type=MESH)

    def t_in(q):
        return pltpu.make_async_remote_copy(
            src_ref=rows_ref, dst_ref=got.at[q], send_sem=send_t.at[q],
            recv_sem=recv_t.at[q], device_id=(me, q), device_id_type=MESH)

    def t_start(i, carry):
        t_out(lax.rem(mt + 1 + i, n_t)).start()
        return carry

    lax.fori_loop(0, n_t - 1, t_start, 0)
    own_t = pltpu.make_async_copy(rows_ref, got.at[mt], local.at[1])
    own_t.start()

    def t_finish(i, carry):
        q = lax.rem(mt + 1 + i, n_t)
        t_in(q).wait_recv()
        t_out(q).wait_send()
        return carry

    lax.fori_loop(0, n_t - 1, t_finish, 0)
    own_t.wait()

    width = got.shape[2]
    values = got[...].astype(jnp.float32)
    sumsq = jnp.sum(jnp.sum(values * values, axis=0), axis=-1, keepdims=True)
    scale = lax.rsqrt(sumsq / (n_t * width) + 1e-06)
    for t in range(n_t):
        piece = values[t] * scale * gain_ref[:, pl.ds(t * width, width)]
        block_ref[:, pl.ds(t * width, width)] = piece.astype(block_ref.dtype)
    tgt = target_ref[...]
    lane = lax.broadcasted_iota(jnp.int32, (tgt.shape[0], 128), 1)
    tail = jnp.where(lane == 0, tgt // 65536, jnp.where(lane == 1, (tgt // 256) % 256,
                                                          jnp.where(lane == 2, tgt % 256, 0)))
    block_ref[:, pl.ds(n_t * width, 128)] = tail.astype(jnp.float32).astype(block_ref.dtype)

    sends = []

    def put(src_slot, dst_slot, target):
        src = block_ref if src_slot is None else out_ref.at[src_slot]
        copy = pltpu.make_async_remote_copy(
            src_ref=src, dst_ref=out_ref.at[dst_slot], send_sem=send.at[len(sends)],
            recv_sem=recv.at[dst_slot], device_id=target, device_id_type=MESH)
        copy.start()
        sends.append(copy)

    def arrive(dst_slot):
        pltpu.make_async_remote_copy(
            src_ref=block_ref, dst_ref=out_ref.at[dst_slot], send_sem=send.at[0],
            recv_sem=recv.at[dst_slot], device_id=sib_dev, device_id_type=MESH).wait_recv()

    own = pltpu.make_async_copy(block_ref, out_ref.at[me], local.at[0])
    own.start()
    for target in (plus_a, minus_a, plus_b, minus_b, sib_dev):
        put(None, me, target)

    left, right, far = slot(ua - 1, ub, core), slot(ua + 1, ub, core), slot(ua + 2, ub, core)
    arrive(left)
    for target in (plus_b, minus_b, sib_dev):
        put(left, left, target)
    arrive(right)
    for target in (plus_b, minus_b, sib_dev):
        put(right, right, target)
    pick = 1 - (ua + 3 + core) % 2
    fwd = pick * left + (1 - pick) * right
    fwd_dev = (pick * plus_a[0] + (1 - pick) * minus_a[0], mt)
    put(fwd, fwd, fwd_dev)
    arrive(far)
    for target in (plus_b, minus_b, sib_dev):
        put(far, far, target)

    pick_b = 1 - (ub + 3 + core) % 2
    for d in (0, -1, 1, 2):
        lo, hi = slot(ua + d, ub - 1, core), slot(ua + d, ub + 1, core)
        arrive(lo)
        put(lo, lo, sib_dev)
        arrive(hi)
        put(hi, hi, sib_dev)
        fwd = pick_b * lo + (1 - pick_b) * hi
        fwd_dev = (pick_b * plus_b[0] + (1 - pick_b) * minus_b[0], mt)
        put(fwd, fwd, fwd_dev)
    for d in (0, -1, 1, 2):
        far_b = slot(ua + d, ub + 2, core)
        arrive(far_b)
        put(far_b, far_b, sib_dev)

    for c in range(n_chip):
        arrive(c * 2 + 1 - core)
    for copy in sends:
        copy.wait_send()
    own.wait()


def gather_rows(rows, gain, target, n_dp, n_t):
    k, width = rows.shape
    shape = (k, n_t * width + 128)
    return pl.pallas_call(
        rows_kernel,
        out_shape=jax.ShapeDtypeStruct((n_dp,) + shape, rows.dtype),
        in_specs=[pl.BlockSpec(memory_space=pltpu.VMEM)] * 3,
        out_specs=pl.BlockSpec(memory_space=pl.ANY),
        scratch_shapes=[
            pltpu.VMEM((n_t, k, width), rows.dtype),
            pltpu.VMEM(shape, rows.dtype),
            pltpu.SemaphoreType.DMA((n_t,)),
            pltpu.SemaphoreType.DMA((n_t,)),
            pltpu.SemaphoreType.DMA((n_dp,)),
            pltpu.SemaphoreType.DMA((n_dp,)),
            pltpu.SemaphoreType.DMA((2,)),
        ],
        compiler_params=pltpu.CompilerParams(collective_id=2, has_side_effects=True, vmem_limit_bytes=16 * 1024 * 1024),
    )(rows, gain.reshape(1, n_t * width), target.reshape(k, 1))


def per_device(hidden, gain, head, lengths, offsets, targets, mask):
    seq_count, slot_count = offsets.shape
    slots = seq_count * slot_count
    maxlen = hidden.shape[1]
    n_dp = lax.axis_size("dp")
    n_t = lax.axis_size("tensor")
    k = min(LIVE, slots)

    live = mask.reshape(slots) != 0
    rank = jnp.cumsum(live.astype(jnp.int32)) - 1
    sel = live[None, :] & (rank[None, :] == jnp.arange(k, dtype=jnp.int32)[:, None])
    idx = jnp.sum(jnp.where(sel, jnp.arange(slots, dtype=jnp.int32)[None, :], 0), axis=1)
    seq_of = idx // slot_count
    position = lengths[seq_of] - 1 - offsets.reshape(slots)[idx]
    flat_hidden = hidden.reshape(seq_count * maxlen, hidden.shape[2])
    picked = jnp.take(flat_hidden, seq_of * maxlen + position, axis=0)
    flat_target = targets.reshape(slots)[idx]

    vocab_width = head.shape[1]
    vocab_start = (lax.axis_index("dp") * n_t + lax.axis_index("tensor")) * vocab_width
    columns = jnp.arange(vocab_width, dtype=jnp.int32)
    width = n_t * picked.shape[1]
    gathered = gather_rows(picked, gain, flat_target, n_dp, n_t).reshape(n_dp * k, width + 128)
    rows_piece = gathered[:, :width]
    got_digits = gathered[:, width : width + 3].astype(jnp.int32)
    target_piece = got_digits[:, 0] * 65536 + got_digits[:, 1] * 256 + got_digits[:, 2]
    logits = jnp.dot(rows_piece, head, preferred_element_type=jnp.float32)
    top = jnp.max(logits, axis=-1)
    expo = jnp.exp(logits - top[:, None])
    total = jnp.sum(expo, axis=-1)
    weighted = jnp.sum(expo * logits, axis=-1)
    hit = columns[None, :] == (target_piece - vocab_start)[:, None]
    chosen = jnp.sum(jnp.where(hit, logits, 0.0), axis=-1)

    parts = jnp.stack([top, total, weighted, chosen]).reshape(4, n_dp, k).transpose(1, 0, 2)
    top, total, weighted, chosen = exchange_stats(parts, n_t)
    lse = top + jnp.log(total)
    score = chosen - lse
    spread = lse - weighted / total

    logprob = jnp.sum(jnp.where(sel, score[:, None], 0.0), axis=0)
    entropy = jnp.sum(jnp.where(sel, spread[:, None], 0.0), axis=0)
    return (logprob.reshape(seq_count, slot_count), entropy.reshape(seq_count, slot_count))


def solution(mesh):
    return jax.shard_map(
        per_device,
        mesh=mesh,
        in_specs=(
            P("dp", None, "tensor"),
            P(),
            P(None, ("dp", "tensor")),
            P("dp"),
            P("dp", None),
            P("dp", None),
            P("dp", None),
        ),
        out_specs=(P("dp", None), P("dp", None)),
        check_vma=False,
    )
```

```python
import functools

import jax
import jax.numpy as jnp
from jax import lax
from jax.experimental import pallas as pl
from jax.experimental.pallas import tpu as pltpu
from jax.sharding import PartitionSpec as P

MESH = pl.DeviceIdType.MESH
LIVE = 16
RING = 4


def merge(parts):
    tops = parts[:, 0, :]
    top = jnp.max(tops, axis=0, keepdims=True)
    factor = jnp.exp(tops - top)
    total = jnp.sum(parts[:, 1, :] * factor, axis=0, keepdims=True)
    weighted = jnp.sum(parts[:, 2, :] * factor, axis=0, keepdims=True)
    chosen = jnp.sum(parts[:, 3, :], axis=0, keepdims=True)
    return jnp.concatenate([top, total, weighted, chosen], axis=0)


def stats_kernel(part_ref, out_ref, got1, sent, got2, send1, recv1, send2, recv2, local):
    n_dp = part_ref.shape[0]
    n_t = got2.shape[0]
    me = lax.axis_index("dp")
    mt = lax.axis_index("tensor")

    barrier = pltpu.get_barrier_semaphore()

    def greet_dp(i, carry):
        p = lax.rem(me + 1 + i, n_dp)
        pl.semaphore_signal(barrier, 1, device_id=(p, mt), device_id_type=MESH)
        return carry

    def greet_t(i, carry):
        q = lax.rem(mt + 1 + i, n_t)
        pl.semaphore_signal(barrier, 1, device_id=(me, q), device_id_type=MESH)
        return carry

    lax.fori_loop(0, n_dp - 1, greet_dp, 0)
    lax.fori_loop(0, n_t - 1, greet_t, 0)
    pl.semaphore_wait(barrier, n_dp - 1 + n_t - 1)

    def out1(p):
        return pltpu.make_async_remote_copy(
            src_ref=part_ref.at[p], dst_ref=got1.at[me], send_sem=send1.at[p],
            recv_sem=recv1.at[me], device_id=(p, mt), device_id_type=MESH)

    def in1(p):
        return pltpu.make_async_remote_copy(
            src_ref=part_ref.at[p], dst_ref=got1.at[p], send_sem=send1.at[p],
            recv_sem=recv1.at[p], device_id=(p, mt), device_id_type=MESH)

    def start1(i, carry):
        out1(lax.rem(me + 1 + i, n_dp)).start()
        return carry

    lax.fori_loop(0, n_dp - 1, start1, 0)
    own1 = pltpu.make_async_copy(part_ref.at[me], got1.at[me], local.at[0])
    own1.start()

    def finish1(i, carry):
        p = lax.rem(me + 1 + i, n_dp)
        in1(p).wait_recv()
        out1(p).wait_send()
        return carry

    lax.fori_loop(0, n_dp - 1, finish1, 0)
    own1.wait()

    sent[...] = merge(got1[...])

    def out2(q):
        return pltpu.make_async_remote_copy(
            src_ref=sent, dst_ref=got2.at[mt], send_sem=send2.at[q],
            recv_sem=recv2.at[mt], device_id=(me, q), device_id_type=MESH)

    def in2(q):
        return pltpu.make_async_remote_copy(
            src_ref=sent, dst_ref=got2.at[q], send_sem=send2.at[q],
            recv_sem=recv2.at[q], device_id=(me, q), device_id_type=MESH)

    def start2(i, carry):
        out2(lax.rem(mt + 1 + i, n_t)).start()
        return carry

    lax.fori_loop(0, n_t - 1, start2, 0)
    own2 = pltpu.make_async_copy(sent, got2.at[mt], local.at[1])
    own2.start()

    def finish2(i, carry):
        q = lax.rem(mt + 1 + i, n_t)
        in2(q).wait_recv()
        out2(q).wait_send()
        return carry

    lax.fori_loop(0, n_t - 1, finish2, 0)
    own2.wait()

    out_ref[...] = merge(got2[...])


def exchange_stats(parts, n_t):
    n_dp, four, k = parts.shape
    return pl.pallas_call(
        stats_kernel,
        out_shape=jax.ShapeDtypeStruct((four, k), jnp.float32),
        in_specs=[pl.BlockSpec(memory_space=pltpu.VMEM)],
        out_specs=pl.BlockSpec(memory_space=pltpu.VMEM),
        scratch_shapes=[
            pltpu.VMEM((n_dp, four, k), jnp.float32),
            pltpu.VMEM((four, k), jnp.float32),
            pltpu.VMEM((n_t, four, k), jnp.float32),
            pltpu.SemaphoreType.DMA((n_dp,)),
            pltpu.SemaphoreType.DMA((n_dp,)),
            pltpu.SemaphoreType.DMA((n_t,)),
            pltpu.SemaphoreType.DMA((n_t,)),
            pltpu.SemaphoreType.DMA((2,)),
        ],
        compiler_params=pltpu.CompilerParams(collective_id=0, has_side_effects=True, vmem_limit_bytes=16 * 1024 * 1024),
    )(parts)


def rows_kernel(rows_ref, gain_ref, target_ref, out_ref, got, block_ref, send_t, recv_t, send, recv, local):
    n_dp = out_ref.shape[0]
    n_chip = n_dp // 2
    me = lax.axis_index("dp")
    mt = lax.axis_index("tensor")
    chip = me // 2
    core = me % 2
    x = chip % RING
    y = chip // RING
    ua = x + (y - x) * core
    ub = y + (x - y) * core
    sib = me + 1 - 2 * core

    def slot(a, b, parity):
        a = (a + 2 * RING) % RING
        b = (b + 2 * RING) % RING
        xx = a + (b - a) * core
        yy = b + (a - b) * core
        return (yy * RING + xx) * 2 + parity

    def dev(a, b):
        return (slot(a, b, core), mt)

    plus_a, minus_a = dev(ua + 1, ub), dev(ua - 1, ub)
    plus_b, minus_b = dev(ua, ub + 1), dev(ua, ub - 1)
    sib_dev = (sib, mt)

    n_t = got.shape[0]
    barrier = pltpu.get_barrier_semaphore()
    for target in (plus_a, minus_a, plus_b, minus_b, sib_dev):
        pl.semaphore_signal(barrier, 1, device_id=target, device_id_type=MESH)

    def greet(i, carry):
        q = lax.rem(mt + 1 + i, n_t)
        pl.semaphore_signal(barrier, 1, device_id=(me, q), device_id_type=MESH)
        return carry

    lax.fori_loop(0, n_t - 1, greet, 0)
    pl.semaphore_wait(barrier, 5 + n_t - 1)

    def t_out(q):
        return pltpu.make_async_remote_copy(
            src_ref=rows_ref, dst_ref=got.at[mt], send_sem=send_t.at[q],
            recv_sem=recv_t.at[mt], device_id=(me, q), device_id_type=MESH)

    def t_in(q):
        return pltpu.make_async_remote_copy(
            src_ref=rows_ref, dst_ref=got.at[q], send_sem=send_t.at[q],
            recv_sem=recv_t.at[q], device_id=(me, q), device_id_type=MESH)

    def t_start(i, carry):
        t_out(lax.rem(mt + 1 + i, n_t)).start()
        return carry

    lax.fori_loop(0, n_t - 1, t_start, 0)
    own_t = pltpu.make_async_copy(rows_ref, got.at[mt], local.at[1])
    own_t.start()

    def t_finish(i, carry):
        q = lax.rem(mt + 1 + i, n_t)
        t_in(q).wait_recv()
        t_out(q).wait_send()
        return carry

    lax.fori_loop(0, n_t - 1, t_finish, 0)
    own_t.wait()

    width = got.shape[2]
    values = got[...].astype(jnp.float32)
    sumsq = jnp.sum(jnp.sum(values * values, axis=0), axis=-1, keepdims=True)
    scale = lax.rsqrt(sumsq / (n_t * width) + 1e-06)
    for t in range(n_t):
        piece = values[t] * scale * gain_ref[:, pl.ds(t * width, width)]
        block_ref[:, pl.ds(t * width, width)] = piece.astype(block_ref.dtype)
    tgt = target_ref[...]
    lane = lax.broadcasted_iota(jnp.int32, (tgt.shape[0], 128), 1)
    tail = jnp.where(lane == 0, tgt // 65536, jnp.where(lane == 1, (tgt // 256) % 256,
                                                          jnp.where(lane == 2, tgt % 256, 0)))
    block_ref[:, pl.ds(n_t * width, 128)] = tail.astype(jnp.float32).astype(block_ref.dtype)

    sends = []

    def put(src_slot, dst_slot, target):
        src = block_ref if src_slot is None else out_ref.at[src_slot]
        copy = pltpu.make_async_remote_copy(
            src_ref=src, dst_ref=out_ref.at[dst_slot], send_sem=send.at[len(sends)],
            recv_sem=recv.at[dst_slot], device_id=target, device_id_type=MESH)
        copy.start()
        sends.append(copy)

    def arrive(dst_slot):
        pltpu.make_async_remote_copy(
            src_ref=block_ref, dst_ref=out_ref.at[dst_slot], send_sem=send.at[0],
            recv_sem=recv.at[dst_slot], device_id=sib_dev, device_id_type=MESH).wait_recv()

    own = pltpu.make_async_copy(block_ref, out_ref.at[me], local.at[0])
    own.start()
    for target in (plus_a, minus_a, plus_b, minus_b, sib_dev):
        put(None, me, target)

    left, right, far = slot(ua - 1, ub, core), slot(ua + 1, ub, core), slot(ua + 2, ub, core)
    arrive(left)
    for target in (plus_b, minus_b, sib_dev):
        put(left, left, target)
    arrive(right)
    for target in (plus_b, minus_b, sib_dev):
        put(right, right, target)
    pick = 1 - (ua + 3 + core) % 2
    fwd = pick * left + (1 - pick) * right
    fwd_dev = (pick * plus_a[0] + (1 - pick) * minus_a[0], mt)
    put(fwd, fwd, fwd_dev)
    arrive(far)
    for target in (plus_b, minus_b, sib_dev):
        put(far, far, target)

    pick_b = 1 - (ub + 3 + core) % 2
    for d in (0, -1, 1, 2):
        lo, hi = slot(ua + d, ub - 1, core), slot(ua + d, ub + 1, core)
        arrive(lo)
        put(lo, lo, sib_dev)
        arrive(hi)
        put(hi, hi, sib_dev)
        fwd = pick_b * lo + (1 - pick_b) * hi
        fwd_dev = (pick_b * plus_b[0] + (1 - pick_b) * minus_b[0], mt)
        put(fwd, fwd, fwd_dev)
    for d in (0, -1, 1, 2):
        far_b = slot(ua + d, ub + 2, core)
        arrive(far_b)
        put(far_b, far_b, sib_dev)

    for c in range(n_chip):
        arrive(c * 2 + 1 - core)
    for copy in sends:
        copy.wait_send()
    own.wait()


def gather_rows(rows, gain, target, n_dp, n_t):
    k, width = rows.shape
    shape = (k, n_t * width + 128)
    return pl.pallas_call(
        rows_kernel,
        out_shape=jax.ShapeDtypeStruct((n_dp,) + shape, rows.dtype),
        in_specs=[pl.BlockSpec(memory_space=pltpu.VMEM)] * 3,
        out_specs=pl.BlockSpec(memory_space=pl.ANY),
        scratch_shapes=[
            pltpu.VMEM((n_t, k, width), rows.dtype),
            pltpu.VMEM(shape, rows.dtype),
            pltpu.SemaphoreType.DMA((n_t,)),
            pltpu.SemaphoreType.DMA((n_t,)),
            pltpu.SemaphoreType.DMA((n_dp,)),
            pltpu.SemaphoreType.DMA((n_dp,)),
            pltpu.SemaphoreType.DMA((2,)),
        ],
        compiler_params=pltpu.CompilerParams(collective_id=2, has_side_effects=True, vmem_limit_bytes=16 * 1024 * 1024),
    )(rows, gain.reshape(1, n_t * width), target.reshape(k, 1))


def per_device(hidden, gain, head, lengths, offsets, targets, mask):
    seq_count, slot_count = offsets.shape
    slots = seq_count * slot_count
    maxlen = hidden.shape[1]
    n_dp = lax.axis_size("dp")
    n_t = lax.axis_size("tensor")
    k = min(LIVE, slots)

    live = (mask.reshape(slots) != 0).astype(jnp.int32)
    slot_ids = jnp.arange(slots, dtype=jnp.int32)
    rank = jnp.sum(jnp.where(slot_ids[:, None] >= slot_ids[None, :], live[None, :], 0), axis=1) - 1
    sel = (live[None, :] != 0) & (rank[None, :] == jnp.arange(k, dtype=jnp.int32)[:, None])
    seq_of = jnp.sum(jnp.where(sel, (slot_ids // slot_count)[None, :], 0), axis=1)
    offset_of = jnp.sum(jnp.where(sel, offsets.reshape(1, slots), 0), axis=1)
    flat_target = jnp.sum(jnp.where(sel, targets.reshape(1, slots), 0), axis=1)
    length_of = jnp.sum(jnp.where(seq_of[:, None] == jnp.arange(seq_count)[None, :], lengths[None, :], 0), axis=1)
    position = length_of - 1 - offset_of
    flat_hidden = hidden.reshape(seq_count * maxlen, hidden.shape[2])
    picked = jnp.take(flat_hidden, seq_of * maxlen + position, axis=0)

    vocab_width = head.shape[1]
    vocab_start = (lax.axis_index("dp") * n_t + lax.axis_index("tensor")) * vocab_width
    columns = jnp.arange(vocab_width, dtype=jnp.int32)
    width = n_t * picked.shape[1]
    gathered = gather_rows(picked, gain, flat_target, n_dp, n_t).reshape(n_dp * k, width + 128)
    rows_piece = gathered[:, :width]
    got_digits = gathered[:, width : width + 3].astype(jnp.int32)
    target_piece = got_digits[:, 0] * 65536 + got_digits[:, 1] * 256 + got_digits[:, 2]
    logits = jnp.dot(rows_piece, head, preferred_element_type=jnp.float32)
    top = jnp.max(logits, axis=-1)
    expo = jnp.exp(logits - top[:, None])
    total = jnp.sum(expo, axis=-1)
    weighted = jnp.sum(expo * logits, axis=-1)
    hit = columns[None, :] == (target_piece - vocab_start)[:, None]
    chosen = jnp.sum(jnp.where(hit, logits, 0.0), axis=-1)

    parts = jnp.stack([top, total, weighted, chosen]).reshape(4, n_dp, k).transpose(1, 0, 2)
    top, total, weighted, chosen = exchange_stats(parts, n_t)
    lse = top + jnp.log(total)
    score = chosen - lse
    spread = lse - weighted / total

    logprob = jnp.sum(jnp.where(sel, score[:, None], 0.0), axis=0)
    entropy = jnp.sum(jnp.where(sel, spread[:, None], 0.0), axis=0)
    return (logprob.reshape(seq_count, slot_count), entropy.reshape(seq_count, slot_count))


def solution(mesh):
    return jax.shard_map(
        per_device,
        mesh=mesh,
        in_specs=(
            P("dp", None, "tensor"),
            P(),
            P(None, ("dp", "tensor")),
            P("dp"),
            P("dp", None),
            P("dp", None),
            P("dp", None),
        ),
        out_specs=(P("dp", None), P("dp", None)),
        check_vma=False,
    )
```

```python
import functools

import jax
import jax.numpy as jnp
from jax import lax
from jax.experimental import pallas as pl
from jax.experimental.pallas import tpu as pltpu
from jax.sharding import PartitionSpec as P

MESH = pl.DeviceIdType.MESH
LIVE = 16
RING = 4


def merge(parts):
    tops = parts[:, 0, :]
    top = jnp.max(tops, axis=0, keepdims=True)
    factor = jnp.exp(tops - top)
    total = jnp.sum(parts[:, 1, :] * factor, axis=0, keepdims=True)
    weighted = jnp.sum(parts[:, 2, :] * factor, axis=0, keepdims=True)
    chosen = jnp.sum(parts[:, 3, :], axis=0, keepdims=True)
    return jnp.concatenate([top, total, weighted, chosen], axis=0)


def stats_kernel(part_ref, out_ref, got1, sent, got2, send1, recv1, send2, recv2, local):
    n_dp = part_ref.shape[0]
    n_t = got2.shape[0]
    me = lax.axis_index("dp")
    mt = lax.axis_index("tensor")

    barrier = pltpu.get_barrier_semaphore()

    def greet_dp(i, carry):
        p = lax.rem(me + 1 + i, n_dp)
        pl.semaphore_signal(barrier, 1, device_id=(p, mt), device_id_type=MESH)
        return carry

    def greet_t(i, carry):
        q = lax.rem(mt + 1 + i, n_t)
        pl.semaphore_signal(barrier, 1, device_id=(me, q), device_id_type=MESH)
        return carry

    lax.fori_loop(0, n_dp - 1, greet_dp, 0)
    lax.fori_loop(0, n_t - 1, greet_t, 0)
    pl.semaphore_wait(barrier, n_dp - 1 + n_t - 1)

    def out1(p):
        return pltpu.make_async_remote_copy(
            src_ref=part_ref.at[p], dst_ref=got1.at[me], send_sem=send1.at[p],
            recv_sem=recv1.at[me], device_id=(p, mt), device_id_type=MESH)

    def in1(p):
        return pltpu.make_async_remote_copy(
            src_ref=part_ref.at[p], dst_ref=got1.at[p], send_sem=send1.at[p],
            recv_sem=recv1.at[p], device_id=(p, mt), device_id_type=MESH)

    def start1(i, carry):
        out1(lax.rem(me + 1 + i, n_dp)).start()
        return carry

    lax.fori_loop(0, n_dp - 1, start1, 0)
    own1 = pltpu.make_async_copy(part_ref.at[me], got1.at[me], local.at[0])
    own1.start()

    def finish1(i, carry):
        p = lax.rem(me + 1 + i, n_dp)
        in1(p).wait_recv()
        out1(p).wait_send()
        return carry

    lax.fori_loop(0, n_dp - 1, finish1, 0)
    own1.wait()

    sent[...] = merge(got1[...])

    def out2(q):
        return pltpu.make_async_remote_copy(
            src_ref=sent, dst_ref=got2.at[mt], send_sem=send2.at[q],
            recv_sem=recv2.at[mt], device_id=(me, q), device_id_type=MESH)

    def in2(q):
        return pltpu.make_async_remote_copy(
            src_ref=sent, dst_ref=got2.at[q], send_sem=send2.at[q],
            recv_sem=recv2.at[q], device_id=(me, q), device_id_type=MESH)

    def start2(i, carry):
        out2(lax.rem(mt + 1 + i, n_t)).start()
        return carry

    lax.fori_loop(0, n_t - 1, start2, 0)
    own2 = pltpu.make_async_copy(sent, got2.at[mt], local.at[1])
    own2.start()

    def finish2(i, carry):
        q = lax.rem(mt + 1 + i, n_t)
        in2(q).wait_recv()
        out2(q).wait_send()
        return carry

    lax.fori_loop(0, n_t - 1, finish2, 0)
    own2.wait()

    out_ref[...] = merge(got2[...])


def exchange_stats(parts, n_t):
    n_dp, four, k = parts.shape
    return pl.pallas_call(
        stats_kernel,
        out_shape=jax.ShapeDtypeStruct((four, k), jnp.float32),
        in_specs=[pl.BlockSpec(memory_space=pltpu.VMEM)],
        out_specs=pl.BlockSpec(memory_space=pltpu.VMEM),
        scratch_shapes=[
            pltpu.VMEM((n_dp, four, k), jnp.float32),
            pltpu.VMEM((four, k), jnp.float32),
            pltpu.VMEM((n_t, four, k), jnp.float32),
            pltpu.SemaphoreType.DMA((n_dp,)),
            pltpu.SemaphoreType.DMA((n_dp,)),
            pltpu.SemaphoreType.DMA((n_t,)),
            pltpu.SemaphoreType.DMA((n_t,)),
            pltpu.SemaphoreType.DMA((2,)),
        ],
        compiler_params=pltpu.CompilerParams(collective_id=0, has_side_effects=True, vmem_limit_bytes=16 * 1024 * 1024),
    )(parts)


def rows_kernel(rows_ref, gain_ref, target_ref, out_ref, got, block_ref, send_t, recv_t, send, recv, local):
    n_dp = out_ref.shape[0]
    n_chip = n_dp // 2
    me = lax.axis_index("dp")
    mt = lax.axis_index("tensor")
    chip = me // 2
    core = me % 2
    x = chip % RING
    y = chip // RING
    ua = x + (y - x) * core
    ub = y + (x - y) * core
    sib = me + 1 - 2 * core

    def slot(a, b, parity):
        a = (a + 2 * RING) % RING
        b = (b + 2 * RING) % RING
        xx = a + (b - a) * core
        yy = b + (a - b) * core
        return (yy * RING + xx) * 2 + parity

    def dev(a, b):
        return (slot(a, b, core), mt)

    plus_a, minus_a = dev(ua + 1, ub), dev(ua - 1, ub)
    plus_b, minus_b = dev(ua, ub + 1), dev(ua, ub - 1)
    sib_dev = (sib, mt)

    n_t = got.shape[0]
    barrier = pltpu.get_barrier_semaphore()
    for target in (plus_a, minus_a, plus_b, minus_b, sib_dev):
        pl.semaphore_signal(barrier, 1, device_id=target, device_id_type=MESH)

    def greet(i, carry):
        q = lax.rem(mt + 1 + i, n_t)
        pl.semaphore_signal(barrier, 1, device_id=(me, q), device_id_type=MESH)
        return carry

    lax.fori_loop(0, n_t - 1, greet, 0)
    pl.semaphore_wait(barrier, 5 + n_t - 1)

    def t_out(q):
        return pltpu.make_async_remote_copy(
            src_ref=rows_ref, dst_ref=got.at[mt], send_sem=send_t.at[q],
            recv_sem=recv_t.at[mt], device_id=(me, q), device_id_type=MESH)

    def t_in(q):
        return pltpu.make_async_remote_copy(
            src_ref=rows_ref, dst_ref=got.at[q], send_sem=send_t.at[q],
            recv_sem=recv_t.at[q], device_id=(me, q), device_id_type=MESH)

    def t_start(i, carry):
        t_out(lax.rem(mt + 1 + i, n_t)).start()
        return carry

    lax.fori_loop(0, n_t - 1, t_start, 0)
    own_t = pltpu.make_async_copy(rows_ref, got.at[mt], local.at[1])
    own_t.start()

    def t_finish(i, carry):
        q = lax.rem(mt + 1 + i, n_t)
        t_in(q).wait_recv()
        t_out(q).wait_send()
        return carry

    lax.fori_loop(0, n_t - 1, t_finish, 0)
    own_t.wait()

    width = got.shape[2]
    values = got[...].astype(jnp.float32)
    sumsq = jnp.sum(jnp.sum(values * values, axis=0), axis=-1, keepdims=True)
    scale = lax.rsqrt(sumsq / (n_t * width) + 1e-06)
    for t in range(n_t):
        piece = values[t] * scale * gain_ref[:, pl.ds(t * width, width)]
        block_ref[:, pl.ds(t * width, width)] = piece.astype(block_ref.dtype)
    tgt = target_ref[...]
    lane = lax.broadcasted_iota(jnp.int32, (tgt.shape[0], 128), 1)
    tail = jnp.where(lane == 0, tgt // 65536, jnp.where(lane == 1, (tgt // 256) % 256,
                                                          jnp.where(lane == 2, tgt % 256, 0)))
    block_ref[:, pl.ds(n_t * width, 128)] = tail.astype(jnp.float32).astype(block_ref.dtype)

    sends = []
    cols = block_ref.shape[1]
    split = (cols // 256) * 128
    halves = ((0, split), (split, cols - split))

    def put(src_slot, dst_slot, target, h):
        c0, cw = halves[h]
        src = block_ref if src_slot is None else out_ref.at[src_slot]
        copy = pltpu.make_async_remote_copy(
            src_ref=src.at[:, pl.ds(c0, cw)], dst_ref=out_ref.at[dst_slot, :, pl.ds(c0, cw)],
            send_sem=send.at[len(sends)], recv_sem=recv.at[dst_slot, h], device_id=target,
            device_id_type=MESH)
        copy.start()
        sends.append(copy)

    def arrive(dst_slot, h):
        c0, cw = halves[h]
        pltpu.make_async_remote_copy(
            src_ref=block_ref.at[:, pl.ds(c0, cw)], dst_ref=out_ref.at[dst_slot, :, pl.ds(c0, cw)],
            send_sem=send.at[0], recv_sem=recv.at[dst_slot, h], device_id=sib_dev,
            device_id_type=MESH).wait_recv()

    own = pltpu.make_async_copy(block_ref, out_ref.at[me], local.at[0])
    own.start()
    for h in (0, 1):
        for target in (plus_a, minus_a, plus_b, minus_b, sib_dev):
            put(None, me, target, h)

    left, right, far = slot(ua - 1, ub, core), slot(ua + 1, ub, core), slot(ua + 2, ub, core)
    pick = 1 - (ua + 3 + core) % 2
    fwd = pick * left + (1 - pick) * right
    fwd_dev = (pick * plus_a[0] + (1 - pick) * minus_a[0], mt)
    for h in (0, 1):
        arrive(left, h)
        arrive(right, h)
        put(fwd, fwd, fwd_dev, h)
        for src in (left, right):
            for target in (plus_b, minus_b, sib_dev):
                put(src, src, target, h)
    for h in (0, 1):
        arrive(far, h)
        for target in (plus_b, minus_b, sib_dev):
            put(far, far, target, h)

    pick_b = 1 - (ub + 3 + core) % 2
    for d in (0, -1, 1, 2):
        lo, hi = slot(ua + d, ub - 1, core), slot(ua + d, ub + 1, core)
        fwd = pick_b * lo + (1 - pick_b) * hi
        fwd_dev = (pick_b * plus_b[0] + (1 - pick_b) * minus_b[0], mt)
        for h in (0, 1):
            arrive(lo, h)
            arrive(hi, h)
            put(fwd, fwd, fwd_dev, h)
            put(lo, lo, sib_dev, h)
            put(hi, hi, sib_dev, h)
    for d in (0, -1, 1, 2):
        far_b = slot(ua + d, ub + 2, core)
        for h in (0, 1):
            arrive(far_b, h)
            put(far_b, far_b, sib_dev, h)

    for c in range(n_chip):
        for h in (0, 1):
            arrive(c * 2 + 1 - core, h)
    for copy in sends:
        copy.wait_send()
    own.wait()


def gather_rows(rows, gain, target, n_dp, n_t):
    k, width = rows.shape
    shape = (k, n_t * width + 128)
    return pl.pallas_call(
        rows_kernel,
        out_shape=jax.ShapeDtypeStruct((n_dp,) + shape, rows.dtype),
        in_specs=[pl.BlockSpec(memory_space=pltpu.VMEM)] * 3,
        out_specs=pl.BlockSpec(memory_space=pl.ANY),
        scratch_shapes=[
            pltpu.VMEM((n_t, k, width), rows.dtype),
            pltpu.VMEM(shape, rows.dtype),
            pltpu.SemaphoreType.DMA((n_t,)),
            pltpu.SemaphoreType.DMA((n_t,)),
            pltpu.SemaphoreType.DMA((2 * n_dp,)),
            pltpu.SemaphoreType.DMA((n_dp, 2)),
            pltpu.SemaphoreType.DMA((2,)),
        ],
        compiler_params=pltpu.CompilerParams(collective_id=2, has_side_effects=True, vmem_limit_bytes=16 * 1024 * 1024),
    )(rows, gain.reshape(1, n_t * width), target.reshape(k, 1))


def per_device(hidden, gain, head, lengths, offsets, targets, mask):
    seq_count, slot_count = offsets.shape
    slots = seq_count * slot_count
    maxlen = hidden.shape[1]
    n_dp = lax.axis_size("dp")
    n_t = lax.axis_size("tensor")
    k = min(LIVE, slots)

    live = (mask.reshape(slots) != 0).astype(jnp.int32)
    slot_ids = jnp.arange(slots, dtype=jnp.int32)
    rank = jnp.sum(jnp.where(slot_ids[:, None] >= slot_ids[None, :], live[None, :], 0), axis=1) - 1
    sel = (live[None, :] != 0) & (rank[None, :] == jnp.arange(k, dtype=jnp.int32)[:, None])
    seq_of = jnp.sum(jnp.where(sel, (slot_ids // slot_count)[None, :], 0), axis=1)
    offset_of = jnp.sum(jnp.where(sel, offsets.reshape(1, slots), 0), axis=1)
    flat_target = jnp.sum(jnp.where(sel, targets.reshape(1, slots), 0), axis=1)
    length_of = jnp.sum(jnp.where(seq_of[:, None] == jnp.arange(seq_count)[None, :], lengths[None, :], 0), axis=1)
    position = length_of - 1 - offset_of
    flat_hidden = hidden.reshape(seq_count * maxlen, hidden.shape[2])
    picked = jnp.take(flat_hidden, seq_of * maxlen + position, axis=0)

    vocab_width = head.shape[1]
    vocab_start = (lax.axis_index("dp") * n_t + lax.axis_index("tensor")) * vocab_width
    columns = jnp.arange(vocab_width, dtype=jnp.int32)
    width = n_t * picked.shape[1]
    gathered = gather_rows(picked, gain, flat_target, n_dp, n_t).reshape(n_dp * k, width + 128)
    rows_piece = gathered[:, :width]
    got_digits = gathered[:, width : width + 3].astype(jnp.int32)
    target_piece = got_digits[:, 0] * 65536 + got_digits[:, 1] * 256 + got_digits[:, 2]
    logits = jnp.dot(rows_piece, head, preferred_element_type=jnp.float32)
    top = jnp.max(logits, axis=-1)
    expo = jnp.exp(logits - top[:, None])
    total = jnp.sum(expo, axis=-1)
    weighted = jnp.sum(expo * logits, axis=-1)
    hit = columns[None, :] == (target_piece - vocab_start)[:, None]
    chosen = jnp.sum(jnp.where(hit, logits, 0.0), axis=-1)

    parts = jnp.stack([top, total, weighted, chosen]).reshape(4, n_dp, k).transpose(1, 0, 2)
    top, total, weighted, chosen = exchange_stats(parts, n_t)
    lse = top + jnp.log(total)
    score = chosen - lse
    spread = lse - weighted / total

    logprob = jnp.sum(jnp.where(sel, score[:, None], 0.0), axis=0)
    entropy = jnp.sum(jnp.where(sel, spread[:, None], 0.0), axis=0)
    return (logprob.reshape(seq_count, slot_count), entropy.reshape(seq_count, slot_count))


def solution(mesh):
    return jax.shard_map(
        per_device,
        mesh=mesh,
        in_specs=(
            P("dp", None, "tensor"),
            P(),
            P(None, ("dp", "tensor")),
            P("dp"),
            P("dp", None),
            P("dp", None),
            P("dp", None),
        ),
        out_specs=(P("dp", None), P("dp", None)),
        check_vma=False,
    )
```

```python
import functools

import jax
import jax.numpy as jnp
from jax import lax
from jax.experimental import pallas as pl
from jax.experimental.pallas import tpu as pltpu
from jax.sharding import PartitionSpec as P

MESH = pl.DeviceIdType.MESH
LIVE = 16
RING = 4


def merge(parts):
    tops = parts[:, :, 0:1]
    top = jnp.max(tops, axis=0)
    factor = jnp.exp(tops - top[None])
    total = jnp.sum(parts[:, :, 1:2] * factor, axis=0)
    weighted = jnp.sum(parts[:, :, 2:3] * factor, axis=0)
    chosen = jnp.sum(parts[:, :, 3:4], axis=0)
    return pack(top, total, weighted, chosen)


def pack(top, total, weighted, chosen):
    lane = lax.broadcasted_iota(jnp.int32, (top.shape[0], 128), 1)
    return jnp.where(lane == 0, top, jnp.where(lane == 1, total, jnp.where(
        lane == 2, weighted, jnp.where(lane == 3, chosen, 0.0))))


def stats_kernel(rows_ref, head_ref, out_ref, parts, got1, sent, got2, send1, recv1, send2, recv2, local):
    n_dp, k, _ = got1.shape
    n_t = got2.shape[0]
    me = lax.axis_index("dp")
    mt = lax.axis_index("tensor")
    vocab = head_ref.shape[1]
    width = head_ref.shape[0]

    barrier = pltpu.get_barrier_semaphore()

    def greet_dp(i, carry):
        p = lax.rem(me + 1 + i, n_dp)
        pl.semaphore_signal(barrier, 1, device_id=(p, mt), device_id_type=MESH)
        return carry

    def greet_t(i, carry):
        q = lax.rem(mt + 1 + i, n_t)
        pl.semaphore_signal(barrier, 1, device_id=(me, q), device_id_type=MESH)
        return carry

    lax.fori_loop(0, n_dp - 1, greet_dp, 0)
    lax.fori_loop(0, n_t - 1, greet_t, 0)

    vocab_start = (me * n_t + mt) * vocab
    chunk = 128

    def local_stats(c, carry):
        r0 = pl.multiple_of(c * chunk, chunk)
        logits = jnp.dot(rows_ref[pl.ds(r0, chunk), pl.ds(0, width)], head_ref[...],
                         preferred_element_type=jnp.float32)
        top = jnp.max(logits, axis=1, keepdims=True)
        expo = jnp.exp(logits - top)
        total = jnp.sum(expo, axis=1, keepdims=True)
        weighted = jnp.sum(expo * logits, axis=1, keepdims=True)
        digits = rows_ref[pl.ds(r0, chunk), pl.ds(width, 128)].astype(jnp.float32)
        lane = lax.broadcasted_iota(jnp.int32, digits.shape, 1)
        place = jnp.where(lane == 0, 65536.0, jnp.where(lane == 1, 256.0, jnp.where(lane == 2, 1.0, 0.0)))
        target = jnp.sum(digits * place, axis=1, keepdims=True).astype(jnp.int32)
        column = lax.broadcasted_iota(jnp.int32, logits.shape, 1) + vocab_start
        chosen = jnp.sum(jnp.where(column == target, logits, 0.0), axis=1, keepdims=True)
        parts[pl.ds(r0, chunk), :] = pack(top, total, weighted, chosen)
        return carry

    lax.fori_loop(0, rows_ref.shape[0] // chunk, local_stats, 0)
    pl.semaphore_wait(barrier, n_dp - 1 + n_t - 1)

    def out1(p):
        return pltpu.make_async_remote_copy(
            src_ref=parts.at[pl.ds(p * k, k)], dst_ref=got1.at[me], send_sem=send1.at[p],
            recv_sem=recv1.at[me], device_id=(p, mt), device_id_type=MESH)

    def in1(p):
        return pltpu.make_async_remote_copy(
            src_ref=parts.at[pl.ds(p * k, k)], dst_ref=got1.at[p], send_sem=send1.at[p],
            recv_sem=recv1.at[p], device_id=(p, mt), device_id_type=MESH)

    def start1(i, carry):
        out1(lax.rem(me + 1 + i, n_dp)).start()
        return carry

    lax.fori_loop(0, n_dp - 1, start1, 0)
    own1 = pltpu.make_async_copy(parts.at[pl.ds(me * k, k)], got1.at[me], local.at[0])
    own1.start()

    def finish1(i, carry):
        p = lax.rem(me + 1 + i, n_dp)
        in1(p).wait_recv()
        out1(p).wait_send()
        return carry

    lax.fori_loop(0, n_dp - 1, finish1, 0)
    own1.wait()

    sent[...] = merge(got1[...])

    def out2(q):
        return pltpu.make_async_remote_copy(
            src_ref=sent, dst_ref=got2.at[mt], send_sem=send2.at[q],
            recv_sem=recv2.at[mt], device_id=(me, q), device_id_type=MESH)

    def in2(q):
        return pltpu.make_async_remote_copy(
            src_ref=sent, dst_ref=got2.at[q], send_sem=send2.at[q],
            recv_sem=recv2.at[q], device_id=(me, q), device_id_type=MESH)

    def start2(i, carry):
        out2(lax.rem(mt + 1 + i, n_t)).start()
        return carry

    lax.fori_loop(0, n_t - 1, start2, 0)
    own2 = pltpu.make_async_copy(sent, got2.at[mt], local.at[1])
    own2.start()

    def finish2(i, carry):
        q = lax.rem(mt + 1 + i, n_t)
        in2(q).wait_recv()
        out2(q).wait_send()
        return carry

    lax.fori_loop(0, n_t - 1, finish2, 0)
    own2.wait()

    out_ref[...] = merge(got2[...])


def exchange_stats(rows, head, n_dp, n_t, k):
    return pl.pallas_call(
        stats_kernel,
        out_shape=jax.ShapeDtypeStruct((k, 128), jnp.float32),
        in_specs=[pl.BlockSpec(memory_space=pltpu.VMEM)] * 2,
        out_specs=pl.BlockSpec(memory_space=pltpu.VMEM),
        scratch_shapes=[
            pltpu.VMEM((n_dp * k, 128), jnp.float32),
            pltpu.VMEM((n_dp, k, 128), jnp.float32),
            pltpu.VMEM((k, 128), jnp.float32),
            pltpu.VMEM((n_t, k, 128), jnp.float32),
            pltpu.SemaphoreType.DMA((n_dp,)),
            pltpu.SemaphoreType.DMA((n_dp,)),
            pltpu.SemaphoreType.DMA((n_t,)),
            pltpu.SemaphoreType.DMA((n_t,)),
            pltpu.SemaphoreType.DMA((2,)),
        ],
        compiler_params=pltpu.CompilerParams(collective_id=0, has_side_effects=True, vmem_limit_bytes=32 * 1024 * 1024),
    )(rows, head)


def rows_kernel(rows_ref, gain_ref, target_ref, out_ref, got, block_ref, send_t, recv_t, send, recv, local):
    n_dp = out_ref.shape[0]
    n_chip = n_dp // 2
    me = lax.axis_index("dp")
    mt = lax.axis_index("tensor")
    chip = me // 2
    core = me % 2
    x = chip % RING
    y = chip // RING
    ua = x + (y - x) * core
    ub = y + (x - y) * core
    sib = me + 1 - 2 * core

    def slot(a, b, parity):
        a = (a + 2 * RING) % RING
        b = (b + 2 * RING) % RING
        xx = a + (b - a) * core
        yy = b + (a - b) * core
        return (yy * RING + xx) * 2 + parity

    def dev(a, b):
        return (slot(a, b, core), mt)

    plus_a, minus_a = dev(ua + 1, ub), dev(ua - 1, ub)
    plus_b, minus_b = dev(ua, ub + 1), dev(ua, ub - 1)
    sib_dev = (sib, mt)

    n_t = got.shape[0]
    barrier = pltpu.get_barrier_semaphore()
    for target in (plus_a, minus_a, plus_b, minus_b, sib_dev):
        pl.semaphore_signal(barrier, 1, device_id=target, device_id_type=MESH)

    def greet(i, carry):
        q = lax.rem(mt + 1 + i, n_t)
        pl.semaphore_signal(barrier, 1, device_id=(me, q), device_id_type=MESH)
        return carry

    lax.fori_loop(0, n_t - 1, greet, 0)
    pl.semaphore_wait(barrier, 5 + n_t - 1)

    def t_out(q):
        return pltpu.make_async_remote_copy(
            src_ref=rows_ref, dst_ref=got.at[mt], send_sem=send_t.at[q],
            recv_sem=recv_t.at[mt], device_id=(me, q), device_id_type=MESH)

    def t_in(q):
        return pltpu.make_async_remote_copy(
            src_ref=rows_ref, dst_ref=got.at[q], send_sem=send_t.at[q],
            recv_sem=recv_t.at[q], device_id=(me, q), device_id_type=MESH)

    def t_start(i, carry):
        t_out(lax.rem(mt + 1 + i, n_t)).start()
        return carry

    lax.fori_loop(0, n_t - 1, t_start, 0)
    own_t = pltpu.make_async_copy(rows_ref, got.at[mt], local.at[1])
    own_t.start()

    def t_finish(i, carry):
        q = lax.rem(mt + 1 + i, n_t)
        t_in(q).wait_recv()
        t_out(q).wait_send()
        return carry

    lax.fori_loop(0, n_t - 1, t_finish, 0)
    own_t.wait()

    width = got.shape[2]
    values = got[...].astype(jnp.float32)
    sumsq = jnp.sum(jnp.sum(values * values, axis=0), axis=-1, keepdims=True)
    scale = lax.rsqrt(sumsq / (n_t * width) + 1e-06)
    for t in range(n_t):
        piece = values[t] * scale * gain_ref[:, pl.ds(t * width, width)]
        block_ref[:, pl.ds(t * width, width)] = piece.astype(block_ref.dtype)
    tgt = target_ref[...]
    lane = lax.broadcasted_iota(jnp.int32, (tgt.shape[0], 128), 1)
    tail = jnp.where(lane == 0, tgt // 65536, jnp.where(lane == 1, (tgt // 256) % 256,
                                                          jnp.where(lane == 2, tgt % 256, 0)))
    block_ref[:, pl.ds(n_t * width, 128)] = tail.astype(jnp.float32).astype(block_ref.dtype)

    sends = []
    cols = block_ref.shape[1]
    split = (cols // 256) * 128
    halves = ((0, split), (split, cols - split))

    def put(src_slot, dst_slot, target, h):
        c0, cw = halves[h]
        src = block_ref if src_slot is None else out_ref.at[src_slot]
        copy = pltpu.make_async_remote_copy(
            src_ref=src.at[:, pl.ds(c0, cw)], dst_ref=out_ref.at[dst_slot, :, pl.ds(c0, cw)],
            send_sem=send.at[len(sends)], recv_sem=recv.at[dst_slot, h], device_id=target,
            device_id_type=MESH)
        copy.start()
        sends.append(copy)

    def arrive(dst_slot, h):
        c0, cw = halves[h]
        pltpu.make_async_remote_copy(
            src_ref=block_ref.at[:, pl.ds(c0, cw)], dst_ref=out_ref.at[dst_slot, :, pl.ds(c0, cw)],
            send_sem=send.at[0], recv_sem=recv.at[dst_slot, h], device_id=sib_dev,
            device_id_type=MESH).wait_recv()

    own = pltpu.make_async_copy(block_ref, out_ref.at[me], local.at[0])
    own.start()
    for h in (0, 1):
        for target in (plus_a, minus_a, plus_b, minus_b, sib_dev):
            put(None, me, target, h)

    left, right, far = slot(ua - 1, ub, core), slot(ua + 1, ub, core), slot(ua + 2, ub, core)
    pick = 1 - (ua + 3 + core) % 2
    fwd = pick * left + (1 - pick) * right
    fwd_dev = (pick * plus_a[0] + (1 - pick) * minus_a[0], mt)
    for h in (0, 1):
        arrive(left, h)
        arrive(right, h)
        put(fwd, fwd, fwd_dev, h)
        for src in (left, right):
            for target in (plus_b, minus_b, sib_dev):
                put(src, src, target, h)
    for h in (0, 1):
        arrive(far, h)
        for target in (plus_b, minus_b, sib_dev):
            put(far, far, target, h)

    pick_b = 1 - (ub + 3 + core) % 2
    for d in (0, -1, 1, 2):
        lo, hi = slot(ua + d, ub - 1, core), slot(ua + d, ub + 1, core)
        fwd = pick_b * lo + (1 - pick_b) * hi
        fwd_dev = (pick_b * plus_b[0] + (1 - pick_b) * minus_b[0], mt)
        for h in (0, 1):
            arrive(lo, h)
            arrive(hi, h)
            put(fwd, fwd, fwd_dev, h)
            put(lo, lo, sib_dev, h)
            put(hi, hi, sib_dev, h)
    for d in (0, -1, 1, 2):
        far_b = slot(ua + d, ub + 2, core)
        for h in (0, 1):
            arrive(far_b, h)
            put(far_b, far_b, sib_dev, h)

    for c in range(n_chip):
        for h in (0, 1):
            arrive(c * 2 + 1 - core, h)
    for copy in sends:
        copy.wait_send()
    own.wait()


def gather_rows(rows, gain, target, n_dp, n_t):
    k, width = rows.shape
    shape = (k, n_t * width + 128)
    return pl.pallas_call(
        rows_kernel,
        out_shape=jax.ShapeDtypeStruct((n_dp,) + shape, rows.dtype),
        in_specs=[pl.BlockSpec(memory_space=pltpu.VMEM)] * 3,
        out_specs=pl.BlockSpec(memory_space=pl.ANY),
        scratch_shapes=[
            pltpu.VMEM((n_t, k, width), rows.dtype),
            pltpu.VMEM(shape, rows.dtype),
            pltpu.SemaphoreType.DMA((n_t,)),
            pltpu.SemaphoreType.DMA((n_t,)),
            pltpu.SemaphoreType.DMA((2 * n_dp,)),
            pltpu.SemaphoreType.DMA((n_dp, 2)),
            pltpu.SemaphoreType.DMA((2,)),
        ],
        compiler_params=pltpu.CompilerParams(collective_id=2, has_side_effects=True, vmem_limit_bytes=16 * 1024 * 1024),
    )(rows, gain.reshape(1, n_t * width), target.reshape(k, 1))


def per_device(hidden, gain, head, lengths, offsets, targets, mask):
    seq_count, slot_count = offsets.shape
    slots = seq_count * slot_count
    maxlen = hidden.shape[1]
    n_dp = lax.axis_size("dp")
    n_t = lax.axis_size("tensor")
    k = min(LIVE, slots)

    live = (mask.reshape(slots) != 0).astype(jnp.int32)
    slot_ids = jnp.arange(slots, dtype=jnp.int32)
    rank = jnp.sum(jnp.where(slot_ids[:, None] >= slot_ids[None, :], live[None, :], 0), axis=1) - 1
    sel = (live[None, :] != 0) & (rank[None, :] == jnp.arange(k, dtype=jnp.int32)[:, None])
    seq_of = jnp.sum(jnp.where(sel, (slot_ids // slot_count)[None, :], 0), axis=1)
    offset_of = jnp.sum(jnp.where(sel, offsets.reshape(1, slots), 0), axis=1)
    flat_target = jnp.sum(jnp.where(sel, targets.reshape(1, slots), 0), axis=1)
    length_of = jnp.sum(jnp.where(seq_of[:, None] == jnp.arange(seq_count)[None, :], lengths[None, :], 0), axis=1)
    position = length_of - 1 - offset_of
    flat_hidden = hidden.reshape(seq_count * maxlen, hidden.shape[2])
    picked = jnp.take(flat_hidden, seq_of * maxlen + position, axis=0)

    width = n_t * picked.shape[1]
    gathered = gather_rows(picked, gain, flat_target, n_dp, n_t).reshape(n_dp * k, width + 128)
    merged = exchange_stats(gathered, head, n_dp, n_t, k)
    top, total, weighted, chosen = merged[:, 0], merged[:, 1], merged[:, 2], merged[:, 3]
    lse = top + jnp.log(total)
    score = chosen - lse
    spread = lse - weighted / total

    logprob = jnp.sum(jnp.where(sel, score[:, None], 0.0), axis=0)
    entropy = jnp.sum(jnp.where(sel, spread[:, None], 0.0), axis=0)
    return (logprob.reshape(seq_count, slot_count), entropy.reshape(seq_count, slot_count))


def solution(mesh):
    return jax.shard_map(
        per_device,
        mesh=mesh,
        in_specs=(
            P("dp", None, "tensor"),
            P(),
            P(None, ("dp", "tensor")),
            P("dp"),
            P("dp", None),
            P("dp", None),
            P("dp", None),
        ),
        out_specs=(P("dp", None), P("dp", None)),
        check_vma=False,
    )
```

```python
import functools

import jax
import jax.numpy as jnp
from jax import lax
from jax.experimental import pallas as pl
from jax.experimental.pallas import tpu as pltpu
from jax.sharding import PartitionSpec as P

MESH = pl.DeviceIdType.MESH
LIVE = 16
RING = 4
PIECES = 4


def merge(parts):
    tops = parts[:, 0, :]
    top = jnp.max(tops, axis=0, keepdims=True)
    factor = jnp.exp(tops - top)
    total = jnp.sum(parts[:, 1, :] * factor, axis=0, keepdims=True)
    weighted = jnp.sum(parts[:, 2, :] * factor, axis=0, keepdims=True)
    chosen = jnp.sum(parts[:, 3, :], axis=0, keepdims=True)
    return jnp.concatenate([top, total, weighted, chosen], axis=0)


def stats_kernel(part_ref, out_ref, got1, sent, got2, send1, recv1, send2, recv2, local):
    n_dp = part_ref.shape[0]
    n_t = got2.shape[0]
    me = lax.axis_index("dp")
    mt = lax.axis_index("tensor")

    barrier = pltpu.get_barrier_semaphore()

    def greet_dp(i, carry):
        p = lax.rem(me + 1 + i, n_dp)
        pl.semaphore_signal(barrier, 1, device_id=(p, mt), device_id_type=MESH)
        return carry

    def greet_t(i, carry):
        q = lax.rem(mt + 1 + i, n_t)
        pl.semaphore_signal(barrier, 1, device_id=(me, q), device_id_type=MESH)
        return carry

    lax.fori_loop(0, n_dp - 1, greet_dp, 0)
    lax.fori_loop(0, n_t - 1, greet_t, 0)
    pl.semaphore_wait(barrier, n_dp - 1 + n_t - 1)

    def out1(p):
        return pltpu.make_async_remote_copy(
            src_ref=part_ref.at[p], dst_ref=got1.at[me], send_sem=send1.at[p],
            recv_sem=recv1.at[me], device_id=(p, mt), device_id_type=MESH)

    def in1(p):
        return pltpu.make_async_remote_copy(
            src_ref=part_ref.at[p], dst_ref=got1.at[p], send_sem=send1.at[p],
            recv_sem=recv1.at[p], device_id=(p, mt), device_id_type=MESH)

    def start1(i, carry):
        out1(lax.rem(me + 1 + i, n_dp)).start()
        return carry

    lax.fori_loop(0, n_dp - 1, start1, 0)
    own1 = pltpu.make_async_copy(part_ref.at[me], got1.at[me], local.at[0])
    own1.start()

    def finish1(i, carry):
        p = lax.rem(me + 1 + i, n_dp)
        in1(p).wait_recv()
        out1(p).wait_send()
        return carry

    lax.fori_loop(0, n_dp - 1, finish1, 0)
    own1.wait()

    sent[...] = merge(got1[...])

    def out2(q):
        return pltpu.make_async_remote_copy(
            src_ref=sent, dst_ref=got2.at[mt], send_sem=send2.at[q],
            recv_sem=recv2.at[mt], device_id=(me, q), device_id_type=MESH)

    def in2(q):
        return pltpu.make_async_remote_copy(
            src_ref=sent, dst_ref=got2.at[q], send_sem=send2.at[q],
            recv_sem=recv2.at[q], device_id=(me, q), device_id_type=MESH)

    def start2(i, carry):
        out2(lax.rem(mt + 1 + i, n_t)).start()
        return carry

    lax.fori_loop(0, n_t - 1, start2, 0)
    own2 = pltpu.make_async_copy(sent, got2.at[mt], local.at[1])
    own2.start()

    def finish2(i, carry):
        q = lax.rem(mt + 1 + i, n_t)
        in2(q).wait_recv()
        out2(q).wait_send()
        return carry

    lax.fori_loop(0, n_t - 1, finish2, 0)
    own2.wait()

    out_ref[...] = merge(got2[...])


def exchange_stats(parts, n_t):
    n_dp, four, k = parts.shape
    return pl.pallas_call(
        stats_kernel,
        out_shape=jax.ShapeDtypeStruct((four, k), jnp.float32),
        in_specs=[pl.BlockSpec(memory_space=pltpu.VMEM)],
        out_specs=pl.BlockSpec(memory_space=pltpu.VMEM),
        scratch_shapes=[
            pltpu.VMEM((n_dp, four, k), jnp.float32),
            pltpu.VMEM((four, k), jnp.float32),
            pltpu.VMEM((n_t, four, k), jnp.float32),
            pltpu.SemaphoreType.DMA((n_dp,)),
            pltpu.SemaphoreType.DMA((n_dp,)),
            pltpu.SemaphoreType.DMA((n_t,)),
            pltpu.SemaphoreType.DMA((n_t,)),
            pltpu.SemaphoreType.DMA((2,)),
        ],
        compiler_params=pltpu.CompilerParams(collective_id=0, has_side_effects=True, vmem_limit_bytes=16 * 1024 * 1024),
    )(parts)


def rows_kernel(rows_ref, gain_ref, target_ref, out_ref, got, block_ref, send_t, recv_t, send, recv, local):
    n_dp = out_ref.shape[0]
    n_chip = n_dp // 2
    me = lax.axis_index("dp")
    mt = lax.axis_index("tensor")
    chip = me // 2
    core = me % 2
    x = chip % RING
    y = chip // RING
    ua = x + (y - x) * core
    ub = y + (x - y) * core
    sib = me + 1 - 2 * core

    def slot(a, b, parity):
        a = (a + 2 * RING) % RING
        b = (b + 2 * RING) % RING
        xx = a + (b - a) * core
        yy = b + (a - b) * core
        return (yy * RING + xx) * 2 + parity

    def dev(a, b):
        return (slot(a, b, core), mt)

    plus_a, minus_a = dev(ua + 1, ub), dev(ua - 1, ub)
    plus_b, minus_b = dev(ua, ub + 1), dev(ua, ub - 1)
    sib_dev = (sib, mt)

    n_t = got.shape[0]
    barrier = pltpu.get_barrier_semaphore()
    for target in (plus_a, minus_a, plus_b, minus_b, sib_dev):
        pl.semaphore_signal(barrier, 1, device_id=target, device_id_type=MESH)

    def greet(i, carry):
        q = lax.rem(mt + 1 + i, n_t)
        pl.semaphore_signal(barrier, 1, device_id=(me, q), device_id_type=MESH)
        return carry

    lax.fori_loop(0, n_t - 1, greet, 0)
    pl.semaphore_wait(barrier, 5 + n_t - 1)

    def t_out(q):
        return pltpu.make_async_remote_copy(
            src_ref=rows_ref, dst_ref=got.at[mt], send_sem=send_t.at[q],
            recv_sem=recv_t.at[mt], device_id=(me, q), device_id_type=MESH)

    def t_in(q):
        return pltpu.make_async_remote_copy(
            src_ref=rows_ref, dst_ref=got.at[q], send_sem=send_t.at[q],
            recv_sem=recv_t.at[q], device_id=(me, q), device_id_type=MESH)

    def t_start(i, carry):
        t_out(lax.rem(mt + 1 + i, n_t)).start()
        return carry

    lax.fori_loop(0, n_t - 1, t_start, 0)
    own_t = pltpu.make_async_copy(rows_ref, got.at[mt], local.at[1])
    own_t.start()

    def t_finish(i, carry):
        q = lax.rem(mt + 1 + i, n_t)
        t_in(q).wait_recv()
        t_out(q).wait_send()
        return carry

    lax.fori_loop(0, n_t - 1, t_finish, 0)
    own_t.wait()

    width = got.shape[2]
    values = got[...].astype(jnp.float32)
    sumsq = jnp.sum(jnp.sum(values * values, axis=0), axis=-1, keepdims=True)
    scale = lax.rsqrt(sumsq / (n_t * width) + 1e-06)
    for t in range(n_t):
        piece = values[t] * scale * gain_ref[:, pl.ds(t * width, width)]
        block_ref[:, pl.ds(t * width, width)] = piece.astype(block_ref.dtype)
    tgt = target_ref[...]
    lane = lax.broadcasted_iota(jnp.int32, (tgt.shape[0], 128), 1)
    tail = jnp.where(lane == 0, tgt // 65536, jnp.where(lane == 1, (tgt // 256) % 256,
                                                          jnp.where(lane == 2, tgt % 256, 0)))
    block_ref[:, pl.ds(n_t * width, 128)] = tail.astype(jnp.float32).astype(block_ref.dtype)

    sends = []
    cols = block_ref.shape[1]
    pieces = min(PIECES, cols // 128)
    edges = [(cols // 128 * i // pieces) * 128 for i in range(pieces)] + [cols]
    halves = tuple((edges[i], edges[i + 1] - edges[i]) for i in range(pieces))

    def put(src_slot, dst_slot, target, h):
        c0, cw = halves[h]
        src = block_ref if src_slot is None else out_ref.at[src_slot]
        copy = pltpu.make_async_remote_copy(
            src_ref=src.at[:, pl.ds(c0, cw)], dst_ref=out_ref.at[dst_slot, :, pl.ds(c0, cw)],
            send_sem=send.at[len(sends)], recv_sem=recv.at[dst_slot, h], device_id=target,
            device_id_type=MESH)
        copy.start()
        sends.append(copy)

    def arrive(dst_slot, h):
        c0, cw = halves[h]
        pltpu.make_async_remote_copy(
            src_ref=block_ref.at[:, pl.ds(c0, cw)], dst_ref=out_ref.at[dst_slot, :, pl.ds(c0, cw)],
            send_sem=send.at[0], recv_sem=recv.at[dst_slot, h], device_id=sib_dev,
            device_id_type=MESH).wait_recv()

    own = pltpu.make_async_copy(block_ref, out_ref.at[me], local.at[0])
    own.start()
    for h in range(pieces):
        for target in (plus_a, minus_a, plus_b, minus_b, sib_dev):
            put(None, me, target, h)

    left, right, far = slot(ua - 1, ub, core), slot(ua + 1, ub, core), slot(ua + 2, ub, core)
    pick = 1 - (ua + 3 + core) % 2
    fwd = pick * left + (1 - pick) * right
    fwd_dev = (pick * plus_a[0] + (1 - pick) * minus_a[0], mt)
    for h in range(pieces):
        arrive(left, h)
        arrive(right, h)
        put(fwd, fwd, fwd_dev, h)
        for src in (left, right):
            for target in (plus_b, minus_b, sib_dev):
                put(src, src, target, h)
    for h in range(pieces):
        arrive(far, h)
        for target in (plus_b, minus_b, sib_dev):
            put(far, far, target, h)

    pick_b = 1 - (ub + 3 + core) % 2
    for d in (0, -1, 1, 2):
        lo, hi = slot(ua + d, ub - 1, core), slot(ua + d, ub + 1, core)
        fwd = pick_b * lo + (1 - pick_b) * hi
        fwd_dev = (pick_b * plus_b[0] + (1 - pick_b) * minus_b[0], mt)
        for h in range(pieces):
            arrive(lo, h)
            arrive(hi, h)
            put(fwd, fwd, fwd_dev, h)
            put(lo, lo, sib_dev, h)
            put(hi, hi, sib_dev, h)
    for d in (0, -1, 1, 2):
        far_b = slot(ua + d, ub + 2, core)
        for h in range(pieces):
            arrive(far_b, h)
            put(far_b, far_b, sib_dev, h)

    for c in range(n_chip):
        for h in range(pieces):
            arrive(c * 2 + 1 - core, h)
    for copy in sends:
        copy.wait_send()
    own.wait()


def gather_rows(rows, gain, target, n_dp, n_t):
    k, width = rows.shape
    shape = (k, n_t * width + 128)
    return pl.pallas_call(
        rows_kernel,
        out_shape=jax.ShapeDtypeStruct((n_dp,) + shape, rows.dtype),
        in_specs=[pl.BlockSpec(memory_space=pltpu.VMEM)] * 3,
        out_specs=pl.BlockSpec(memory_space=pl.ANY),
        scratch_shapes=[
            pltpu.VMEM((n_t, k, width), rows.dtype),
            pltpu.VMEM(shape, rows.dtype),
            pltpu.SemaphoreType.DMA((n_t,)),
            pltpu.SemaphoreType.DMA((n_t,)),
            pltpu.SemaphoreType.DMA((PIECES * n_dp,)),
            pltpu.SemaphoreType.DMA((n_dp, PIECES)),
            pltpu.SemaphoreType.DMA((2,)),
        ],
        compiler_params=pltpu.CompilerParams(collective_id=2, has_side_effects=True, vmem_limit_bytes=16 * 1024 * 1024),
    )(rows, gain.reshape(1, n_t * width), target.reshape(k, 1))


def per_device(hidden, gain, head, lengths, offsets, targets, mask):
    seq_count, slot_count = offsets.shape
    slots = seq_count * slot_count
    maxlen = hidden.shape[1]
    n_dp = lax.axis_size("dp")
    n_t = lax.axis_size("tensor")
    k = min(LIVE, slots)

    live = (mask.reshape(slots) != 0).astype(jnp.int32)
    slot_ids = jnp.arange(slots, dtype=jnp.int32)
    rank = jnp.sum(jnp.where(slot_ids[:, None] >= slot_ids[None, :], live[None, :], 0), axis=1) - 1
    sel = (live[None, :] != 0) & (rank[None, :] == jnp.arange(k, dtype=jnp.int32)[:, None])
    seq_of = jnp.sum(jnp.where(sel, (slot_ids // slot_count)[None, :], 0), axis=1)
    offset_of = jnp.sum(jnp.where(sel, offsets.reshape(1, slots), 0), axis=1)
    flat_target = jnp.sum(jnp.where(sel, targets.reshape(1, slots), 0), axis=1)
    length_of = jnp.sum(jnp.where(seq_of[:, None] == jnp.arange(seq_count)[None, :], lengths[None, :], 0), axis=1)
    position = length_of - 1 - offset_of
    flat_hidden = hidden.reshape(seq_count * maxlen, hidden.shape[2])
    picked = jnp.take(flat_hidden, seq_of * maxlen + position, axis=0)

    vocab_width = head.shape[1]
    vocab_start = (lax.axis_index("dp") * n_t + lax.axis_index("tensor")) * vocab_width
    columns = jnp.arange(vocab_width, dtype=jnp.int32)
    width = n_t * picked.shape[1]
    gathered = gather_rows(picked, gain, flat_target, n_dp, n_t).reshape(n_dp * k, width + 128)
    rows_piece = gathered[:, :width]
    got_digits = gathered[:, width : width + 3].astype(jnp.int32)
    target_piece = got_digits[:, 0] * 65536 + got_digits[:, 1] * 256 + got_digits[:, 2]
    logits = jnp.dot(rows_piece, head, preferred_element_type=jnp.float32)
    top = jnp.max(logits, axis=-1)
    expo = jnp.exp(logits - top[:, None])
    total = jnp.sum(expo, axis=-1)
    weighted = jnp.sum(expo * logits, axis=-1)
    hit = columns[None, :] == (target_piece - vocab_start)[:, None]
    chosen = jnp.sum(jnp.where(hit, logits, 0.0), axis=-1)

    parts = jnp.stack([top, total, weighted, chosen]).reshape(4, n_dp, k).transpose(1, 0, 2)
    top, total, weighted, chosen = exchange_stats(parts, n_t)
    lse = top + jnp.log(total)
    score = chosen - lse
    spread = lse - weighted / total

    logprob = jnp.sum(jnp.where(sel, score[:, None], 0.0), axis=0)
    entropy = jnp.sum(jnp.where(sel, spread[:, None], 0.0), axis=0)
    return (logprob.reshape(seq_count, slot_count), entropy.reshape(seq_count, slot_count))


def solution(mesh):
    return jax.shard_map(
        per_device,
        mesh=mesh,
        in_specs=(
            P("dp", None, "tensor"),
            P(),
            P(None, ("dp", "tensor")),
            P("dp"),
            P("dp", None),
            P("dp", None),
            P("dp", None),
        ),
        out_specs=(P("dp", None), P("dp", None)),
        check_vma=False,
    )
```

```python
import functools

import jax
import jax.numpy as jnp
from jax import lax
from jax.experimental import pallas as pl
from jax.experimental.pallas import tpu as pltpu
from jax.sharding import PartitionSpec as P

MESH = pl.DeviceIdType.MESH
LIVE = 16
RING = 4


def merge(parts):
    tops = parts[:, 0, :]
    top = jnp.max(tops, axis=0, keepdims=True)
    factor = jnp.exp(tops - top)
    total = jnp.sum(parts[:, 1, :] * factor, axis=0, keepdims=True)
    weighted = jnp.sum(parts[:, 2, :] * factor, axis=0, keepdims=True)
    chosen = jnp.sum(parts[:, 3, :], axis=0, keepdims=True)
    return jnp.concatenate([top, total, weighted, chosen], axis=0)


def stats_kernel(part_ref, out_ref, got1, sent, got2, send1, recv1, send2, recv2, local):
    n_dp = part_ref.shape[0]
    n_t = got2.shape[0]
    me = lax.axis_index("dp")
    mt = lax.axis_index("tensor")

    barrier = pltpu.get_barrier_semaphore()

    def greet_dp(i, carry):
        p = lax.rem(me + 1 + i, n_dp)
        pl.semaphore_signal(barrier, 1, device_id=(p, mt), device_id_type=MESH)
        return carry

    def greet_t(i, carry):
        q = lax.rem(mt + 1 + i, n_t)
        pl.semaphore_signal(barrier, 1, device_id=(me, q), device_id_type=MESH)
        return carry

    lax.fori_loop(0, n_dp - 1, greet_dp, 0)
    lax.fori_loop(0, n_t - 1, greet_t, 0)
    pl.semaphore_wait(barrier, n_dp - 1 + n_t - 1)

    def out1(p):
        return pltpu.make_async_remote_copy(
            src_ref=part_ref.at[p], dst_ref=got1.at[me], send_sem=send1.at[p],
            recv_sem=recv1.at[me], device_id=(p, mt), device_id_type=MESH)

    def in1(p):
        return pltpu.make_async_remote_copy(
            src_ref=part_ref.at[p], dst_ref=got1.at[p], send_sem=send1.at[p],
            recv_sem=recv1.at[p], device_id=(p, mt), device_id_type=MESH)

    def start1(i, carry):
        out1(lax.rem(me + 1 + i, n_dp)).start()
        return carry

    lax.fori_loop(0, n_dp - 1, start1, 0)
    own1 = pltpu.make_async_copy(part_ref.at[me], got1.at[me], local.at[0])
    own1.start()

    def finish1(i, carry):
        p = lax.rem(me + 1 + i, n_dp)
        in1(p).wait_recv()
        out1(p).wait_send()
        return carry

    lax.fori_loop(0, n_dp - 1, finish1, 0)
    own1.wait()

    sent[...] = merge(got1[...])

    def out2(q):
        return pltpu.make_async_remote_copy(
            src_ref=sent, dst_ref=got2.at[mt], send_sem=send2.at[q],
            recv_sem=recv2.at[mt], device_id=(me, q), device_id_type=MESH)

    def in2(q):
        return pltpu.make_async_remote_copy(
            src_ref=sent, dst_ref=got2.at[q], send_sem=send2.at[q],
            recv_sem=recv2.at[q], device_id=(me, q), device_id_type=MESH)

    def start2(i, carry):
        out2(lax.rem(mt + 1 + i, n_t)).start()
        return carry

    lax.fori_loop(0, n_t - 1, start2, 0)
    own2 = pltpu.make_async_copy(sent, got2.at[mt], local.at[1])
    own2.start()

    def finish2(i, carry):
        q = lax.rem(mt + 1 + i, n_t)
        in2(q).wait_recv()
        out2(q).wait_send()
        return carry

    lax.fori_loop(0, n_t - 1, finish2, 0)
    own2.wait()

    out_ref[...] = merge(got2[...])


def exchange_stats(parts, n_t):
    n_dp, four, k = parts.shape
    return pl.pallas_call(
        stats_kernel,
        out_shape=jax.ShapeDtypeStruct((four, k), jnp.float32),
        in_specs=[pl.BlockSpec(memory_space=pltpu.VMEM)],
        out_specs=pl.BlockSpec(memory_space=pltpu.VMEM),
        scratch_shapes=[
            pltpu.VMEM((n_dp, four, k), jnp.float32),
            pltpu.VMEM((four, k), jnp.float32),
            pltpu.VMEM((n_t, four, k), jnp.float32),
            pltpu.SemaphoreType.DMA((n_dp,)),
            pltpu.SemaphoreType.DMA((n_dp,)),
            pltpu.SemaphoreType.DMA((n_t,)),
            pltpu.SemaphoreType.DMA((n_t,)),
            pltpu.SemaphoreType.DMA((2,)),
        ],
        compiler_params=pltpu.CompilerParams(collective_id=0, has_side_effects=True, vmem_limit_bytes=16 * 1024 * 1024),
    )(parts)


def rows_kernel(rows_ref, gain_ref, target_ref, out_ref, got, block_ref, send_t, recv_t, send, recv, local):
    n_dp = out_ref.shape[0]
    n_chip = n_dp // 2
    me = lax.axis_index("dp")
    mt = lax.axis_index("tensor")
    chip = me // 2
    core = me % 2
    x = chip % RING
    y = chip // RING
    ua = x + (y - x) * core
    ub = y + (x - y) * core
    sib = me + 1 - 2 * core

    def slot(a, b, parity):
        a = (a + 2 * RING) % RING
        b = (b + 2 * RING) % RING
        xx = a + (b - a) * core
        yy = b + (a - b) * core
        return (yy * RING + xx) * 2 + parity

    def dev(a, b):
        return (slot(a, b, core), mt)

    plus_a, minus_a = dev(ua + 1, ub), dev(ua - 1, ub)
    plus_b, minus_b = dev(ua, ub + 1), dev(ua, ub - 1)
    sib_dev = (sib, mt)

    n_t = got.shape[0]
    barrier = pltpu.get_barrier_semaphore()
    for target in (plus_a, minus_a, plus_b, minus_b, sib_dev):
        pl.semaphore_signal(barrier, 1, device_id=target, device_id_type=MESH)

    def greet(i, carry):
        q = lax.rem(mt + 1 + i, n_t)
        pl.semaphore_signal(barrier, 1, device_id=(me, q), device_id_type=MESH)
        return carry

    lax.fori_loop(0, n_t - 1, greet, 0)
    pl.semaphore_wait(barrier, 5 + n_t - 1)

    def t_out(q):
        return pltpu.make_async_remote_copy(
            src_ref=rows_ref, dst_ref=got.at[mt], send_sem=send_t.at[q],
            recv_sem=recv_t.at[mt], device_id=(me, q), device_id_type=MESH)

    def t_in(q):
        return pltpu.make_async_remote_copy(
            src_ref=rows_ref, dst_ref=got.at[q], send_sem=send_t.at[q],
            recv_sem=recv_t.at[q], device_id=(me, q), device_id_type=MESH)

    def t_start(i, carry):
        t_out(lax.rem(mt + 1 + i, n_t)).start()
        return carry

    lax.fori_loop(0, n_t - 1, t_start, 0)
    own_t = pltpu.make_async_copy(rows_ref, got.at[mt], local.at[1])
    own_t.start()

    def t_finish(i, carry):
        q = lax.rem(mt + 1 + i, n_t)
        t_in(q).wait_recv()
        t_out(q).wait_send()
        return carry

    lax.fori_loop(0, n_t - 1, t_finish, 0)
    own_t.wait()

    width = got.shape[2]
    values = got[...].astype(jnp.float32)
    sumsq = jnp.sum(jnp.sum(values * values, axis=0), axis=-1, keepdims=True)
    scale = lax.rsqrt(sumsq / (n_t * width) + 1e-06)
    for t in range(n_t):
        piece = values[t] * scale * gain_ref[:, pl.ds(t * width, width)]
        block_ref[:, pl.ds(t * width, width)] = piece.astype(block_ref.dtype)
    tgt = target_ref[...]
    lane = lax.broadcasted_iota(jnp.int32, (tgt.shape[0], 128), 1)
    tail = jnp.where(lane == 0, tgt // 65536, jnp.where(lane == 1, (tgt // 256) % 256,
                                                          jnp.where(lane == 2, tgt % 256, 0)))
    block_ref[:, pl.ds(n_t * width, 128)] = tail.astype(jnp.float32).astype(block_ref.dtype)

    sends = []
    cols = block_ref.shape[1]
    split = (cols // 256) * 128
    halves = ((0, split), (split, cols - split))

    def put(src_slot, dst_slot, target, h):
        c0, cw = halves[h]
        src = block_ref if src_slot is None else out_ref.at[src_slot]
        copy = pltpu.make_async_remote_copy(
            src_ref=src.at[:, pl.ds(c0, cw)], dst_ref=out_ref.at[dst_slot, :, pl.ds(c0, cw)],
            send_sem=send.at[len(sends)], recv_sem=recv.at[dst_slot, h], device_id=target,
            device_id_type=MESH)
        copy.start()
        sends.append(copy)

    def arrive(dst_slot, h):
        c0, cw = halves[h]
        pltpu.make_async_remote_copy(
            src_ref=block_ref.at[:, pl.ds(c0, cw)], dst_ref=out_ref.at[dst_slot, :, pl.ds(c0, cw)],
            send_sem=send.at[0], recv_sem=recv.at[dst_slot, h], device_id=sib_dev,
            device_id_type=MESH).wait_recv()

    own = pltpu.make_async_copy(block_ref, out_ref.at[me], local.at[0])
    own.start()
    for h in (0, 1):
        for target in (plus_a, minus_a, plus_b, minus_b, sib_dev):
            put(None, me, target, h)

    left, right, far = slot(ua - 1, ub, core), slot(ua + 1, ub, core), slot(ua + 2, ub, core)
    pick = 1 - (ua + 3 + core) % 2
    fwd = pick * left + (1 - pick) * right
    fwd_dev = (pick * plus_a[0] + (1 - pick) * minus_a[0], mt)
    other = left + right - fwd
    for h in (0, 1):
        arrive(fwd, h)
        put(fwd, fwd, fwd_dev, h)
        arrive(other, h)
        for src in (left, right):
            for target in (plus_b, minus_b, sib_dev):
                put(src, src, target, h)
    for h in (0, 1):
        arrive(far, h)
        for target in (plus_b, minus_b, sib_dev):
            put(far, far, target, h)

    pick_b = 1 - (ub + 3 + core) % 2
    for d in (0, -1, 1, 2):
        lo, hi = slot(ua + d, ub - 1, core), slot(ua + d, ub + 1, core)
        fwd = pick_b * lo + (1 - pick_b) * hi
        fwd_dev = (pick_b * plus_b[0] + (1 - pick_b) * minus_b[0], mt)
        other = lo + hi - fwd
        for h in (0, 1):
            arrive(fwd, h)
            put(fwd, fwd, fwd_dev, h)
            arrive(other, h)
            put(lo, lo, sib_dev, h)
            put(hi, hi, sib_dev, h)
    for d in (0, -1, 1, 2):
        far_b = slot(ua + d, ub + 2, core)
        for h in (0, 1):
            arrive(far_b, h)
            put(far_b, far_b, sib_dev, h)

    for c in range(n_chip):
        for h in (0, 1):
            arrive(c * 2 + 1 - core, h)
    for copy in sends:
        copy.wait_send()
    own.wait()


def gather_rows(rows, gain, target, n_dp, n_t):
    k, width = rows.shape
    shape = (k, n_t * width + 128)
    return pl.pallas_call(
        rows_kernel,
        out_shape=jax.ShapeDtypeStruct((n_dp,) + shape, rows.dtype),
        in_specs=[pl.BlockSpec(memory_space=pltpu.VMEM)] * 3,
        out_specs=pl.BlockSpec(memory_space=pl.ANY),
        scratch_shapes=[
            pltpu.VMEM((n_t, k, width), rows.dtype),
            pltpu.VMEM(shape, rows.dtype),
            pltpu.SemaphoreType.DMA((n_t,)),
            pltpu.SemaphoreType.DMA((n_t,)),
            pltpu.SemaphoreType.DMA((2 * n_dp,)),
            pltpu.SemaphoreType.DMA((n_dp, 2)),
            pltpu.SemaphoreType.DMA((2,)),
        ],
        compiler_params=pltpu.CompilerParams(collective_id=2, has_side_effects=True, vmem_limit_bytes=16 * 1024 * 1024),
    )(rows, gain.reshape(1, n_t * width), target.reshape(k, 1))


def per_device(hidden, gain, head, lengths, offsets, targets, mask):
    seq_count, slot_count = offsets.shape
    slots = seq_count * slot_count
    maxlen = hidden.shape[1]
    n_dp = lax.axis_size("dp")
    n_t = lax.axis_size("tensor")
    k = min(LIVE, slots)

    live = (mask.reshape(slots) != 0).astype(jnp.int32)
    slot_ids = jnp.arange(slots, dtype=jnp.int32)
    rank = jnp.sum(jnp.where(slot_ids[:, None] >= slot_ids[None, :], live[None, :], 0), axis=1) - 1
    sel = (live[None, :] != 0) & (rank[None, :] == jnp.arange(k, dtype=jnp.int32)[:, None])
    seq_of = jnp.sum(jnp.where(sel, (slot_ids // slot_count)[None, :], 0), axis=1)
    offset_of = jnp.sum(jnp.where(sel, offsets.reshape(1, slots), 0), axis=1)
    flat_target = jnp.sum(jnp.where(sel, targets.reshape(1, slots), 0), axis=1)
    length_of = jnp.sum(jnp.where(seq_of[:, None] == jnp.arange(seq_count)[None, :], lengths[None, :], 0), axis=1)
    position = length_of - 1 - offset_of
    flat_hidden = hidden.reshape(seq_count * maxlen, hidden.shape[2])
    picked = jnp.take(flat_hidden, seq_of * maxlen + position, axis=0)

    vocab_width = head.shape[1]
    vocab_start = (lax.axis_index("dp") * n_t + lax.axis_index("tensor")) * vocab_width
    columns = jnp.arange(vocab_width, dtype=jnp.int32)
    width = n_t * picked.shape[1]
    gathered = gather_rows(picked, gain, flat_target, n_dp, n_t).reshape(n_dp * k, width + 128)
    rows_piece = gathered[:, :width]
    got_digits = gathered[:, width : width + 3].astype(jnp.int32)
    target_piece = got_digits[:, 0] * 65536 + got_digits[:, 1] * 256 + got_digits[:, 2]
    logits = jnp.dot(rows_piece, head, preferred_element_type=jnp.float32)
    top = jnp.max(logits, axis=-1)
    expo = jnp.exp(logits - top[:, None])
    total = jnp.sum(expo, axis=-1)
    weighted = jnp.sum(expo * logits, axis=-1)
    hit = columns[None, :] == (target_piece - vocab_start)[:, None]
    chosen = jnp.sum(jnp.where(hit, logits, 0.0), axis=-1)

    parts = jnp.stack([top, total, weighted, chosen]).reshape(4, n_dp, k).transpose(1, 0, 2)
    top, total, weighted, chosen = exchange_stats(parts, n_t)
    lse = top + jnp.log(total)
    score = chosen - lse
    spread = lse - weighted / total

    logprob = jnp.sum(jnp.where(sel, score[:, None], 0.0), axis=0)
    entropy = jnp.sum(jnp.where(sel, spread[:, None], 0.0), axis=0)
    return (logprob.reshape(seq_count, slot_count), entropy.reshape(seq_count, slot_count))


def solution(mesh):
    return jax.shard_map(
        per_device,
        mesh=mesh,
        in_specs=(
            P("dp", None, "tensor"),
            P(),
            P(None, ("dp", "tensor")),
            P("dp"),
            P("dp", None),
            P("dp", None),
            P("dp", None),
        ),
        out_specs=(P("dp", None), P("dp", None)),
        check_vma=False,
    )
```

```python
import functools

import jax
import jax.numpy as jnp
from jax import lax
from jax.experimental import pallas as pl
from jax.experimental.pallas import tpu as pltpu
from jax.sharding import PartitionSpec as P

MESH = pl.DeviceIdType.MESH
LIVE = 16
RING = 4


def merge(parts):
    tops = parts[:, 0, :]
    top = jnp.max(tops, axis=0, keepdims=True)
    factor = jnp.exp(tops - top)
    total = jnp.sum(parts[:, 1, :] * factor, axis=0, keepdims=True)
    weighted = jnp.sum(parts[:, 2, :] * factor, axis=0, keepdims=True)
    chosen = jnp.sum(parts[:, 3, :], axis=0, keepdims=True)
    return jnp.concatenate([top, total, weighted, chosen], axis=0)


def stats_kernel(part_ref, out_ref, got1, sent, got2, send1, recv1, send2, recv2, local):
    n_dp = part_ref.shape[0]
    n_t = got2.shape[0]
    me = lax.axis_index("dp")
    mt = lax.axis_index("tensor")

    barrier = pltpu.get_barrier_semaphore()

    def greet_dp(i, carry):
        p = lax.rem(me + 1 + i, n_dp)
        pl.semaphore_signal(barrier, 1, device_id=(p, mt), device_id_type=MESH)
        return carry

    def greet_t(i, carry):
        q = lax.rem(mt + 1 + i, n_t)
        pl.semaphore_signal(barrier, 1, device_id=(me, q), device_id_type=MESH)
        return carry

    lax.fori_loop(0, n_dp - 1, greet_dp, 0)
    lax.fori_loop(0, n_t - 1, greet_t, 0)
    pl.semaphore_wait(barrier, n_dp - 1 + n_t - 1)

    def out1(p):
        return pltpu.make_async_remote_copy(
            src_ref=part_ref.at[p], dst_ref=got1.at[me], send_sem=send1.at[p],
            recv_sem=recv1.at[me], device_id=(p, mt), device_id_type=MESH)

    def in1(p):
        return pltpu.make_async_remote_copy(
            src_ref=part_ref.at[p], dst_ref=got1.at[p], send_sem=send1.at[p],
            recv_sem=recv1.at[p], device_id=(p, mt), device_id_type=MESH)

    def start1(i, carry):
        out1(lax.rem(me + 1 + i, n_dp)).start()
        return carry

    lax.fori_loop(0, n_dp - 1, start1, 0)
    own1 = pltpu.make_async_copy(part_ref.at[me], got1.at[me], local.at[0])
    own1.start()

    def finish1(i, carry):
        in1(lax.rem(me + 1 + i, n_dp)).wait_recv()
        return carry

    lax.fori_loop(0, n_dp - 1, finish1, 0)
    own1.wait()

    sent[...] = merge(got1[...])

    def out2(q):
        return pltpu.make_async_remote_copy(
            src_ref=sent, dst_ref=got2.at[mt], send_sem=send2.at[q],
            recv_sem=recv2.at[mt], device_id=(me, q), device_id_type=MESH)

    def in2(q):
        return pltpu.make_async_remote_copy(
            src_ref=sent, dst_ref=got2.at[q], send_sem=send2.at[q],
            recv_sem=recv2.at[q], device_id=(me, q), device_id_type=MESH)

    def start2(i, carry):
        out2(lax.rem(mt + 1 + i, n_t)).start()
        return carry

    lax.fori_loop(0, n_t - 1, start2, 0)
    own2 = pltpu.make_async_copy(sent, got2.at[mt], local.at[1])
    own2.start()

    def finish2(i, carry):
        in2(lax.rem(mt + 1 + i, n_t)).wait_recv()
        return carry

    lax.fori_loop(0, n_t - 1, finish2, 0)
    own2.wait()

    out_ref[...] = merge(got2[...])

    def drain1(i, carry):
        out1(lax.rem(me + 1 + i, n_dp)).wait_send()
        return carry

    def drain2(i, carry):
        out2(lax.rem(mt + 1 + i, n_t)).wait_send()
        return carry

    lax.fori_loop(0, n_dp - 1, drain1, 0)
    lax.fori_loop(0, n_t - 1, drain2, 0)


def exchange_stats(parts, n_t):
    n_dp, four, k = parts.shape
    return pl.pallas_call(
        stats_kernel,
        out_shape=jax.ShapeDtypeStruct((four, k), jnp.float32),
        in_specs=[pl.BlockSpec(memory_space=pltpu.VMEM)],
        out_specs=pl.BlockSpec(memory_space=pltpu.VMEM),
        scratch_shapes=[
            pltpu.VMEM((n_dp, four, k), jnp.float32),
            pltpu.VMEM((four, k), jnp.float32),
            pltpu.VMEM((n_t, four, k), jnp.float32),
            pltpu.SemaphoreType.DMA((n_dp,)),
            pltpu.SemaphoreType.DMA((n_dp,)),
            pltpu.SemaphoreType.DMA((n_t,)),
            pltpu.SemaphoreType.DMA((n_t,)),
            pltpu.SemaphoreType.DMA((2,)),
        ],
        compiler_params=pltpu.CompilerParams(collective_id=0, has_side_effects=True, vmem_limit_bytes=16 * 1024 * 1024),
    )(parts)


def rows_kernel(rows_ref, gain_ref, target_ref, out_ref, got, block_ref, send_t, recv_t, send, recv, local):
    n_dp = out_ref.shape[0]
    n_chip = n_dp // 2
    me = lax.axis_index("dp")
    mt = lax.axis_index("tensor")
    chip = me // 2
    core = me % 2
    x = chip % RING
    y = chip // RING
    ua = x + (y - x) * core
    ub = y + (x - y) * core
    sib = me + 1 - 2 * core

    def slot(a, b, parity):
        a = (a + 2 * RING) % RING
        b = (b + 2 * RING) % RING
        xx = a + (b - a) * core
        yy = b + (a - b) * core
        return (yy * RING + xx) * 2 + parity

    def dev(a, b):
        return (slot(a, b, core), mt)

    plus_a, minus_a = dev(ua + 1, ub), dev(ua - 1, ub)
    plus_b, minus_b = dev(ua, ub + 1), dev(ua, ub - 1)
    sib_dev = (sib, mt)

    n_t = got.shape[0]
    barrier = pltpu.get_barrier_semaphore()
    for target in (plus_a, minus_a, plus_b, minus_b, sib_dev):
        pl.semaphore_signal(barrier, 1, device_id=target, device_id_type=MESH)

    def greet(i, carry):
        q = lax.rem(mt + 1 + i, n_t)
        pl.semaphore_signal(barrier, 1, device_id=(me, q), device_id_type=MESH)
        return carry

    lax.fori_loop(0, n_t - 1, greet, 0)
    pl.semaphore_wait(barrier, 5 + n_t - 1)

    def t_out(q):
        return pltpu.make_async_remote_copy(
            src_ref=rows_ref, dst_ref=got.at[mt], send_sem=send_t.at[q],
            recv_sem=recv_t.at[mt], device_id=(me, q), device_id_type=MESH)

    def t_in(q):
        return pltpu.make_async_remote_copy(
            src_ref=rows_ref, dst_ref=got.at[q], send_sem=send_t.at[q],
            recv_sem=recv_t.at[q], device_id=(me, q), device_id_type=MESH)

    def t_start(i, carry):
        t_out(lax.rem(mt + 1 + i, n_t)).start()
        return carry

    lax.fori_loop(0, n_t - 1, t_start, 0)
    own_t = pltpu.make_async_copy(rows_ref, got.at[mt], local.at[1])
    own_t.start()

    def t_finish(i, carry):
        q = lax.rem(mt + 1 + i, n_t)
        t_in(q).wait_recv()
        t_out(q).wait_send()
        return carry

    lax.fori_loop(0, n_t - 1, t_finish, 0)
    own_t.wait()

    width = got.shape[2]
    values = got[...].astype(jnp.float32)
    sumsq = jnp.sum(jnp.sum(values * values, axis=0), axis=-1, keepdims=True)
    scale = lax.rsqrt(sumsq / (n_t * width) + 1e-06)
    for t in range(n_t):
        piece = values[t] * scale * gain_ref[:, pl.ds(t * width, width)]
        block_ref[:, pl.ds(t * width, width)] = piece.astype(block_ref.dtype)
    tgt = target_ref[...]
    lane = lax.broadcasted_iota(jnp.int32, (tgt.shape[0], 128), 1)
    tail = jnp.where(lane == 0, tgt // 65536, jnp.where(lane == 1, (tgt // 256) % 256,
                                                          jnp.where(lane == 2, tgt % 256, 0)))
    block_ref[:, pl.ds(n_t * width, 128)] = tail.astype(jnp.float32).astype(block_ref.dtype)

    sends = []
    cols = block_ref.shape[1]
    split = (cols // 256) * 128
    halves = ((0, split), (split, cols - split))

    def put(src_slot, dst_slot, target, h):
        c0, cw = halves[h]
        src = block_ref if src_slot is None else out_ref.at[src_slot]
        copy = pltpu.make_async_remote_copy(
            src_ref=src.at[:, pl.ds(c0, cw)], dst_ref=out_ref.at[dst_slot, :, pl.ds(c0, cw)],
            send_sem=send.at[len(sends)], recv_sem=recv.at[dst_slot, h], device_id=target,
            device_id_type=MESH)
        copy.start()
        sends.append(copy)

    def arrive(dst_slot, h):
        c0, cw = halves[h]
        pltpu.make_async_remote_copy(
            src_ref=block_ref.at[:, pl.ds(c0, cw)], dst_ref=out_ref.at[dst_slot, :, pl.ds(c0, cw)],
            send_sem=send.at[0], recv_sem=recv.at[dst_slot, h], device_id=sib_dev,
            device_id_type=MESH).wait_recv()

    own = pltpu.make_async_copy(block_ref, out_ref.at[me], local.at[0])
    own.start()
    for h in (0, 1):
        for target in (plus_a, minus_a, plus_b, minus_b, sib_dev):
            put(None, me, target, h)

    left, right, far = slot(ua - 1, ub, core), slot(ua + 1, ub, core), slot(ua + 2, ub, core)
    pick = 1 - (ua + 3 + core) % 2
    fwd = pick * left + (1 - pick) * right
    fwd_dev = (pick * plus_a[0] + (1 - pick) * minus_a[0], mt)
    for h in (0, 1):
        arrive(left, h)
        arrive(right, h)
        put(fwd, fwd, fwd_dev, h)
        for src in (left, right):
            for target in (plus_b, minus_b, sib_dev):
                put(src, src, target, h)
    for h in (0, 1):
        arrive(far, h)
        for target in (plus_b, minus_b, sib_dev):
            put(far, far, target, h)

    pick_b = 1 - (ub + 3 + core) % 2
    for d in (0, -1, 1, 2):
        lo, hi = slot(ua + d, ub - 1, core), slot(ua + d, ub + 1, core)
        fwd = pick_b * lo + (1 - pick_b) * hi
        fwd_dev = (pick_b * plus_b[0] + (1 - pick_b) * minus_b[0], mt)
        for h in (0, 1):
            arrive(lo, h)
            arrive(hi, h)
            put(fwd, fwd, fwd_dev, h)
            put(lo, lo, sib_dev, h)
            put(hi, hi, sib_dev, h)
    for d in (0, -1, 1, 2):
        far_b = slot(ua + d, ub + 2, core)
        for h in (0, 1):
            arrive(far_b, h)
            put(far_b, far_b, sib_dev, h)

    for c in range(n_chip):
        for h in (0, 1):
            arrive(c * 2 + 1 - core, h)
    for copy in sends:
        copy.wait_send()
    own.wait()


def gather_rows(rows, gain, target, n_dp, n_t):
    k, width = rows.shape
    shape = (k, n_t * width + 128)
    return pl.pallas_call(
        rows_kernel,
        out_shape=jax.ShapeDtypeStruct((n_dp,) + shape, rows.dtype),
        in_specs=[pl.BlockSpec(memory_space=pltpu.VMEM)] * 3,
        out_specs=pl.BlockSpec(memory_space=pl.ANY),
        scratch_shapes=[
            pltpu.VMEM((n_t, k, width), rows.dtype),
            pltpu.VMEM(shape, rows.dtype),
            pltpu.SemaphoreType.DMA((n_t,)),
            pltpu.SemaphoreType.DMA((n_t,)),
            pltpu.SemaphoreType.DMA((2 * n_dp,)),
            pltpu.SemaphoreType.DMA((n_dp, 2)),
            pltpu.SemaphoreType.DMA((2,)),
        ],
        compiler_params=pltpu.CompilerParams(collective_id=2, has_side_effects=True, vmem_limit_bytes=16 * 1024 * 1024),
    )(rows, gain.reshape(1, n_t * width), target.reshape(k, 1))


def per_device(hidden, gain, head, lengths, offsets, targets, mask):
    seq_count, slot_count = offsets.shape
    slots = seq_count * slot_count
    maxlen = hidden.shape[1]
    n_dp = lax.axis_size("dp")
    n_t = lax.axis_size("tensor")
    k = min(LIVE, slots)

    live = (mask.reshape(slots) != 0).astype(jnp.int32)
    slot_ids = jnp.arange(slots, dtype=jnp.int32)
    rank = jnp.sum(jnp.where(slot_ids[:, None] >= slot_ids[None, :], live[None, :], 0), axis=1) - 1
    sel = (live[None, :] != 0) & (rank[None, :] == jnp.arange(k, dtype=jnp.int32)[:, None])
    seq_of = jnp.sum(jnp.where(sel, (slot_ids // slot_count)[None, :], 0), axis=1)
    offset_of = jnp.sum(jnp.where(sel, offsets.reshape(1, slots), 0), axis=1)
    flat_target = jnp.sum(jnp.where(sel, targets.reshape(1, slots), 0), axis=1)
    length_of = jnp.sum(jnp.where(seq_of[:, None] == jnp.arange(seq_count)[None, :], lengths[None, :], 0), axis=1)
    position = length_of - 1 - offset_of
    flat_hidden = hidden.reshape(seq_count * maxlen, hidden.shape[2])
    picked = jnp.take(flat_hidden, seq_of * maxlen + position, axis=0)

    vocab_width = head.shape[1]
    vocab_start = (lax.axis_index("dp") * n_t + lax.axis_index("tensor")) * vocab_width
    columns = jnp.arange(vocab_width, dtype=jnp.int32)
    width = n_t * picked.shape[1]
    gathered = gather_rows(picked, gain, flat_target, n_dp, n_t).reshape(n_dp * k, width + 128)
    rows_piece = gathered[:, :width]
    got_digits = gathered[:, width : width + 3].astype(jnp.int32)
    target_piece = got_digits[:, 0] * 65536 + got_digits[:, 1] * 256 + got_digits[:, 2]
    logits = jnp.dot(rows_piece, head, preferred_element_type=jnp.float32)
    top = jnp.max(logits, axis=-1)
    expo = jnp.exp(logits - top[:, None])
    total = jnp.sum(expo, axis=-1)
    weighted = jnp.sum(expo * logits, axis=-1)
    hit = columns[None, :] == (target_piece - vocab_start)[:, None]
    chosen = jnp.sum(jnp.where(hit, logits, 0.0), axis=-1)

    parts = jnp.stack([top, total, weighted, chosen]).reshape(4, n_dp, k).transpose(1, 0, 2)
    top, total, weighted, chosen = exchange_stats(parts, n_t)
    lse = top + jnp.log(total)
    score = chosen - lse
    spread = lse - weighted / total

    logprob = jnp.sum(jnp.where(sel, score[:, None], 0.0), axis=0)
    entropy = jnp.sum(jnp.where(sel, spread[:, None], 0.0), axis=0)
    return (logprob.reshape(seq_count, slot_count), entropy.reshape(seq_count, slot_count))


def solution(mesh):
    return jax.shard_map(
        per_device,
        mesh=mesh,
        in_specs=(
            P("dp", None, "tensor"),
            P(),
            P(None, ("dp", "tensor")),
            P("dp"),
            P("dp", None),
            P("dp", None),
            P("dp", None),
        ),
        out_specs=(P("dp", None), P("dp", None)),
        check_vma=False,
    )
```

```python
import functools

import jax
import jax.numpy as jnp
from jax import lax
from jax.experimental import pallas as pl
from jax.experimental.pallas import tpu as pltpu
from jax.sharding import PartitionSpec as P

MESH = pl.DeviceIdType.MESH
LIVE = 16
RING = 4


def merge(parts):
    tops = parts[:, 0, :]
    top = jnp.max(tops, axis=0, keepdims=True)
    factor = jnp.exp(tops - top)
    total = jnp.sum(parts[:, 1, :] * factor, axis=0, keepdims=True)
    weighted = jnp.sum(parts[:, 2, :] * factor, axis=0, keepdims=True)
    chosen = jnp.sum(parts[:, 3, :], axis=0, keepdims=True)
    return jnp.concatenate([top, total, weighted, chosen], axis=0)


def stats_kernel(part_ref, out_ref, got1, sent, got2, send1, recv1, send2, recv2, local):
    n_dp = part_ref.shape[0]
    n_t = got2.shape[0]
    me = lax.axis_index("dp")
    mt = lax.axis_index("tensor")

    barrier = pltpu.get_barrier_semaphore()

    def greet_dp(i, carry):
        p = lax.rem(me + 1 + i, n_dp)
        pl.semaphore_signal(barrier, 1, device_id=(p, mt), device_id_type=MESH)
        return carry

    def greet_t(i, carry):
        q = lax.rem(mt + 1 + i, n_t)
        pl.semaphore_signal(barrier, 1, device_id=(me, q), device_id_type=MESH)
        return carry

    lax.fori_loop(0, n_dp - 1, greet_dp, 0)
    lax.fori_loop(0, n_t - 1, greet_t, 0)
    pl.semaphore_wait(barrier, n_dp - 1 + n_t - 1)

    def out1(p):
        return pltpu.make_async_remote_copy(
            src_ref=part_ref.at[p], dst_ref=got1.at[me], send_sem=send1.at[p],
            recv_sem=recv1.at[me], device_id=(p, mt), device_id_type=MESH)

    def in1(p):
        return pltpu.make_async_remote_copy(
            src_ref=part_ref.at[p], dst_ref=got1.at[p], send_sem=send1.at[p],
            recv_sem=recv1.at[p], device_id=(p, mt), device_id_type=MESH)

    def start1(i, carry):
        out1(lax.rem(me + 1 + i, n_dp)).start()
        return carry

    lax.fori_loop(0, n_dp - 1, start1, 0)
    own1 = pltpu.make_async_copy(part_ref.at[me], got1.at[me], local.at[0])
    own1.start()

    def finish1(i, carry):
        p = lax.rem(me + 1 + i, n_dp)
        in1(p).wait_recv()
        out1(p).wait_send()
        return carry

    lax.fori_loop(0, n_dp - 1, finish1, 0)
    own1.wait()

    sent[...] = merge(got1[...])

    def out2(q):
        return pltpu.make_async_remote_copy(
            src_ref=sent, dst_ref=got2.at[mt], send_sem=send2.at[q],
            recv_sem=recv2.at[mt], device_id=(me, q), device_id_type=MESH)

    def in2(q):
        return pltpu.make_async_remote_copy(
            src_ref=sent, dst_ref=got2.at[q], send_sem=send2.at[q],
            recv_sem=recv2.at[q], device_id=(me, q), device_id_type=MESH)

    def start2(i, carry):
        out2(lax.rem(mt + 1 + i, n_t)).start()
        return carry

    lax.fori_loop(0, n_t - 1, start2, 0)
    own2 = pltpu.make_async_copy(sent, got2.at[mt], local.at[1])
    own2.start()

    def finish2(i, carry):
        q = lax.rem(mt + 1 + i, n_t)
        in2(q).wait_recv()
        out2(q).wait_send()
        return carry

    lax.fori_loop(0, n_t - 1, finish2, 0)
    own2.wait()

    out_ref[...] = merge(got2[...])


def exchange_stats(parts, n_t):
    n_dp, four, k = parts.shape
    return pl.pallas_call(
        stats_kernel,
        out_shape=jax.ShapeDtypeStruct((four, k), jnp.float32),
        in_specs=[pl.BlockSpec(memory_space=pltpu.VMEM)],
        out_specs=pl.BlockSpec(memory_space=pltpu.VMEM),
        scratch_shapes=[
            pltpu.VMEM((n_dp, four, k), jnp.float32),
            pltpu.VMEM((four, k), jnp.float32),
            pltpu.VMEM((n_t, four, k), jnp.float32),
            pltpu.SemaphoreType.DMA((n_dp,)),
            pltpu.SemaphoreType.DMA((n_dp,)),
            pltpu.SemaphoreType.DMA((n_t,)),
            pltpu.SemaphoreType.DMA((n_t,)),
            pltpu.SemaphoreType.DMA((2,)),
        ],
        compiler_params=pltpu.CompilerParams(collective_id=0, has_side_effects=True, vmem_limit_bytes=16 * 1024 * 1024),
    )(parts)


def rows_kernel(rows_ref, gain_ref, target_ref, out_ref, got, block_ref, send_t, recv_t, send, recv, local):
    n_dp = out_ref.shape[0]
    n_chip = n_dp // 2
    me = lax.axis_index("dp")
    mt = lax.axis_index("tensor")
    chip = me // 2
    core = me % 2
    x = chip % RING
    y = chip // RING
    ua = x + (y - x) * core
    ub = y + (x - y) * core
    sib = me + 1 - 2 * core

    def slot(a, b, parity):
        a = (a + 2 * RING) % RING
        b = (b + 2 * RING) % RING
        xx = a + (b - a) * core
        yy = b + (a - b) * core
        return (yy * RING + xx) * 2 + parity

    def dev(a, b):
        return (slot(a, b, core), mt)

    plus_a, minus_a = dev(ua + 1, ub), dev(ua - 1, ub)
    plus_b, minus_b = dev(ua, ub + 1), dev(ua, ub - 1)
    sib_dev = (sib, mt)

    n_t = got.shape[0]
    barrier = pltpu.get_barrier_semaphore()
    for target in (plus_a, minus_a, plus_b, minus_b, sib_dev):
        pl.semaphore_signal(barrier, 1, device_id=target, device_id_type=MESH)

    def greet(i, carry):
        q = lax.rem(mt + 1 + i, n_t)
        pl.semaphore_signal(barrier, 1, device_id=(me, q), device_id_type=MESH)
        return carry

    lax.fori_loop(0, n_t - 1, greet, 0)
    pl.semaphore_wait(barrier, 5 + n_t - 1)

    def t_out(q):
        return pltpu.make_async_remote_copy(
            src_ref=rows_ref, dst_ref=got.at[mt], send_sem=send_t.at[q],
            recv_sem=recv_t.at[mt], device_id=(me, q), device_id_type=MESH)

    def t_in(q):
        return pltpu.make_async_remote_copy(
            src_ref=rows_ref, dst_ref=got.at[q], send_sem=send_t.at[q],
            recv_sem=recv_t.at[q], device_id=(me, q), device_id_type=MESH)

    def t_start(i, carry):
        t_out(lax.rem(mt + 1 + i, n_t)).start()
        return carry

    lax.fori_loop(0, n_t - 1, t_start, 0)
    own_t = pltpu.make_async_copy(rows_ref, got.at[mt], local.at[1])
    own_t.start()

    def t_finish(i, carry):
        t_in(lax.rem(mt + 1 + i, n_t)).wait_recv()
        return carry

    lax.fori_loop(0, n_t - 1, t_finish, 0)
    own_t.wait()

    width = got.shape[2]
    values = got[...].astype(jnp.float32)
    sumsq = jnp.sum(jnp.sum(values * values, axis=0), axis=-1, keepdims=True)
    scale = lax.rsqrt(sumsq / (n_t * width) + 1e-06)
    for t in range(n_t):
        piece = values[t] * scale * gain_ref[:, pl.ds(t * width, width)]
        block_ref[:, pl.ds(t * width, width)] = piece.astype(block_ref.dtype)
    tgt = target_ref[...]
    lane = lax.broadcasted_iota(jnp.int32, (tgt.shape[0], 128), 1)
    tail = jnp.where(lane == 0, tgt // 65536, jnp.where(lane == 1, (tgt // 256) % 256,
                                                          jnp.where(lane == 2, tgt % 256, 0)))
    block_ref[:, pl.ds(n_t * width, 128)] = tail.astype(jnp.float32).astype(block_ref.dtype)

    sends = []
    cols = block_ref.shape[1]
    split = (cols // 256) * 128
    halves = ((0, split), (split, cols - split))

    def put(src_slot, dst_slot, target, h):
        c0, cw = halves[h]
        src = block_ref if src_slot is None else out_ref.at[src_slot]
        copy = pltpu.make_async_remote_copy(
            src_ref=src.at[:, pl.ds(c0, cw)], dst_ref=out_ref.at[dst_slot, :, pl.ds(c0, cw)],
            send_sem=send.at[len(sends)], recv_sem=recv.at[dst_slot, h], device_id=target,
            device_id_type=MESH)
        copy.start()
        sends.append(copy)

    def arrive(dst_slot, h):
        c0, cw = halves[h]
        pltpu.make_async_remote_copy(
            src_ref=block_ref.at[:, pl.ds(c0, cw)], dst_ref=out_ref.at[dst_slot, :, pl.ds(c0, cw)],
            send_sem=send.at[0], recv_sem=recv.at[dst_slot, h], device_id=sib_dev,
            device_id_type=MESH).wait_recv()

    own = pltpu.make_async_copy(block_ref, out_ref.at[me], local.at[0])
    own.start()
    for h in (0, 1):
        for target in (plus_a, minus_a, plus_b, minus_b, sib_dev):
            put(None, me, target, h)

    left, right, far = slot(ua - 1, ub, core), slot(ua + 1, ub, core), slot(ua + 2, ub, core)
    pick = 1 - (ua + 3 + core) % 2
    fwd = pick * left + (1 - pick) * right
    fwd_dev = (pick * plus_a[0] + (1 - pick) * minus_a[0], mt)
    for h in (0, 1):
        arrive(left, h)
        arrive(right, h)
        put(fwd, fwd, fwd_dev, h)
        for src in (left, right):
            for target in (plus_b, minus_b, sib_dev):
                put(src, src, target, h)
    for h in (0, 1):
        arrive(far, h)
        for target in (plus_b, minus_b, sib_dev):
            put(far, far, target, h)

    pick_b = 1 - (ub + 3 + core) % 2
    for d in (0, -1, 1, 2):
        lo, hi = slot(ua + d, ub - 1, core), slot(ua + d, ub + 1, core)
        fwd = pick_b * lo + (1 - pick_b) * hi
        fwd_dev = (pick_b * plus_b[0] + (1 - pick_b) * minus_b[0], mt)
        for h in (0, 1):
            arrive(lo, h)
            arrive(hi, h)
            put(fwd, fwd, fwd_dev, h)
            put(lo, lo, sib_dev, h)
            put(hi, hi, sib_dev, h)
    for d in (0, -1, 1, 2):
        far_b = slot(ua + d, ub + 2, core)
        for h in (0, 1):
            arrive(far_b, h)
            put(far_b, far_b, sib_dev, h)

    for c in range(n_chip):
        for h in (0, 1):
            arrive(c * 2 + 1 - core, h)
    for copy in sends:
        copy.wait_send()
    own.wait()

    def t_drain(i, carry):
        t_out(lax.rem(mt + 1 + i, n_t)).wait_send()
        return carry

    lax.fori_loop(0, n_t - 1, t_drain, 0)


def gather_rows(rows, gain, target, n_dp, n_t):
    k, width = rows.shape
    shape = (k, n_t * width + 128)
    return pl.pallas_call(
        rows_kernel,
        out_shape=jax.ShapeDtypeStruct((n_dp,) + shape, rows.dtype),
        in_specs=[pl.BlockSpec(memory_space=pltpu.VMEM)] * 3,
        out_specs=pl.BlockSpec(memory_space=pl.ANY),
        scratch_shapes=[
            pltpu.VMEM((n_t, k, width), rows.dtype),
            pltpu.VMEM(shape, rows.dtype),
            pltpu.SemaphoreType.DMA((n_t,)),
            pltpu.SemaphoreType.DMA((n_t,)),
            pltpu.SemaphoreType.DMA((2 * n_dp,)),
            pltpu.SemaphoreType.DMA((n_dp, 2)),
            pltpu.SemaphoreType.DMA((2,)),
        ],
        compiler_params=pltpu.CompilerParams(collective_id=2, has_side_effects=True, vmem_limit_bytes=16 * 1024 * 1024),
    )(rows, gain.reshape(1, n_t * width), target.reshape(k, 1))


def per_device(hidden, gain, head, lengths, offsets, targets, mask):
    seq_count, slot_count = offsets.shape
    slots = seq_count * slot_count
    maxlen = hidden.shape[1]
    n_dp = lax.axis_size("dp")
    n_t = lax.axis_size("tensor")
    k = min(LIVE, slots)

    live = (mask.reshape(slots) != 0).astype(jnp.int32)
    slot_ids = jnp.arange(slots, dtype=jnp.int32)
    rank = jnp.sum(jnp.where(slot_ids[:, None] >= slot_ids[None, :], live[None, :], 0), axis=1) - 1
    sel = (live[None, :] != 0) & (rank[None, :] == jnp.arange(k, dtype=jnp.int32)[:, None])
    seq_of = jnp.sum(jnp.where(sel, (slot_ids // slot_count)[None, :], 0), axis=1)
    offset_of = jnp.sum(jnp.where(sel, offsets.reshape(1, slots), 0), axis=1)
    flat_target = jnp.sum(jnp.where(sel, targets.reshape(1, slots), 0), axis=1)
    length_of = jnp.sum(jnp.where(seq_of[:, None] == jnp.arange(seq_count)[None, :], lengths[None, :], 0), axis=1)
    position = length_of - 1 - offset_of
    flat_hidden = hidden.reshape(seq_count * maxlen, hidden.shape[2])
    picked = jnp.take(flat_hidden, seq_of * maxlen + position, axis=0)

    vocab_width = head.shape[1]
    vocab_start = (lax.axis_index("dp") * n_t + lax.axis_index("tensor")) * vocab_width
    columns = jnp.arange(vocab_width, dtype=jnp.int32)
    width = n_t * picked.shape[1]
    gathered = gather_rows(picked, gain, flat_target, n_dp, n_t).reshape(n_dp * k, width + 128)
    rows_piece = gathered[:, :width]
    got_digits = gathered[:, width : width + 3].astype(jnp.int32)
    target_piece = got_digits[:, 0] * 65536 + got_digits[:, 1] * 256 + got_digits[:, 2]
    logits = jnp.dot(rows_piece, head, preferred_element_type=jnp.float32)
    top = jnp.max(logits, axis=-1)
    expo = jnp.exp(logits - top[:, None])
    total = jnp.sum(expo, axis=-1)
    weighted = jnp.sum(expo * logits, axis=-1)
    hit = columns[None, :] == (target_piece - vocab_start)[:, None]
    chosen = jnp.sum(jnp.where(hit, logits, 0.0), axis=-1)

    parts = jnp.stack([top, total, weighted, chosen]).reshape(4, n_dp, k).transpose(1, 0, 2)
    top, total, weighted, chosen = exchange_stats(parts, n_t)
    lse = top + jnp.log(total)
    score = chosen - lse
    spread = lse - weighted / total

    logprob = jnp.sum(jnp.where(sel, score[:, None], 0.0), axis=0)
    entropy = jnp.sum(jnp.where(sel, spread[:, None], 0.0), axis=0)
    return (logprob.reshape(seq_count, slot_count), entropy.reshape(seq_count, slot_count))


def solution(mesh):
    return jax.shard_map(
        per_device,
        mesh=mesh,
        in_specs=(
            P("dp", None, "tensor"),
            P(),
            P(None, ("dp", "tensor")),
            P("dp"),
            P("dp", None),
            P("dp", None),
            P("dp", None),
        ),
        out_specs=(P("dp", None), P("dp", None)),
        check_vma=False,
    )
```
